32 devices in a mesh: seq: 4 (over y, x), batch: 8 (over z, core).
Axes of the slice: x: 2, y: 2, z: 4, core: 2. Of those that a mesh axis runs over, the one named last changes fastest.
Arguments:
- byte_states: bfloat16 [2, 8, 1024, 512], P(None, 'batch', 'seq'), may hold values from -6 to 6
- teacher: bfloat16 [2, 8, 1024, 512], P(None, 'batch', 'seq'), may hold values from -96 to 96
- lengths: int32 [2, 8], P(None, 'batch'), may hold values from 256 to 1024, as said below
- conv_taps: bfloat16 [2, 9, 512], P(None, None, ('seq', 'batch')), may hold values from -2.5 to 2.5
- conv_bias: bfloat16 [2, 3, 512], P(None, None, ('seq', 'batch')), may hold values from -2.5 to 2.5
- join_weight: bfloat16 [2, 512, 512], P(None, ('seq', 'batch')), may hold values from -0.25 to 0.25
- join_bias: bfloat16 [2, 512], P(None, ('seq', 'batch')), may hold values from -2.5 to 2.5
- gain_attn: bfloat16 [2, 512], P(None, ('seq', 'batch')), may hold values from 0.5 to 1.5
- attn_in_weight: bfloat16 [2, 3, 512, 512], P(None, None, ('seq', 'batch')), may hold values from -0.125 to 0.125
- attn_out_weight: bfloat16 [2, 512, 512], P(None, ('seq', 'batch')), may hold values from -14 to 14
- position_bias: bfloat16 [2, 256], P(None, ('seq', 'batch')), may hold values from -8 to 4
- gain_mlp: bfloat16 [2, 512], P(None, ('seq', 'batch')), may hold values from 0.5 to 1.5
- mlp_in_weight: bfloat16 [2, 2, 512, 2048], P(None, None, ('seq', 'batch')), may hold values from -0.25 to 0.25
- mlp_out_weight: bfloat16 [2, 2048, 512], P(None, ('seq', 'batch')), may hold values from -0.1875 to 0.1875
Outputs:
- activations: float32 [2, 8, 1024, 512], P(None, 'batch', 'seq')
- loss: float32 [], replicated
- input_grad: float32 [2, 8, 1024, 512], P(None, 'batch', 'seq')
- grad_conv_taps: float32 [2, 9, 512], P(None, None, ('seq', 'batch'))
- grad_conv_bias: float32 [2, 3, 512], P(None, None, ('seq', 'batch'))
- grad_join_weight: float32 [2, 512, 512], P(None, ('seq', 'batch'))
- grad_join_bias: float32 [2, 512], P(None, ('seq', 'batch'))
- grad_gain_attn: float32 [2, 512], P(None, ('seq', 'batch'))
- grad_attn_in_weight: float32 [2, 3, 512, 512], P(None, None, ('seq', 'batch'))
- grad_attn_out_weight: float32 [2, 512, 512], P(None, ('seq', 'batch'))
- grad_position_bias: float32 [2, 256], P(None, ('seq', 'batch'))
- grad_gain_mlp: float32 [2, 512], P(None, ('seq', 'batch'))
- grad_mlp_in_weight: float32 [2, 2, 512, 2048], P(None, None, ('seq', 'batch'))
- grad_mlp_out_weight: float32 [2, 2048, 512], P(None, ('seq', 'batch'))
The draws below stay inside these ranges and needn't reach their ends.
Inputs may be any that keep to these rules, and one draw needn't show every extreme that they name: `lengths`: each sequence's valid length lies between 256 and 1024; in every draw some sequence is exactly 1024 long.
All inputs are finite; a program needn't handle non-finite values.
Results may differ from the reference program's by a relative error of at most 0.017.
Values may be sent and summed in bfloat16 or wider, within the bound.
No kernel may reach another device: no remote copies, remote signals or barrier semaphores. Data moves between devices by JAX's collectives and lax.ppermute only.
A program may use at most 320 MiB of HBM per device.

```python
import jax
import jax.numpy as jnp
from jax import lax

D = 512
HEADS = 8
HEAD_DIM = 64
FF = 2048
BUCKETS = 32
LAYERS = 2
MB = 2
INNER = 512
SEQ_LEN = 1024
BATCH_SEQS = 8


def draw_lengths(key, part):
    total_seqs = MB * BATCH_SEQS
    values = jax.random.randint(key, (total_seqs,), SEQ_LEN // 4, SEQ_LEN + 1)
    chosen = jax.random.randint(jax.random.fold_in(key, 7), (), 0, total_seqs)
    values = jnp.where(jnp.arange(total_seqs) == chosen, SEQ_LEN, values)
    return values.reshape(MB, BATCH_SEQS).astype(jnp.int32)


def draw_position_bias(key, part):
    low_ends = jnp.array([0, 1, 2, 3, 4, 5, 6, 7, 8, 12, 16, 23, 32, 46, 64, 91], jnp.int32)
    high_ends = jnp.array([1, 2, 3, 4, 5, 6, 7, 8, 12, 16, 23, 32, 46, 64, 91, 1 << 30], jnp.int32)
    side_index = jnp.arange(BUCKETS * HEADS) // HEADS % 16
    width_table = jnp.maximum(jnp.minimum(high_ends[side_index], SEQ_LEN) - low_ends[side_index], 1).astype(jnp.float32)
    base_bias = -0.5 * jnp.log(width_table)
    own_key = jax.random.fold_in(key, 11)
    jitter_values = jnp.clip(jax.random.normal(own_key, (LAYERS, BUCKETS * HEADS), jnp.float32), -3.5, 3.5)
    return (base_bias[None, :] + jitter_values).astype(jnp.float32).astype(jnp.bfloat16)


def block_scale(stream_key, shape, split, smallest, top_value):
    factor_of, own = 1.0, jax.random.fold_in(stream_key, 6)
    for axis_at, shards_of in split:
        draws = jnp.exp(jax.random.uniform(jax.random.fold_in(own, axis_at), (shards_of,), jnp.float32, smallest / len(split), top_value / len(split)))
        factor_of = factor_of * jnp.repeat(draws, shape[axis_at] // shards_of).reshape([-1 if axis == axis_at else 1 for axis in range(len(shape))])
    return factor_of


def centred(stream_key, shape, scale, bound, pieces=(), dtype=jnp.bfloat16):
    factor_of = block_scale(stream_key, shape, pieces, -0.22, 0.18) if pieces else 1.0
    entries = jax.random.normal(stream_key, shape, jnp.float32) * scale * factor_of
    return jnp.minimum(jnp.maximum(entries, -bound), bound).astype(dtype)


def setup_inputs(seed: int = 0) -> dict:
    key_list = jax.random.split(jax.random.key(seed), 15)
    return {
        "byte_states": centred(key_list[0], (MB, BATCH_SEQS, SEQ_LEN, D), 1.0, 6.0, ((1, 8), (2, 4))),
        "teacher": centred(key_list[1], (MB, BATCH_SEQS, SEQ_LEN, D), 16.0, 96.0, ((1, 8), (2, 4))),
        "lengths": draw_lengths(jax.random.fold_in(key_list[14], 71), 0),
        "conv_taps": centred(key_list[3], (LAYERS, 9, D), 0.4, 2.5, ((2, 32),)),
        "conv_bias": centred(key_list[4], (LAYERS, 3, D), 0.3, 2.5, ((2, 32),)),
        "join_weight": centred(key_list[5], (LAYERS, D, D), D ** -0.5, 0.25, ((1, 32),)),
        "join_bias": centred(key_list[6], (LAYERS, D), 0.3, 2.5, ((1, 32),)),
        "gain_attn": jnp.clip(1.0 + 0.1 * jax.random.normal(key_list[7], (LAYERS, D), jnp.float32), 0.5, 1.5).astype(jnp.bfloat16),
        "attn_in_weight": centred(key_list[8], (LAYERS, 3, D, INNER), (D * 5) ** -0.5, 0.125, ((2, 32),)),
        "attn_out_weight": centred(key_list[9], (LAYERS, INNER, D), 2.2, 14.0, ((1, 32),)),
        "position_bias": draw_position_bias(jax.random.fold_in(key_list[14], 71), 0),
        "gain_mlp": jnp.clip(1.0 + 0.1 * jax.random.normal(key_list[11], (LAYERS, D), jnp.float32), 0.5, 1.5).astype(jnp.bfloat16),
        "mlp_in_weight": centred(key_list[12], (LAYERS, 2, D, FF), D ** -0.5, 0.25, ((2, 32),)),
        "mlp_out_weight": centred(key_list[13], (LAYERS, FF, D), (FF // 2) ** -0.5, 0.1875, ((1, 32),)),
    }


@jax.custom_vjp
def low(v):
    return lax.optimization_barrier(v.astype(jnp.bfloat16)).astype(jnp.float32)

@jax.custom_vjp
def low_back(v):
    return v

def low_keep(v):
    return (low(v), None)

def low_pass(kept, grad):
    return (grad,)

def back_keep(v):
    return (v, None)

def back_low(kept, grad):
    return (low(grad),)
low.defvjp(low_keep, low_pass)
low_back.defvjp(back_keep, back_low)
eps = 1e-06
bounds = (12, 16, 23, 32, 46, 64, 91)
windows = ((2, 0), (3, 2), (4, 5))
exact_mode = lax.Precision.HIGHEST

def bucket_ids(offsets):
    magnitude = jnp.abs(offsets)
    far_ids = 8 + sum(((magnitude >= bound_value).astype(jnp.int32) for bound_value in bounds))
    near_ids = jnp.where(magnitude < 8, magnitude, far_ids)
    return (jnp.where(offsets > 0, 16, 0) + near_ids).astype(jnp.int32)

def rms_norm(values, gain):
    return values * lax.rsqrt(lax.optimization_barrier(jnp.mean(values * values, -1, keepdims=True)) + eps) * gain

def conv_sum(extended, tap_rows, biases, row_count):
    total = jnp.zeros((row_count, extended.shape[1]), jnp.float32) + lax.optimization_barrier(jnp.sum(biases, 0))
    for window, offset in windows:
        for tap_index in range(window):
            first_row = 4 - window + tap_index
            total = total + tap_rows[offset + tap_index] * extended[first_row:first_row + row_count]
    return total

def matmul_exact(left, right):
    return jnp.dot(left, right, precision=exact_mode)

def layer_forward(state, weights, distance_ids, key_valid):
    tap_rows, biases, join_matrix, join_shift, gain_first, attn_in, attn_out, pos_table, gain_second, mlp_in, mlp_out = weights
    seq_count = state.shape[0]
    rounded_in = low(state)
    extended = jnp.concatenate([jnp.zeros((3, state.shape[1]), jnp.float32), rounded_in], 0)
    mixed = low(low_back(conv_sum(extended, tap_rows, biases, seq_count)))
    joined = state + low_back(matmul_exact(mixed, join_matrix) + join_shift)
    normed = low(rms_norm(joined, gain_first))
    query = low(low_back(matmul_exact(normed, attn_in[0]))).reshape(seq_count, HEADS, HEAD_DIM)
    key_heads = low(low_back(matmul_exact(normed, attn_in[1]))).reshape(seq_count, HEADS, HEAD_DIM)
    value_heads = low(low_back(matmul_exact(normed, attn_in[2]))).reshape(seq_count, HEADS, HEAD_DIM)
    offsets = (jnp.arange(2 * seq_count - 1) - (seq_count - 1)).astype(jnp.int32)
    one_hot_ids = (bucket_ids(offsets)[:, None] == jnp.arange(BUCKETS)[None, :]).astype(jnp.float32)
    by_distance = matmul_exact(one_hot_ids, pos_table.reshape(BUCKETS, HEADS))
    rel_bias = jnp.transpose(by_distance[distance_ids], (2, 0, 1))
    scores = jnp.einsum('ihd,jhd->hij', query, key_heads, precision=exact_mode) + rel_bias
    scores = low_back(scores)
    scores = jnp.where(key_valid[None, None, :], scores, -1e+30)
    probs = jax.nn.softmax(scores, axis=-1)
    attended = jnp.einsum('hij,jhd->ihd', low(probs), value_heads, precision=exact_mode).reshape(seq_count, INNER)
    attended = low(low_back(attended))
    mid_state = joined + low_back(matmul_exact(attended, attn_out))
    normed_mid = low(rms_norm(mid_state, gain_second))
    gate_in = low_back(matmul_exact(normed_mid, mlp_in[0]))
    up_in = low_back(matmul_exact(normed_mid, mlp_in[1]))
    hidden = low(jax.nn.gelu(gate_in, approximate=True) * up_in)
    return mid_state + low_back(matmul_exact(hidden, mlp_out))

def reference(byte_states, teacher, lengths, conv_taps, conv_bias, join_weight, join_bias, gain_attn, attn_in_weight, attn_out_weight, position_bias, gain_mlp, mlp_in_weight, mlp_out_weight):
    params = tuple((array_in.astype(jnp.float32) for array_in in (conv_taps, conv_bias, join_weight, join_bias, gain_attn, attn_in_weight, attn_out_weight, position_bias, gain_mlp, mlp_in_weight, mlp_out_weight)))
    states = byte_states.astype(jnp.float32).reshape(MB * BATCH_SEQS, SEQ_LEN, D)
    targets = teacher.astype(jnp.float32).reshape(MB * BATCH_SEQS, SEQ_LEN, D)
    seq_lengths = lengths.reshape(MB * BATCH_SEQS).astype(jnp.int32)
    total_valid = jnp.sum(lengths).astype(jnp.float32)
    positions = jnp.arange(SEQ_LEN).astype(jnp.int32)
    distance_ids = (positions[None, :] - positions[:, None] + SEQ_LEN - 1).astype(jnp.int32)

    def one_sequence(weights, state, target, length):
        key_valid = positions < length
        for layer_index in range(LAYERS):
            state = layer_forward(state, tuple((stacked[layer_index] for stacked in weights)), distance_ids, key_valid)
        diff = jnp.where(key_valid[:, None], state - target, 0.0)
        return (state, jnp.sum(diff * diff))
    checked = jax.checkpoint(one_sequence)

    def objective(state_in, weights):

        def step_fn(carry, item):
            out_state, squares = checked(weights, item[0], item[1], item[2])
            return (carry + squares, out_state)
        total, outs = lax.scan(step_fn, jnp.zeros((), jnp.float32), (state_in, targets, seq_lengths))
        return (total / (total_valid * D), outs)
    loss, pullback, outs = jax.vjp(objective, states, params, has_aux=True)
    grad_states, grad_params = pullback(jnp.ones_like(loss))
    return (outs.reshape(MB, BATCH_SEQS, SEQ_LEN, D), loss, grad_states.reshape(MB, BATCH_SEQS, SEQ_LEN, D), grad_params[0], grad_params[1], grad_params[2], grad_params[3], grad_params[4], grad_params[5], grad_params[6], grad_params[7], grad_params[8], grad_params[9], grad_params[10])
```

```python
import jax
import jax.numpy as jnp
from jax import lax
from jax.experimental import pallas as pl
from jax.experimental.pallas import tpu as pltpu
from jax.sharding import Mesh
from jax.sharding import PartitionSpec as P

HEADS = 8
HEAD_DIM = 64
BUCKETS = 32


eps = 1e-06
bounds = (12, 16, 23, 32, 46, 64, 91)
windows = ((2, 0), (3, 2), (4, 5))


def passed_along(block, axis, distance):
    devices = range(lax.axis_size(axis))
    route = [(i - distance, i) for i in devices if i - distance in devices]
    return lax.ppermute(block, axis, route)


def bucket_ids(offsets):
    magnitude = jnp.abs(offsets)
    far_ids = 8 + sum(((magnitude >= bound_value).astype(jnp.int32) for bound_value in bounds))
    near_ids = jnp.where(magnitude < 8, magnitude, far_ids)
    return jnp.where(offsets > 0, 16, 0) + near_ids


def rms_norm(values, gain):
    return values * lax.rsqrt(jnp.mean(values * values, -1, keepdims=True) + eps) * gain


def conv_sum(extended, tap_rows, biases, row_count):
    total = jnp.zeros((row_count, extended.shape[1]), jnp.float32) + jnp.sum(biases, 0)
    for window, offset in windows:
        for tap_index in range(window):
            first_row = 4 - window + tap_index
            total = (
                total + tap_rows[offset + tap_index] * extended[first_row : first_row + row_count]
            )
    return total


def project(left, right):
    return jnp.dot(left, right, preferred_element_type=jnp.float32)


def project_left(left, right):
    return lax.dot_general(
        left, right, (((0,), (0,)), ((), ())), preferred_element_type=jnp.float32
    )


def project_right(left, right):
    return lax.dot_general(
        left, right, (((1,), (1,)), ((), ())), preferred_element_type=jnp.float32
    )


def score_block(query, keys_all, pos_table, one_hot_ids, key_valid):
    query_heads = query.reshape(query.shape[0], HEADS, HEAD_DIM)
    key_heads = keys_all.reshape(keys_all.shape[0], HEADS, HEAD_DIM)
    rel_bias = jnp.einsum(
        "slb,bh->hsl",
        one_hot_ids,
        pos_table.reshape(BUCKETS, HEADS),
        preferred_element_type=jnp.float32,
    )
    scores = (
        jnp.einsum("shd,lhd->hsl", query_heads, key_heads, preferred_element_type=jnp.float32)
        + rel_bias
    )
    return jnp.where(key_valid[None, None, :], scores, -1e30)


def layer_forward(state, weights, one_hot_ids, key_valid):
    (
        tap_rows,
        biases,
        join_matrix,
        join_shift,
        gain_first,
        attn_in,
        attn_out,
        pos_table,
        gain_second,
        mlp_in,
        mlp_out,
    ) = weights
    row_count = state.shape[0]
    rounded_in = state.astype(jnp.bfloat16)
    prior_rows = passed_along(rounded_in[row_count - 3 :], "seq", 1)
    extended = jnp.concatenate([prior_rows, rounded_in], 0).astype(jnp.float32)
    mixed = conv_sum(
        extended, tap_rows.astype(jnp.float32), biases.astype(jnp.float32), row_count
    ).astype(jnp.bfloat16)
    joined = state + project(mixed, join_matrix) + join_shift.astype(jnp.float32)
    normed = rms_norm(joined, gain_first.astype(jnp.float32)).astype(jnp.bfloat16)
    projected = jnp.einsum(
        "sd,cdi->csi", normed, attn_in, preferred_element_type=jnp.float32
    ).astype(jnp.bfloat16)
    keys_all, values_all = (
        lax.all_gather(projected[1], "seq", axis=0, tiled=True),
        lax.all_gather(projected[2], "seq", axis=0, tiled=True),
    )
    scores = score_block(projected[0], keys_all, pos_table, one_hot_ids, key_valid)
    row_max = jnp.max(scores, -1, keepdims=True)
    log_total = row_max + jnp.log(jnp.sum(jnp.exp(scores - row_max), -1, keepdims=True))
    probs = jnp.exp(scores - log_total)
    value_heads = values_all.reshape(values_all.shape[0], HEADS, HEAD_DIM)
    attended = jnp.einsum(
        "hsl,lhd->shd", probs.astype(jnp.bfloat16), value_heads, preferred_element_type=jnp.float32
    )
    attended = attended.reshape(row_count, -1).astype(jnp.bfloat16)
    mid_state = joined + project(attended, attn_out)
    normed_mid = rms_norm(mid_state, gain_second.astype(jnp.float32)).astype(jnp.bfloat16)
    gate_up = jnp.einsum("sd,cdf->csf", normed_mid, mlp_in, preferred_element_type=jnp.float32)
    hidden = (jax.nn.gelu(gate_up[0], approximate=True) * gate_up[1]).astype(jnp.bfloat16)
    out_state = mid_state + project(hidden, mlp_out)
    saved = (
        extended,
        mixed,
        joined,
        normed,
        projected,
        keys_all,
        values_all,
        log_total,
        attended,
        mid_state,
        normed_mid,
        gate_up,
        hidden,
    )
    return (out_state, saved)


def gated_unit(gate_in, up_in):
    return jax.nn.gelu(gate_in, approximate=True) * up_in


def layer_backward(grad_out, saved, weights, one_hot_ids, key_valid):
    (
        tap_rows,
        biases,
        join_matrix,
        join_shift,
        gain_first,
        attn_in,
        attn_out,
        pos_table,
        gain_second,
        mlp_in,
        mlp_out,
    ) = weights
    (
        extended,
        mixed,
        joined,
        normed,
        projected,
        keys_all,
        values_all,
        log_total,
        attended,
        mid_state,
        normed_mid,
        gate_up,
        hidden,
    ) = saved
    row_count = grad_out.shape[0]
    model_width = grad_out.shape[1]
    grad_branch = grad_out.astype(jnp.bfloat16)
    grad_mlp_out = project_left(hidden, grad_branch)
    grad_hidden = project_right(grad_branch, mlp_out)
    unused_value, gelu_back = jax.vjp(gated_unit, gate_up[0], gate_up[1])
    grad_gate, grad_up = gelu_back(grad_hidden)
    grad_gate_up = jnp.stack([grad_gate, grad_up]).astype(jnp.bfloat16)
    grad_mlp_in = jnp.einsum(
        "sd,csf->cdf", normed_mid, grad_gate_up, preferred_element_type=jnp.float32
    )
    grad_normed_mid = jnp.einsum(
        "csf,cdf->sd", grad_gate_up, mlp_in, preferred_element_type=jnp.float32
    )
    unused_mid, mid_back = jax.vjp(rms_norm, mid_state, gain_second.astype(jnp.float32))
    grad_mid_part, grad_gain_second = mid_back(grad_normed_mid)
    grad_mid = grad_out + grad_mid_part
    grad_attn = grad_mid.astype(jnp.bfloat16)
    grad_attn_out = project_left(attended, grad_attn)
    grad_attended = (
        project_right(grad_attn, attn_out).astype(jnp.bfloat16).reshape(row_count, HEADS, HEAD_DIM)
    )
    query = projected[0]
    scores = score_block(query, keys_all, pos_table, one_hot_ids, key_valid)
    probs = jnp.exp(scores - log_total)
    value_heads = values_all.reshape(values_all.shape[0], HEADS, HEAD_DIM)
    key_heads = keys_all.reshape(keys_all.shape[0], HEADS, HEAD_DIM)
    query_heads = query.reshape(row_count, HEADS, HEAD_DIM)
    grad_probs = jnp.einsum(
        "shd,lhd->hsl", grad_attended, value_heads, preferred_element_type=jnp.float32
    )
    row_delta = jnp.sum(probs * grad_probs, -1, keepdims=True)
    grad_scores = (probs * (grad_probs - row_delta)).astype(jnp.bfloat16)
    grad_table = jnp.einsum(
        "slb,hsl->bh", one_hot_ids, grad_scores, preferred_element_type=jnp.float32
    ).reshape(-1)
    grad_query = jnp.einsum(
        "hsl,lhd->shd", grad_scores, key_heads, preferred_element_type=jnp.float32
    ).reshape(row_count, -1)
    grad_values_all = jnp.einsum(
        "hsl,shd->lhd",
        probs.astype(jnp.bfloat16),
        grad_attended,
        preferred_element_type=jnp.float32,
    )
    grad_keys_all = jnp.einsum(
        "hsl,shd->lhd", grad_scores, query_heads, preferred_element_type=jnp.float32
    )
    key_total = grad_keys_all.shape[0]
    grad_key, grad_value = (
        lax.psum_scatter(
            grad_keys_all.reshape(key_total, -1).astype(jnp.bfloat16),
            "seq",
            scatter_dimension=0,
            tiled=True,
        ).astype(jnp.float32),
        lax.psum_scatter(
            grad_values_all.reshape(key_total, -1).astype(jnp.bfloat16),
            "seq",
            scatter_dimension=0,
            tiled=True,
        ).astype(jnp.float32),
    )
    grad_projected = jnp.stack([grad_query, grad_key, grad_value]).astype(jnp.bfloat16)
    grad_attn_in = jnp.einsum(
        "sd,csi->cdi", normed, grad_projected, preferred_element_type=jnp.float32
    )
    grad_normed = jnp.einsum(
        "csi,cdi->sd", grad_projected, attn_in, preferred_element_type=jnp.float32
    )
    unused_joined, joined_back = jax.vjp(rms_norm, joined, gain_first.astype(jnp.float32))
    grad_joined_part, grad_gain_first = joined_back(grad_normed)
    grad_joined = grad_mid + grad_joined_part
    grad_join = grad_joined.astype(jnp.bfloat16)
    grad_join_matrix = project_left(mixed, grad_join)
    grad_join_shift = jnp.sum(grad_join.astype(jnp.float32), 0)
    grad_mixed = project_right(grad_join, join_matrix).astype(jnp.bfloat16).astype(jnp.float32)
    grad_biases = jnp.broadcast_to(jnp.sum(grad_mixed, 0), (3, model_width))
    tap_float = tap_rows.astype(jnp.float32)
    grad_taps = [None] * 9
    grad_extended = jnp.zeros((row_count + 3, model_width), jnp.float32)
    for window, offset in windows:
        for tap_index in range(window):
            first_row = 4 - window + tap_index
            grad_taps[offset + tap_index] = jnp.sum(
                grad_mixed * extended[first_row : first_row + row_count], 0
            )
            grad_extended = grad_extended + jnp.pad(
                tap_float[offset + tap_index] * grad_mixed, ((first_row, 3 - first_row), (0, 0))
            )
    back_rows = passed_along(grad_extended[:3], "seq", -1)
    grad_in = grad_joined + grad_extended[3:] + jnp.pad(back_rows, ((row_count - 3, 0), (0, 0)))
    layer_grads = (
        jnp.stack(grad_taps),
        grad_biases,
        grad_join_matrix,
        grad_join_shift,
        grad_gain_first,
        grad_attn_in,
        grad_attn_out,
        grad_table,
        grad_gain_second,
        grad_mlp_in,
        grad_mlp_out,
    )
    return (grad_in, layer_grads)


def body(
    byte_states,
    teacher,
    lengths,
    conv_taps,
    conv_bias,
    join_weight,
    join_bias,
    gain_attn,
    attn_in_weight,
    attn_out_weight,
    position_bias,
    gain_mlp,
    mlp_in_weight,
    mlp_out_weight,
):
    layer_count = conv_taps.shape[0]
    micro_count = byte_states.shape[0]
    row_count = byte_states.shape[2]
    model_width = byte_states.shape[3]
    seq_total = row_count * lax.axis_size("seq")
    positions = lax.axis_index("seq") * row_count + jnp.arange(row_count)
    key_positions = jnp.arange(seq_total)
    bucket_grid = bucket_ids(key_positions[None, :] - positions[:, None])
    one_hot_ids = (bucket_grid[:, :, None] == jnp.arange(BUCKETS)[None, None, :]).astype(
        jnp.bfloat16
    )
    total_valid = lax.psum(jnp.sum(lengths.astype(jnp.float32)), "batch")
    sums = [None] * layer_count
    out_rows = []
    grad_rows = []
    local_squares = jnp.zeros((), jnp.float32)
    for batch_index in range(micro_count):
        state = byte_states[batch_index, 0].astype(jnp.float32)
        length = lengths[batch_index, 0]
        key_valid = key_positions < length
        row_valid = positions < length
        kept = []
        for layer_index in range(layer_count):
            weights = (
                lax.all_gather(conv_taps[layer_index], ("seq", "batch"), axis=1, tiled=True),
                lax.all_gather(conv_bias[layer_index], ("seq", "batch"), axis=1, tiled=True),
                lax.all_gather(join_weight[layer_index], ("seq", "batch"), axis=0, tiled=True),
                lax.all_gather(join_bias[layer_index], ("seq", "batch"), axis=0, tiled=True),
                lax.all_gather(gain_attn[layer_index], ("seq", "batch"), axis=0, tiled=True),
                lax.all_gather(attn_in_weight[layer_index], ("seq", "batch"), axis=1, tiled=True),
                lax.all_gather(attn_out_weight[layer_index], ("seq", "batch"), axis=0, tiled=True),
                lax.all_gather(position_bias[layer_index], ("seq", "batch"), axis=0, tiled=True),
                lax.all_gather(gain_mlp[layer_index], ("seq", "batch"), axis=0, tiled=True),
                lax.all_gather(mlp_in_weight[layer_index], ("seq", "batch"), axis=1, tiled=True),
                lax.all_gather(mlp_out_weight[layer_index], ("seq", "batch"), axis=0, tiled=True),
            )
            state, saved = layer_forward(state, weights, one_hot_ids, key_valid)
            kept.append(saved)
        out_rows.append(state)
        diff = jnp.where(
            row_valid[:, None], state - teacher[batch_index, 0].astype(jnp.float32), 0.0
        )
        local_squares = local_squares + jnp.sum(diff * diff)
        grad_state = 2.0 * diff / (total_valid * model_width)
        for layer_index in reversed(range(layer_count)):
            weights = (
                lax.all_gather(conv_taps[layer_index], ("seq", "batch"), axis=1, tiled=True),
                lax.all_gather(conv_bias[layer_index], ("seq", "batch"), axis=1, tiled=True),
                lax.all_gather(join_weight[layer_index], ("seq", "batch"), axis=0, tiled=True),
                lax.all_gather(join_bias[layer_index], ("seq", "batch"), axis=0, tiled=True),
                lax.all_gather(gain_attn[layer_index], ("seq", "batch"), axis=0, tiled=True),
                lax.all_gather(attn_in_weight[layer_index], ("seq", "batch"), axis=1, tiled=True),
                lax.all_gather(attn_out_weight[layer_index], ("seq", "batch"), axis=0, tiled=True),
                lax.all_gather(position_bias[layer_index], ("seq", "batch"), axis=0, tiled=True),
                lax.all_gather(gain_mlp[layer_index], ("seq", "batch"), axis=0, tiled=True),
                lax.all_gather(mlp_in_weight[layer_index], ("seq", "batch"), axis=1, tiled=True),
                lax.all_gather(mlp_out_weight[layer_index], ("seq", "batch"), axis=0, tiled=True),
            )
            grad_state, layer_grads = layer_backward(
                grad_state, kept[layer_index], weights, one_hot_ids, key_valid
            )
            if sums[layer_index] is None:
                sums[layer_index] = layer_grads
            else:
                sums[layer_index] = jax.tree.map(jnp.add, sums[layer_index], layer_grads)
        grad_rows.append(grad_state)
    loss = lax.psum(local_squares, ("seq", "batch")) / (total_valid * model_width)
    stacked_grads = tuple(
        (
            jnp.stack([sums[layer_index][member] for layer_index in range(layer_count)])
            for member in range(11)
        )
    )
    (
        grad_taps,
        grad_biases,
        grad_join_matrix,
        grad_join_shift,
        grad_gain_first,
        grad_attn_in,
        grad_attn_out,
        grad_table,
        grad_gain_second,
        grad_mlp_in,
        grad_mlp_out,
    ) = stacked_grads
    owned = (
        lax.psum_scatter(grad_taps, ("seq", "batch"), scatter_dimension=2, tiled=True),
        lax.psum_scatter(grad_biases, ("seq", "batch"), scatter_dimension=2, tiled=True),
        lax.psum_scatter(grad_join_matrix, ("seq", "batch"), scatter_dimension=1, tiled=True),
        lax.psum_scatter(grad_join_shift, ("seq", "batch"), scatter_dimension=1, tiled=True),
        lax.psum_scatter(grad_gain_first, ("seq", "batch"), scatter_dimension=1, tiled=True),
        lax.psum_scatter(grad_attn_in, ("seq", "batch"), scatter_dimension=2, tiled=True),
        lax.psum_scatter(grad_attn_out, ("seq", "batch"), scatter_dimension=1, tiled=True),
        lax.psum_scatter(grad_table, ("seq", "batch"), scatter_dimension=1, tiled=True),
        lax.psum_scatter(grad_gain_second, ("seq", "batch"), scatter_dimension=1, tiled=True),
        lax.psum_scatter(grad_mlp_in, ("seq", "batch"), scatter_dimension=2, tiled=True),
        lax.psum_scatter(grad_mlp_out, ("seq", "batch"), scatter_dimension=1, tiled=True),
    )
    activations = jnp.stack(out_rows)[:, None]
    input_grad = jnp.stack(grad_rows)[:, None]
    return (
        activations,
        loss,
        input_grad,
        owned[0],
        owned[1],
        owned[2],
        owned[3],
        owned[4],
        owned[5],
        owned[6],
        owned[7],
        owned[8],
        owned[9],
        owned[10],
    )


ALL = ("seq", "z", "core")
LOW = jnp.bfloat16
WIDE = jnp.float32
BLOCK = 256
MASKED = -1e30


def nt(left, right):
    return lax.dot_general(left, right, (((1,), (1,)), ((), ())), preferred_element_type=WIDE)


def nn(left, right):
    return lax.dot_general(left, right, (((1,), (0,)), ((), ())), preferred_element_type=WIDE)


def tn(left, right):
    return lax.dot_general(left, right, (((0,), (0,)), ((), ())), preferred_element_type=WIDE)


def band_kernel(line_ref, band_ref):
    wide = jnp.broadcast_to(line_ref[0], (BLOCK, 4 * BLOCK))
    rolled = pltpu.roll(wide, 0, 1, stride=1, stride_axis=0)
    band_ref[0, 0] = rolled[:, :BLOCK]
    band_ref[0, 1] = rolled[:, BLOCK : 2 * BLOCK]
    band_ref[0, 2] = rolled[:, 3 * BLOCK :]


def build_band(line):
    return pl.pallas_call(
        band_kernel,
        grid=(HEADS,),
        in_specs=[pl.BlockSpec((1, 1, 4 * BLOCK), lambda h: (h, 0, 0))],
        out_specs=pl.BlockSpec((1, 3, BLOCK, BLOCK), lambda h: (h, 0, 0, 0)),
        out_shape=jax.ShapeDtypeStruct((HEADS, 3, BLOCK, BLOCK), WIDE),
        name="bias_band",
    )(line.reshape(HEADS, 1, 4 * BLOCK))


def key_blocks(core, near):
    near_rows = pl.multiple_of(BLOCK * (1 - core), BLOCK)
    far_rows = pl.multiple_of(BLOCK * core, BLOCK)
    below, above = 1 + core, 2 - core
    if near:
        return near_rows, ((0, near_rows, 0), (0, far_rows, below), (1, far_rows, above), (1, near_rows, None))
    return far_rows, ((0, far_rows, 0), (0, near_rows, above), (1, far_rows, None), (1, near_rows, None))


def keys_with_mask(block, lane, head, first_position, length, constant):
    rows = first_position + lax.broadcasted_iota(jnp.int32, (BLOCK, 1), 0)
    mask = jnp.where(rows < length, 0.0, MASKED)
    spare = (1 - head) * HEAD_DIM
    extra = jnp.where(lane == spare, mask, jnp.where(lane == spare + 1, constant, 0.0))
    return jnp.where(lane // HEAD_DIM == head, block.astype(WIDE), extra).astype(LOW)


def query_with_ones(block, lane, head):
    spare = (1 - head) * HEAD_DIM
    extra = jnp.where((lane == spare) | (lane == spare + 1), 1.0, 0.0)
    return jnp.where(lane // HEAD_DIM == head, block.astype(WIDE), extra).astype(LOW)


def only_head(block, lane, head):
    return jnp.where(lane // HEAD_DIM == head, block.astype(WIDE), 0.0).astype(LOW)


def attend_kernel(
    info_ref, far_ref, q_ref, k_ref, v_ref, ko_ref, vo_ref, band_ref, out_ref, lse_ref, score_ref
):
    core, length = info_ref[0], info_ref[1]
    pair = pl.program_id(0)
    lane = lax.broadcasted_iota(jnp.int32, (1, 2 * HEAD_DIM), 1)
    for n in range(2):
        q_rows, blocks = key_blocks(core, n == 0)
        query = q_ref[pl.ds(q_rows, BLOCK), :]
        halves = []
        for head in range(2):
            q_low = query_with_ones(query, lane, head)
            top = None
            for b, (side, start, slot) in enumerate(blocks):
                first = 2 * BLOCK * (core if side == 0 else 1 - core) + start
                keys = (k_ref, ko_ref)[side][pl.ds(start, BLOCK), :]
                constant = far_ref[2 * pair + head] if slot is None else 0.0
                scores = nt(keys_with_mask(keys, lane, head, first, length, constant), q_low)
                if slot is not None:
                    scores = scores + band_ref[head, slot]
                score_ref[b] = scores
                block_top = jnp.max(scores, 0, keepdims=True)
                top = block_top if top is None else jnp.maximum(top, block_top)
            total = jnp.zeros((1, BLOCK), WIDE)
            mixed = jnp.zeros((2 * HEAD_DIM, BLOCK), WIDE)
            for b, (side, start, slot) in enumerate(blocks):
                weights = jnp.exp(score_ref[b] - top)
                total = total + jnp.sum(weights, 0, keepdims=True)
                values = (v_ref, vo_ref)[side][pl.ds(start, BLOCK), :]
                mixed = mixed + tn(values, weights.astype(LOW))
            lse_ref[0, n, head : head + 1, :] = top + jnp.log(total)
            halves.append((mixed / total)[head * HEAD_DIM : (head + 1) * HEAD_DIM])
        out_ref[pl.ds(q_rows, BLOCK), :] = jnp.transpose(jnp.concatenate(halves, 0)).astype(LOW)


def attend(info, far, projected, others, band):
    rows = projected.shape[0]
    pairs = HEADS // 2
    width = 2 * HEAD_DIM
    col = lambda shift: pl.BlockSpec((rows, width), lambda p: (0, p + shift))
    return pl.pallas_call(
        attend_kernel,
        grid=(pairs,),
        in_specs=[
            pl.BlockSpec(memory_space=pltpu.SMEM),
            pl.BlockSpec(memory_space=pltpu.SMEM),
            col(0),
            col(pairs),
            col(2 * pairs),
            col(0),
            col(pairs),
            pl.BlockSpec((2, 3, BLOCK, BLOCK), lambda p: (p, 0, 0, 0)),
        ],
        out_specs=[col(0), pl.BlockSpec((1, 2, 2, BLOCK), lambda p: (p, 0, 0, 0))],
        out_shape=[
            jax.ShapeDtypeStruct((rows, HEADS * HEAD_DIM), LOW),
            jax.ShapeDtypeStruct((pairs, 2, 2, BLOCK), WIDE),
        ],
        scratch_shapes=[pltpu.VMEM((4, BLOCK, BLOCK), WIDE)],
        name="attend",
    )(info, far, projected, projected, projected, others, others, band)


def attend_back_kernel(
    info_ref,
    far_ref,
    q_ref,
    k_ref,
    v_ref,
    ko_ref,
    vo_ref,
    band_ref,
    out_ref,
    gout_ref,
    lse_ref,
    gq_ref,
    gown_ref,
    goth_ref,
    gband_ref,
    gfar_ref,
    gk_acc,
    gv_acc,
    band_acc,
    far_acc,
):
    core, length = info_ref[0], info_ref[1]
    pair = pl.program_id(0)
    width = 2 * HEAD_DIM
    lane = lax.broadcasted_iota(jnp.int32, (1, width), 1)
    gk_acc[...] = jnp.zeros_like(gk_acc)
    gv_acc[...] = jnp.zeros_like(gv_acc)
    band_acc[...] = jnp.zeros_like(band_acc)
    far_acc[...] = jnp.zeros_like(far_acc)
    select = jnp.where(
        lax.broadcasted_iota(jnp.int32, (8, width), 0)
        == lax.broadcasted_iota(jnp.int32, (8, width), 1) // HEAD_DIM,
        1.0,
        0.0,
    )
    for n in range(2):
        q_rows, blocks = key_blocks(core, n == 0)
        query = q_ref[pl.ds(q_rows, BLOCK), :]
        gout = gout_ref[pl.ds(q_rows, BLOCK), :]
        dots = gout.astype(WIDE) * out_ref[pl.ds(q_rows, BLOCK), :].astype(WIDE)
        deltas = lax.dot_general(
            select,
            dots,
            (((1,), (1,)), ((), ())),
            precision=lax.Precision.HIGHEST,
            preferred_element_type=WIDE,
        )
        halves = []
        for head in range(2):
            q_ones = query_with_ones(query, lane, head)
            q_low = only_head(query, lane, head)
            g_low = only_head(gout, lane, head)
            lse = lse_ref[0, n, head : head + 1, :]
            delta = deltas[head : head + 1]
            gq = jnp.zeros((width, BLOCK), WIDE)
            for side, start, slot in blocks:
                first = 2 * BLOCK * (core if side == 0 else 1 - core) + start
                keys = (k_ref, ko_ref)[side][pl.ds(start, BLOCK), :]
                values = (v_ref, vo_ref)[side][pl.ds(start, BLOCK), :]
                constant = far_ref[2 * pair + head] if slot is None else 0.0
                scores = nt(keys_with_mask(keys, lane, head, first, length, constant), q_ones)
                if slot is not None:
                    scores = scores + band_ref[head, slot]
                probs = jnp.exp(scores - lse)
                gprobs = nt(values, g_low)
                gscores = probs * (gprobs - delta)
                if slot is None:
                    part = jnp.sum(gscores.reshape(BLOCK // 8, 8, BLOCK), 0)
                    far_acc[head] = far_acc[head] + part
                else:
                    band_acc[head, slot] = band_acc[head, slot] + gscores
                gs_low = gscores.astype(LOW)
                at = pl.ds(2 * BLOCK * side + start, BLOCK)
                gv_acc[at, :] = gv_acc[at, :] + nn(probs.astype(LOW), g_low)
                gk_acc[at, :] = gk_acc[at, :] + nn(gs_low, q_low)
                gq = gq + tn(keys, gs_low)
            halves.append(gq[head * HEAD_DIM : (head + 1) * HEAD_DIM])
        gq_ref[pl.ds(q_rows, BLOCK), :] = jnp.transpose(jnp.concatenate(halves, 0)).astype(LOW)
    own = 2 * BLOCK
    gown_ref[0] = gk_acc[:own, :]
    gown_ref[1] = gv_acc[:own, :]
    goth_ref[0] = gk_acc[own:, :].astype(LOW)
    goth_ref[1] = gv_acc[own:, :].astype(LOW)
    span = 4 * BLOCK
    gap = jnp.zeros((8, BLOCK), WIDE)
    row = lax.broadcasted_iota(jnp.int32, (8, span), 0)
    for head in range(2):
        lines = jnp.zeros((8, span), WIDE)
        for g in range(BLOCK // 8):
            rows = slice(8 * g, 8 * g + 8)
            piece = jnp.concatenate(
                [band_acc[head, 0, rows], band_acc[head, 1, rows], gap, band_acc[head, 2, rows]], 1
            )
            lines = lines + (pltpu.roll(piece, span - 8 * g, 1) if g else piece)
        for bit in (1, 2, 4):
            lines = jnp.where((row & bit) != 0, pltpu.roll(lines, span - bit, 1), lines)
        gband_ref[0, head : head + 1, :] = jnp.sum(lines, 0, keepdims=True)
        gfar_ref[0, head : head + 1, :] = jnp.sum(far_acc[head], 0, keepdims=True)


def attend_back(info, far, projected, others, band, out, gout, lse):
    rows = projected.shape[0]
    pairs = HEADS // 2
    width = 2 * HEAD_DIM
    inner = HEADS * HEAD_DIM
    col = lambda shift: pl.BlockSpec((rows, width), lambda p: (0, p + shift))
    two = pl.BlockSpec((2, rows, width), lambda p: (0, 0, p))
    return pl.pallas_call(
        attend_back_kernel,
        grid=(pairs,),
        in_specs=[
            pl.BlockSpec(memory_space=pltpu.SMEM),
            pl.BlockSpec(memory_space=pltpu.SMEM),
            col(0),
            col(pairs),
            col(2 * pairs),
            col(0),
            col(pairs),
            pl.BlockSpec((2, 3, BLOCK, BLOCK), lambda p: (p, 0, 0, 0)),
            col(0),
            col(0),
            pl.BlockSpec((1, 2, 2, BLOCK), lambda p: (p, 0, 0, 0)),
        ],
        out_specs=[
            col(0),
            two,
            two,
            pl.BlockSpec((1, 2, 4 * BLOCK), lambda p: (p, 0, 0)),
            pl.BlockSpec((1, 2, BLOCK), lambda p: (p, 0, 0)),
        ],
        out_shape=[
            jax.ShapeDtypeStruct((rows, inner), LOW),
            jax.ShapeDtypeStruct((2, rows, inner), WIDE),
            jax.ShapeDtypeStruct((2, rows, inner), LOW),
            jax.ShapeDtypeStruct((pairs, 2, 4 * BLOCK), WIDE),
            jax.ShapeDtypeStruct((pairs, 2, BLOCK), WIDE),
        ],
        scratch_shapes=[
            pltpu.VMEM((4 * BLOCK, width), WIDE),
            pltpu.VMEM((4 * BLOCK, width), WIDE),
            pltpu.VMEM((2, 3, BLOCK, BLOCK), WIDE),
            pltpu.VMEM((2, 8, BLOCK), WIDE),
        ],
        name="attend_back",
    )(info, far, projected, projected, projected, others, others, band, out, gout, lse)


def chip_body(
    byte_states,
    teacher,
    lengths,
    conv_taps,
    conv_bias,
    join_weight,
    join_bias,
    gain_attn,
    attn_in_weight,
    attn_out_weight,
    position_bias,
    gain_mlp,
    mlp_in_weight,
    mlp_out_weight,
):
    layer_count = conv_taps.shape[0]
    model_width = byte_states.shape[3]
    slot_rows = byte_states.shape[2]
    rows = 2 * slot_rows
    hidden_width = mlp_in_weight.shape[3]
    quarters = hidden_width // model_width
    seqs, zs, cores = (lax.axis_size(name) for name in ALL)
    devices = seqs * zs * cores
    share = model_width // devices
    s_at, z_at, c_at = (lax.axis_index(name) for name in ALL)
    device_at = (s_at * zs + z_at) * cores + c_at

    def number(s, z, c):
        return (s * zs + z) * cores + c

    places = [(s, z, c) for s in range(seqs) for z in range(zs) for c in range(cores)]
    swap = [(number(s, z, c), number(s, z, 1 - c)) for s, z, c in places]
    routes = [
        [(number(s, z, c), number(2 * (s % 2 if turn == 0 else 1 - s % 2) + c, z, s // 2)) for s, z, c in places]
        for turn in range(2)
    ]
    back_routes = [[(b, a) for a, b in route] for route in routes]

    def to_chips(block):
        odd, high = s_at % 2, s_at // 2
        first, second = (
            lax.ppermute(jnp.where(odd == turn, block[0], block[1]), ALL, routes[turn]) for turn in range(2)
        )
        return jnp.concatenate(
            [jnp.where(high == 0, first, second), jnp.where(high == 0, second, first)], 0
        )

    def from_chips(block):
        odd, high = s_at % 2, s_at // 2
        halves = (block[:slot_rows], block[slot_rows:])
        first, second = (
            lax.ppermute(jnp.where(high == turn, halves[0], halves[1]), ALL, back_routes[turn])
            for turn in range(2)
        )
        return jnp.stack([jnp.where(odd == 0, first, second), jnp.where(odd == 0, second, first)])

    def trade(block):
        return lax.ppermute(block, ALL, swap)

    to_high = [(number(s, z, 0), number(s, z, 1)) for s, z, c in places if c == 0]
    to_low = [(b, a) for a, b in to_high]

    lanes = jnp.arange(model_width)
    lane_owner, lane_item = lanes // share, lanes % share
    spread = (lanes[None, :] == device_at * share + jnp.arange(share)[:, None]).astype(LOW)
    length_parts = jnp.stack([lengths[:, 0] // 32, lengths[:, 0] % 32], 1).reshape(-1)

    def packed(l):
        last = jnp.concatenate(
            [
                position_bias[l],
                length_parts.astype(LOW),
                jnp.zeros((share - HEADS - length_parts.shape[0],), LOW),
            ]
        )
        small = jnp.concatenate(
            [
                conv_taps[l],
                conv_bias[l],
                join_bias[l][None],
                gain_attn[l][None],
                gain_mlp[l][None],
                last[None],
            ],
            0,
        )
        small = jnp.dot(small, spread, preferred_element_type=WIDE).astype(LOW)
        inward = mlp_in_weight[l].reshape(2, share, quarters, model_width)
        return jnp.concatenate(
            [
                join_weight[l],
                attn_in_weight[l].reshape(3 * share, model_width),
                attn_out_weight[l],
                inward.transpose(0, 2, 1, 3).reshape(2 * quarters * share, model_width),
                mlp_out_weight[l],
                small,
            ],
            0,
        )

    gathered = [
        lax.all_gather(packed(l), ALL, axis=0, tiled=False).reshape(devices, -1, share, model_width)
        for l in range(layer_count)
    ]

    def unpack(whole):
        small = jnp.sum(whole[:, -1].astype(WIDE), 0)
        square = lambda at: whole[:, at].reshape(model_width, model_width)
        wide = lambda at, count: (
            whole[:, at : at + count].transpose(0, 2, 1, 3).reshape(model_width, count * model_width)
        )
        return dict(
            join=square(0),
            attn_in=wide(1, 3),
            attn_out=square(4),
            gate=wide(5, quarters),
            up=wide(5 + quarters, quarters),
            mlp_out=whole[:, 5 + 2 * quarters : 5 + 3 * quarters].reshape(hidden_width, model_width),
            taps=jnp.stack(
                [
                    small[5],
                    small[2] + small[6],
                    small[0] + small[3] + small[7],
                    small[1] + small[4] + small[8],
                ]
            ),
            bias=small[9] + small[10] + small[11],
            join_bias=small[12],
            gain_attn=small[13],
            gain_mlp=small[14],
            last=small[15],
        )

    weights = [unpack(whole) for whole in gathered]
    state = to_chips(byte_states[:, 0]).astype(WIDE)
    target = to_chips(teacher[:, 0])

    counts = weights[0]["last"]
    scale = jnp.where((lane_item >= HEADS) & (lane_item < HEADS + 4), jnp.where(lane_item % 2 == 0, 32.0, 1.0), 0.0)
    total_valid = jnp.sum(jnp.where(lane_owner < zs * cores, counts * scale, 0.0))
    mine = (lane_owner == z_at * cores + s_at % 2) & ((lane_item - HEADS) // 2 == s_at // 2)
    length = jnp.sum(jnp.where(mine, counts * scale, 0.0)).astype(jnp.int32)
    info = jnp.stack([c_at.astype(jnp.int32), length])
    row_valid = (rows * c_at + jnp.arange(rows) < length)[:, None]

    offsets = -((jnp.arange(4 * BLOCK) + 2 * BLOCK) % (4 * BLOCK) - 2 * BLOCK)
    in_bucket = (lane_owner[:, None] == bucket_ids(offsets)[None, :]).astype(LOW)
    of_head = (lane_item[None, :] == jnp.arange(HEADS)[:, None]).astype(WIDE)
    far_bucket = (lane_owner == jnp.where(c_at == 0, 31, 15)).astype(WIDE)

    def normed(values, gain):
        inverse = lax.rsqrt(jnp.mean(values * values, -1, keepdims=True) + eps)
        return (values * inverse * gain).astype(LOW)

    def normed_back(grad, values, gain):
        inverse = lax.rsqrt(jnp.mean(values * values, -1, keepdims=True) + eps)
        unit = values * inverse
        scaled = grad * gain
        grad_in = inverse * (scaled - unit * jnp.mean(scaled * unit, -1, keepdims=True))
        return grad_in, jnp.sum(grad * unit, 0)

    kept = []
    for l in range(layer_count):
        w = weights[l]
        low_state = state.astype(LOW)
        prior = lax.ppermute(low_state[rows - 8 :], ALL, to_high)[5:]
        extended = jnp.concatenate([prior, low_state], 0).astype(WIDE)
        mixed = w["bias"] + sum(w["taps"][k] * extended[k : k + rows] for k in range(4))
        mixed = mixed.astype(LOW)
        joined = state + nn(mixed, w["join"]) + w["join_bias"]
        norm_a = normed(joined, w["gain_attn"])
        projected = nn(norm_a, w["attn_in"]).astype(LOW)
        others = trade(projected[:, HEADS * HEAD_DIM :])
        line = jnp.dot(
            (of_head * w["last"]).astype(LOW), in_bucket, preferred_element_type=WIDE
        )
        far = jnp.sum(of_head * (w["last"] * far_bucket), 1)
        band = build_band(line)
        attended, lse = attend(info, far, projected, others, band)
        mid = joined + nn(attended, w["attn_out"])
        norm_m = normed(mid, w["gain_mlp"])
        gate = nn(norm_m, w["gate"])
        up = nn(norm_m, w["up"])
        hidden = (jax.nn.gelu(gate, approximate=True) * up).astype(LOW)
        state = mid + nn(hidden, w["mlp_out"])
        kept.append(
            (extended, mixed, joined, norm_a, projected, others, far, band, attended, lse, mid, norm_m, gate, up, hidden)
        )

    activations = from_chips(state)[:, None]
    diff = jnp.where(row_valid, state - target.astype(WIDE), 0.0)
    squares = jnp.sum(diff * diff, 0)
    grad = 2.0 * diff / (total_valid * model_width)
    results = [None] * layer_count
    for l in reversed(range(layer_count)):
        w = weights[l]
        (extended, mixed, joined, norm_a, projected, others, far, band, attended, lse, mid, norm_m, gate, up, hidden) = kept[l]
        g_low = grad.astype(LOW)
        g_mlp_out = tn(hidden, g_low).astype(LOW)
        g_hidden = nt(g_low, w["mlp_out"])
        unused, gelu_back = jax.vjp(gated_unit, gate, up)
        g_gate, g_up = (part.astype(LOW) for part in gelu_back(g_hidden))
        g_in = [tn(norm_m, part).astype(LOW) for part in (g_gate, g_up)]
        g_norm = nt(g_gate, w["gate"]) + nt(g_up, w["up"])
        g_mid, g_gain_mlp = normed_back(g_norm, mid, w["gain_mlp"])
        g_mid = grad + g_mid
        g_mid_low = g_mid.astype(LOW)
        g_attn_out = tn(attended, g_mid_low).astype(LOW)
        g_att = nt(g_mid_low, w["attn_out"]).astype(LOW)
        g_query, g_own, g_other, g_band, g_far = attend_back(
            info, far, projected, others, band, attended, g_att, lse
        )
        g_kv = (g_own + trade(g_other).astype(WIDE)).astype(LOW)
        g_proj = jnp.concatenate([g_query, g_kv[0], g_kv[1]], 1)
        g_attn_in = tn(norm_a, g_proj).astype(LOW)
        g_norm = nt(g_proj, w["attn_in"])
        g_joined, g_gain_attn = normed_back(g_norm, joined, w["gain_attn"])
        g_joined = g_mid + g_joined
        g_join_low = g_joined.astype(LOW)
        g_join = tn(mixed, g_join_low).astype(LOW)
        g_join_bias = jnp.sum(g_join_low.astype(WIDE), 0)
        g_mixed = nt(g_join_low, w["join"]).astype(LOW).astype(WIDE)
        g_taps = [jnp.sum(g_mixed * extended[k : k + rows], 0) for k in range(4)]
        g_bias = jnp.sum(g_mixed, 0)
        head_rows = [
            sum(w["taps"][k] * g_mixed[r - k : r - k + 1] for k in range(r + 1)) for r in range(3)
        ]
        beyond = lax.ppermute(
            jnp.concatenate(head_rows + [jnp.zeros((5, model_width), WIDE)], 0), ALL, to_low
        )
        padded = jnp.concatenate([g_mixed, jnp.zeros((3, model_width), WIDE)], 0)
        g_state = sum(w["taps"][k] * padded[3 - k : 3 - k + rows] for k in range(4))
        tail = jnp.concatenate([jnp.zeros((rows - 8, model_width), WIDE), jnp.zeros((5, model_width), WIDE), beyond[:3]], 0)
        grad = g_joined + g_state + tail

        by_lane = jnp.dot(
            g_band.reshape(HEADS, -1),
            in_bucket.T.astype(WIDE),
            precision=lax.Precision.HIGHEST,
            preferred_element_type=WIDE,
        )
        g_far = jnp.sum(g_far.reshape(HEADS, -1), 1)[:, None]
        g_last = jnp.sum(of_head * (by_lane + g_far * far_bucket), 0)
        small = jnp.stack(
            g_taps
            + [g_bias, g_join_bias, g_gain_attn, g_gain_mlp, g_last, squares]
            + [jnp.zeros((model_width,), WIDE)] * (share - 10)
        ).astype(LOW)
        split = lambda whole: whole.reshape(devices, share, -1, model_width).transpose(0, 2, 1, 3)
        terms = jnp.concatenate(
            [
                split(g_join),
                split(g_attn_in),
                split(g_attn_out),
                split(g_in[0]),
                split(g_in[1]),
                g_mlp_out.reshape(devices, quarters, share, model_width),
                jnp.broadcast_to(small[None, None], (devices, 1, share, model_width)),
            ],
            1,
        ).reshape(seqs, zs, cores, -1, model_width)
        kept_half = jnp.where(c_at == 0, terms[:, :, 0], terms[:, :, 1])
        sent_half = jnp.where(c_at == 0, terms[:, :, 1], terms[:, :, 0])
        half = (kept_half.astype(WIDE) + trade(sent_half).astype(WIDE)).astype(LOW)
        half = lax.psum_scatter(half, "seq", scatter_dimension=0, tiled=False)
        results[l] = lax.psum_scatter(half, "z", scatter_dimension=0, tiled=False)

    input_grad = from_chips(grad)[:, None]
    owned = [result.astype(WIDE).reshape(-1, share, model_width) for result in results]
    small = [lax.dynamic_slice_in_dim(part[-1], device_at * share, share, 1) for part in owned]
    stack = lambda pick: jnp.stack([pick(l) for l in range(layer_count)])
    taps_at = (2, 3, 1, 2, 3, 0, 1, 2, 3)
    loss = jnp.sum(owned[-1][-1][9]) / (total_valid * model_width)
    inward = lambda part: part.transpose(1, 0, 2).reshape(share, hidden_width)
    return (
        activations,
        loss,
        input_grad,
        stack(lambda l: jnp.stack([small[l][k] for k in taps_at])),
        stack(lambda l: jnp.broadcast_to(small[l][4], (3, share))),
        stack(lambda l: owned[l][0]),
        stack(lambda l: small[l][5]),
        stack(lambda l: small[l][6]),
        stack(lambda l: owned[l][1:4]),
        stack(lambda l: owned[l][4]),
        stack(lambda l: small[l][8][:HEADS]),
        stack(lambda l: small[l][7]),
        stack(
            lambda l: jnp.stack(
                [inward(owned[l][5 : 5 + quarters]), inward(owned[l][5 + quarters : 5 + 2 * quarters])]
            )
        ),
        stack(lambda l: owned[l][5 + 2 * quarters : 5 + 3 * quarters].reshape(-1, model_width)),
    )


def chip_plan(mesh):
    grid = Mesh(
        mesh.devices.reshape(mesh.shape["seq"], mesh.shape["batch"] // 2, 2),
        ALL,
    )
    batch = ("z", "core")
    in_specs = (
        P(None, batch, "seq", None),
        P(None, batch, "seq", None),
        P(None, batch),
        P(None, None, ALL),
        P(None, None, ALL),
        P(None, ALL, None),
        P(None, ALL),
        P(None, ALL),
        P(None, None, ALL, None),
        P(None, ALL, None),
        P(None, ALL),
        P(None, ALL),
        P(None, None, ALL, None),
        P(None, ALL, None),
    )
    out_specs = (in_specs[0], P(), in_specs[0]) + in_specs[3:]
    return jax.shard_map(chip_body, mesh=grid, in_specs=in_specs, out_specs=out_specs, check_vma=False)


def shared_plan(mesh):
    in_specs = (
        P(None, "batch", "seq", None),
        P(None, "batch", "seq", None),
        P(None, "batch"),
        P(None, None, ("seq", "batch")),
        P(None, None, ("seq", "batch")),
        P(None, ("seq", "batch"), None),
        P(None, ("seq", "batch")),
        P(None, ("seq", "batch")),
        P(None, None, ("seq", "batch"), None),
        P(None, ("seq", "batch"), None),
        P(None, ("seq", "batch")),
        P(None, ("seq", "batch")),
        P(None, None, ("seq", "batch"), None),
        P(None, ("seq", "batch"), None),
    )
    out_specs = (
        P(None, "batch", "seq", None),
        P(),
        P(None, "batch", "seq", None),
        P(None, None, ("seq", "batch")),
        P(None, None, ("seq", "batch")),
        P(None, ("seq", "batch"), None),
        P(None, ("seq", "batch")),
        P(None, ("seq", "batch")),
        P(None, None, ("seq", "batch"), None),
        P(None, ("seq", "batch"), None),
        P(None, ("seq", "batch")),
        P(None, ("seq", "batch")),
        P(None, None, ("seq", "batch"), None),
        P(None, ("seq", "batch"), None),
    )
    return jax.shard_map(body, mesh=mesh, in_specs=in_specs, out_specs=out_specs, check_vma=False)


def solution(mesh):
    shared = shared_plan(mesh)

    def run(*arrays):
        sequences = arrays[0].shape[0] * arrays[0].shape[1]
        one_per_chip = 2 * sequences == mesh.devices.size and 2 * arrays[0].shape[0] == mesh.shape["seq"]
        lanes_fit = arrays[5].shape[1] == 16 * mesh.devices.size and arrays[0].shape[2] == 4 * BLOCK
        plan = chip_plan(mesh) if one_per_chip and lanes_fit else shared
        return plan(*arrays)

    return run
```

```python
import jax
import jax.numpy as jnp
from jax import lax
from jax.experimental import pallas as pl
from jax.experimental.pallas import tpu as pltpu
from jax.sharding import Mesh
from jax.sharding import PartitionSpec as P

HEADS = 8
HEAD_DIM = 64
BUCKETS = 32


eps = 1e-06
bounds = (12, 16, 23, 32, 46, 64, 91)
windows = ((2, 0), (3, 2), (4, 5))


def passed_along(block, axis, distance):
    devices = range(lax.axis_size(axis))
    route = [(i - distance, i) for i in devices if i - distance in devices]
    return lax.ppermute(block, axis, route)


def bucket_ids(offsets):
    magnitude = jnp.abs(offsets)
    far_ids = 8 + sum(((magnitude >= bound_value).astype(jnp.int32) for bound_value in bounds))
    near_ids = jnp.where(magnitude < 8, magnitude, far_ids)
    return jnp.where(offsets > 0, 16, 0) + near_ids


def rms_norm(values, gain):
    return values * lax.rsqrt(jnp.mean(values * values, -1, keepdims=True) + eps) * gain


def conv_sum(extended, tap_rows, biases, row_count):
    total = jnp.zeros((row_count, extended.shape[1]), jnp.float32) + jnp.sum(biases, 0)
    for window, offset in windows:
        for tap_index in range(window):
            first_row = 4 - window + tap_index
            total = (
                total + tap_rows[offset + tap_index] * extended[first_row : first_row + row_count]
            )
    return total


def project(left, right):
    return jnp.dot(left, right, preferred_element_type=jnp.float32)


def project_left(left, right):
    return lax.dot_general(
        left, right, (((0,), (0,)), ((), ())), preferred_element_type=jnp.float32
    )


def project_right(left, right):
    return lax.dot_general(
        left, right, (((1,), (1,)), ((), ())), preferred_element_type=jnp.float32
    )


def score_block(query, keys_all, pos_table, one_hot_ids, key_valid):
    query_heads = query.reshape(query.shape[0], HEADS, HEAD_DIM)
    key_heads = keys_all.reshape(keys_all.shape[0], HEADS, HEAD_DIM)
    rel_bias = jnp.einsum(
        "slb,bh->hsl",
        one_hot_ids,
        pos_table.reshape(BUCKETS, HEADS),
        preferred_element_type=jnp.float32,
    )
    scores = (
        jnp.einsum("shd,lhd->hsl", query_heads, key_heads, preferred_element_type=jnp.float32)
        + rel_bias
    )
    return jnp.where(key_valid[None, None, :], scores, -1e30)


def layer_forward(state, weights, one_hot_ids, key_valid):
    (
        tap_rows,
        biases,
        join_matrix,
        join_shift,
        gain_first,
        attn_in,
        attn_out,
        pos_table,
        gain_second,
        mlp_in,
        mlp_out,
    ) = weights
    row_count = state.shape[0]
    rounded_in = state.astype(jnp.bfloat16)
    prior_rows = passed_along(rounded_in[row_count - 3 :], "seq", 1)
    extended = jnp.concatenate([prior_rows, rounded_in], 0).astype(jnp.float32)
    mixed = conv_sum(
        extended, tap_rows.astype(jnp.float32), biases.astype(jnp.float32), row_count
    ).astype(jnp.bfloat16)
    joined = state + project(mixed, join_matrix) + join_shift.astype(jnp.float32)
    normed = rms_norm(joined, gain_first.astype(jnp.float32)).astype(jnp.bfloat16)
    projected = jnp.einsum(
        "sd,cdi->csi", normed, attn_in, preferred_element_type=jnp.float32
    ).astype(jnp.bfloat16)
    keys_all, values_all = (
        lax.all_gather(projected[1], "seq", axis=0, tiled=True),
        lax.all_gather(projected[2], "seq", axis=0, tiled=True),
    )
    scores = score_block(projected[0], keys_all, pos_table, one_hot_ids, key_valid)
    row_max = jnp.max(scores, -1, keepdims=True)
    log_total = row_max + jnp.log(jnp.sum(jnp.exp(scores - row_max), -1, keepdims=True))
    probs = jnp.exp(scores - log_total)
    value_heads = values_all.reshape(values_all.shape[0], HEADS, HEAD_DIM)
    attended = jnp.einsum(
        "hsl,lhd->shd", probs.astype(jnp.bfloat16), value_heads, preferred_element_type=jnp.float32
    )
    attended = attended.reshape(row_count, -1).astype(jnp.bfloat16)
    mid_state = joined + project(attended, attn_out)
    normed_mid = rms_norm(mid_state, gain_second.astype(jnp.float32)).astype(jnp.bfloat16)
    gate_up = jnp.einsum("sd,cdf->csf", normed_mid, mlp_in, preferred_element_type=jnp.float32)
    hidden = (jax.nn.gelu(gate_up[0], approximate=True) * gate_up[1]).astype(jnp.bfloat16)
    out_state = mid_state + project(hidden, mlp_out)
    saved = (
        extended,
        mixed,
        joined,
        normed,
        projected,
        keys_all,
        values_all,
        log_total,
        attended,
        mid_state,
        normed_mid,
        gate_up,
        hidden,
    )
    return (out_state, saved)


def gated_unit(gate_in, up_in):
    return jax.nn.gelu(gate_in, approximate=True) * up_in


def layer_backward(grad_out, saved, weights, one_hot_ids, key_valid):
    (
        tap_rows,
        biases,
        join_matrix,
        join_shift,
        gain_first,
        attn_in,
        attn_out,
        pos_table,
        gain_second,
        mlp_in,
        mlp_out,
    ) = weights
    (
        extended,
        mixed,
        joined,
        normed,
        projected,
        keys_all,
        values_all,
        log_total,
        attended,
        mid_state,
        normed_mid,
        gate_up,
        hidden,
    ) = saved
    row_count = grad_out.shape[0]
    model_width = grad_out.shape[1]
    grad_branch = grad_out.astype(jnp.bfloat16)
    grad_mlp_out = project_left(hidden, grad_branch)
    grad_hidden = project_right(grad_branch, mlp_out)
    unused_value, gelu_back = jax.vjp(gated_unit, gate_up[0], gate_up[1])
    grad_gate, grad_up = gelu_back(grad_hidden)
    grad_gate_up = jnp.stack([grad_gate, grad_up]).astype(jnp.bfloat16)
    grad_mlp_in = jnp.einsum(
        "sd,csf->cdf", normed_mid, grad_gate_up, preferred_element_type=jnp.float32
    )
    grad_normed_mid = jnp.einsum(
        "csf,cdf->sd", grad_gate_up, mlp_in, preferred_element_type=jnp.float32
    )
    unused_mid, mid_back = jax.vjp(rms_norm, mid_state, gain_second.astype(jnp.float32))
    grad_mid_part, grad_gain_second = mid_back(grad_normed_mid)
    grad_mid = grad_out + grad_mid_part
    grad_attn = grad_mid.astype(jnp.bfloat16)
    grad_attn_out = project_left(attended, grad_attn)
    grad_attended = (
        project_right(grad_attn, attn_out).astype(jnp.bfloat16).reshape(row_count, HEADS, HEAD_DIM)
    )
    query = projected[0]
    scores = score_block(query, keys_all, pos_table, one_hot_ids, key_valid)
    probs = jnp.exp(scores - log_total)
    value_heads = values_all.reshape(values_all.shape[0], HEADS, HEAD_DIM)
    key_heads = keys_all.reshape(keys_all.shape[0], HEADS, HEAD_DIM)
    query_heads = query.reshape(row_count, HEADS, HEAD_DIM)
    grad_probs = jnp.einsum(
        "shd,lhd->hsl", grad_attended, value_heads, preferred_element_type=jnp.float32
    )
    row_delta = jnp.sum(probs * grad_probs, -1, keepdims=True)
    grad_scores = (probs * (grad_probs - row_delta)).astype(jnp.bfloat16)
    grad_table = jnp.einsum(
        "slb,hsl->bh", one_hot_ids, grad_scores, preferred_element_type=jnp.float32
    ).reshape(-1)
    grad_query = jnp.einsum(
        "hsl,lhd->shd", grad_scores, key_heads, preferred_element_type=jnp.float32
    ).reshape(row_count, -1)
    grad_values_all = jnp.einsum(
        "hsl,shd->lhd",
        probs.astype(jnp.bfloat16),
        grad_attended,
        preferred_element_type=jnp.float32,
    )
    grad_keys_all = jnp.einsum(
        "hsl,shd->lhd", grad_scores, query_heads, preferred_element_type=jnp.float32
    )
    key_total = grad_keys_all.shape[0]
    grad_key, grad_value = (
        lax.psum_scatter(
            grad_keys_all.reshape(key_total, -1).astype(jnp.bfloat16),
            "seq",
            scatter_dimension=0,
            tiled=True,
        ).astype(jnp.float32),
        lax.psum_scatter(
            grad_values_all.reshape(key_total, -1).astype(jnp.bfloat16),
            "seq",
            scatter_dimension=0,
            tiled=True,
        ).astype(jnp.float32),
    )
    grad_projected = jnp.stack([grad_query, grad_key, grad_value]).astype(jnp.bfloat16)
    grad_attn_in = jnp.einsum(
        "sd,csi->cdi", normed, grad_projected, preferred_element_type=jnp.float32
    )
    grad_normed = jnp.einsum(
        "csi,cdi->sd", grad_projected, attn_in, preferred_element_type=jnp.float32
    )
    unused_joined, joined_back = jax.vjp(rms_norm, joined, gain_first.astype(jnp.float32))
    grad_joined_part, grad_gain_first = joined_back(grad_normed)
    grad_joined = grad_mid + grad_joined_part
    grad_join = grad_joined.astype(jnp.bfloat16)
    grad_join_matrix = project_left(mixed, grad_join)
    grad_join_shift = jnp.sum(grad_join.astype(jnp.float32), 0)
    grad_mixed = project_right(grad_join, join_matrix).astype(jnp.bfloat16).astype(jnp.float32)
    grad_biases = jnp.broadcast_to(jnp.sum(grad_mixed, 0), (3, model_width))
    tap_float = tap_rows.astype(jnp.float32)
    grad_taps = [None] * 9
    grad_extended = jnp.zeros((row_count + 3, model_width), jnp.float32)
    for window, offset in windows:
        for tap_index in range(window):
            first_row = 4 - window + tap_index
            grad_taps[offset + tap_index] = jnp.sum(
                grad_mixed * extended[first_row : first_row + row_count], 0
            )
            grad_extended = grad_extended + jnp.pad(
                tap_float[offset + tap_index] * grad_mixed, ((first_row, 3 - first_row), (0, 0))
            )
    back_rows = passed_along(grad_extended[:3], "seq", -1)
    grad_in = grad_joined + grad_extended[3:] + jnp.pad(back_rows, ((row_count - 3, 0), (0, 0)))
    layer_grads = (
        jnp.stack(grad_taps),
        grad_biases,
        grad_join_matrix,
        grad_join_shift,
        grad_gain_first,
        grad_attn_in,
        grad_attn_out,
        grad_table,
        grad_gain_second,
        grad_mlp_in,
        grad_mlp_out,
    )
    return (grad_in, layer_grads)


def body(
    byte_states,
    teacher,
    lengths,
    conv_taps,
    conv_bias,
    join_weight,
    join_bias,
    gain_attn,
    attn_in_weight,
    attn_out_weight,
    position_bias,
    gain_mlp,
    mlp_in_weight,
    mlp_out_weight,
):
    layer_count = conv_taps.shape[0]
    micro_count = byte_states.shape[0]
    row_count = byte_states.shape[2]
    model_width = byte_states.shape[3]
    seq_total = row_count * lax.axis_size("seq")
    positions = lax.axis_index("seq") * row_count + jnp.arange(row_count)
    key_positions = jnp.arange(seq_total)
    bucket_grid = bucket_ids(key_positions[None, :] - positions[:, None])
    one_hot_ids = (bucket_grid[:, :, None] == jnp.arange(BUCKETS)[None, None, :]).astype(
        jnp.bfloat16
    )
    total_valid = lax.psum(jnp.sum(lengths.astype(jnp.float32)), "batch")
    sums = [None] * layer_count
    out_rows = []
    grad_rows = []
    local_squares = jnp.zeros((), jnp.float32)
    for batch_index in range(micro_count):
        state = byte_states[batch_index, 0].astype(jnp.float32)
        length = lengths[batch_index, 0]
        key_valid = key_positions < length
        row_valid = positions < length
        kept = []
        for layer_index in range(layer_count):
            weights = (
                lax.all_gather(conv_taps[layer_index], ("seq", "batch"), axis=1, tiled=True),
                lax.all_gather(conv_bias[layer_index], ("seq", "batch"), axis=1, tiled=True),
                lax.all_gather(join_weight[layer_index], ("seq", "batch"), axis=0, tiled=True),
                lax.all_gather(join_bias[layer_index], ("seq", "batch"), axis=0, tiled=True),
                lax.all_gather(gain_attn[layer_index], ("seq", "batch"), axis=0, tiled=True),
                lax.all_gather(attn_in_weight[layer_index], ("seq", "batch"), axis=1, tiled=True),
                lax.all_gather(attn_out_weight[layer_index], ("seq", "batch"), axis=0, tiled=True),
                lax.all_gather(position_bias[layer_index], ("seq", "batch"), axis=0, tiled=True),
                lax.all_gather(gain_mlp[layer_index], ("seq", "batch"), axis=0, tiled=True),
                lax.all_gather(mlp_in_weight[layer_index], ("seq", "batch"), axis=1, tiled=True),
                lax.all_gather(mlp_out_weight[layer_index], ("seq", "batch"), axis=0, tiled=True),
            )
            state, saved = layer_forward(state, weights, one_hot_ids, key_valid)
            kept.append(saved)
        out_rows.append(state)
        diff = jnp.where(
            row_valid[:, None], state - teacher[batch_index, 0].astype(jnp.float32), 0.0
        )
        local_squares = local_squares + jnp.sum(diff * diff)
        grad_state = 2.0 * diff / (total_valid * model_width)
        for layer_index in reversed(range(layer_count)):
            weights = (
                lax.all_gather(conv_taps[layer_index], ("seq", "batch"), axis=1, tiled=True),
                lax.all_gather(conv_bias[layer_index], ("seq", "batch"), axis=1, tiled=True),
                lax.all_gather(join_weight[layer_index], ("seq", "batch"), axis=0, tiled=True),
                lax.all_gather(join_bias[layer_index], ("seq", "batch"), axis=0, tiled=True),
                lax.all_gather(gain_attn[layer_index], ("seq", "batch"), axis=0, tiled=True),
                lax.all_gather(attn_in_weight[layer_index], ("seq", "batch"), axis=1, tiled=True),
                lax.all_gather(attn_out_weight[layer_index], ("seq", "batch"), axis=0, tiled=True),
                lax.all_gather(position_bias[layer_index], ("seq", "batch"), axis=0, tiled=True),
                lax.all_gather(gain_mlp[layer_index], ("seq", "batch"), axis=0, tiled=True),
                lax.all_gather(mlp_in_weight[layer_index], ("seq", "batch"), axis=1, tiled=True),
                lax.all_gather(mlp_out_weight[layer_index], ("seq", "batch"), axis=0, tiled=True),
            )
            grad_state, layer_grads = layer_backward(
                grad_state, kept[layer_index], weights, one_hot_ids, key_valid
            )
            if sums[layer_index] is None:
                sums[layer_index] = layer_grads
            else:
                sums[layer_index] = jax.tree.map(jnp.add, sums[layer_index], layer_grads)
        grad_rows.append(grad_state)
    loss = lax.psum(local_squares, ("seq", "batch")) / (total_valid * model_width)
    stacked_grads = tuple(
        (
            jnp.stack([sums[layer_index][member] for layer_index in range(layer_count)])
            for member in range(11)
        )
    )
    (
        grad_taps,
        grad_biases,
        grad_join_matrix,
        grad_join_shift,
        grad_gain_first,
        grad_attn_in,
        grad_attn_out,
        grad_table,
        grad_gain_second,
        grad_mlp_in,
        grad_mlp_out,
    ) = stacked_grads
    owned = (
        lax.psum_scatter(grad_taps, ("seq", "batch"), scatter_dimension=2, tiled=True),
        lax.psum_scatter(grad_biases, ("seq", "batch"), scatter_dimension=2, tiled=True),
        lax.psum_scatter(grad_join_matrix, ("seq", "batch"), scatter_dimension=1, tiled=True),
        lax.psum_scatter(grad_join_shift, ("seq", "batch"), scatter_dimension=1, tiled=True),
        lax.psum_scatter(grad_gain_first, ("seq", "batch"), scatter_dimension=1, tiled=True),
        lax.psum_scatter(grad_attn_in, ("seq", "batch"), scatter_dimension=2, tiled=True),
        lax.psum_scatter(grad_attn_out, ("seq", "batch"), scatter_dimension=1, tiled=True),
        lax.psum_scatter(grad_table, ("seq", "batch"), scatter_dimension=1, tiled=True),
        lax.psum_scatter(grad_gain_second, ("seq", "batch"), scatter_dimension=1, tiled=True),
        lax.psum_scatter(grad_mlp_in, ("seq", "batch"), scatter_dimension=2, tiled=True),
        lax.psum_scatter(grad_mlp_out, ("seq", "batch"), scatter_dimension=1, tiled=True),
    )
    activations = jnp.stack(out_rows)[:, None]
    input_grad = jnp.stack(grad_rows)[:, None]
    return (
        activations,
        loss,
        input_grad,
        owned[0],
        owned[1],
        owned[2],
        owned[3],
        owned[4],
        owned[5],
        owned[6],
        owned[7],
        owned[8],
        owned[9],
        owned[10],
    )


ALL = ("seq", "z", "core")
LOW = jnp.bfloat16
WIDE = jnp.float32
BLOCK = 256
MASKED = -1e30


def nt(left, right):
    return lax.dot_general(left, right, (((1,), (1,)), ((), ())), preferred_element_type=WIDE)


def nn(left, right):
    return lax.dot_general(left, right, (((1,), (0,)), ((), ())), preferred_element_type=WIDE)


def tn(left, right):
    return lax.dot_general(left, right, (((0,), (0,)), ((), ())), preferred_element_type=WIDE)


def band_kernel(line_ref, band_ref):
    wide = jnp.broadcast_to(line_ref[0], (BLOCK, 4 * BLOCK))
    rolled = pltpu.roll(wide, 0, 1, stride=1, stride_axis=0)
    band_ref[0, 0] = rolled[:, :BLOCK]
    band_ref[0, 1] = rolled[:, BLOCK : 2 * BLOCK]
    band_ref[0, 2] = rolled[:, 3 * BLOCK :]


def build_band(line):
    return pl.pallas_call(
        band_kernel,
        grid=(HEADS,),
        in_specs=[pl.BlockSpec((1, 1, 4 * BLOCK), lambda h: (h, 0, 0))],
        out_specs=pl.BlockSpec((1, 3, BLOCK, BLOCK), lambda h: (h, 0, 0, 0)),
        out_shape=jax.ShapeDtypeStruct((HEADS, 3, BLOCK, BLOCK), WIDE),
        name="bias_band",
    )(line.reshape(HEADS, 1, 4 * BLOCK))


def key_blocks(core, near):
    near_rows = pl.multiple_of(BLOCK * (1 - core), BLOCK)
    far_rows = pl.multiple_of(BLOCK * core, BLOCK)
    below, above = 1 + core, 2 - core
    if near:
        return near_rows, ((0, near_rows, 0), (0, far_rows, below), (1, far_rows, above), (1, near_rows, None))
    return far_rows, ((0, far_rows, 0), (0, near_rows, above), (1, far_rows, None), (1, near_rows, None))


def keys_with_mask(block, lane, head, first_position, length, constant):
    rows = first_position + lax.broadcasted_iota(jnp.int32, (BLOCK, 1), 0)
    mask = jnp.where(rows < length, 0.0, MASKED)
    spare = (1 - head) * HEAD_DIM
    extra = jnp.where(lane == spare, mask, jnp.where(lane == spare + 1, constant, 0.0))
    return jnp.where(lane // HEAD_DIM == head, block.astype(WIDE), extra).astype(LOW)


def query_with_ones(block, lane, head):
    spare = (1 - head) * HEAD_DIM
    extra = jnp.where((lane == spare) | (lane == spare + 1), 1.0, 0.0)
    return jnp.where(lane // HEAD_DIM == head, block.astype(WIDE), extra).astype(LOW)


def only_head(block, lane, head):
    return jnp.where(lane // HEAD_DIM == head, block.astype(WIDE), 0.0).astype(LOW)


def attend_kernel(
    info_ref, far_ref, q_ref, k_ref, v_ref, ko_ref, vo_ref, band_ref, out_ref, lse_ref, score_ref
):
    core, length = info_ref[0], info_ref[1]
    pair = pl.program_id(0)
    lane = lax.broadcasted_iota(jnp.int32, (1, 2 * HEAD_DIM), 1)
    for n in range(2):
        q_rows, blocks = key_blocks(core, n == 0)
        query = q_ref[pl.ds(q_rows, BLOCK), :]
        halves = []
        for head in range(2):
            q_low = query_with_ones(query, lane, head)
            top = None
            for b, (side, start, slot) in enumerate(blocks):
                first = 2 * BLOCK * (core if side == 0 else 1 - core) + start
                keys = (k_ref, ko_ref)[side][pl.ds(start, BLOCK), :]
                constant = far_ref[2 * pair + head] if slot is None else 0.0
                scores = nt(keys_with_mask(keys, lane, head, first, length, constant), q_low)
                if slot is not None:
                    scores = scores + band_ref[head, slot]
                score_ref[b] = scores
                block_top = jnp.max(scores, 0, keepdims=True)
                top = block_top if top is None else jnp.maximum(top, block_top)
            total = jnp.zeros((1, BLOCK), WIDE)
            mixed = jnp.zeros((2 * HEAD_DIM, BLOCK), WIDE)
            for b, (side, start, slot) in enumerate(blocks):
                weights = jnp.exp(score_ref[b] - top)
                total = total + jnp.sum(weights, 0, keepdims=True)
                values = (v_ref, vo_ref)[side][pl.ds(start, BLOCK), :]
                mixed = mixed + tn(values, weights.astype(LOW))
            lse_ref[0, n, head : head + 1, :] = top + jnp.log(total)
            halves.append((mixed / total)[head * HEAD_DIM : (head + 1) * HEAD_DIM])
        out_ref[pl.ds(q_rows, BLOCK), :] = jnp.transpose(jnp.concatenate(halves, 0)).astype(LOW)


def attend(info, far, projected, others, band):
    rows = projected.shape[0]
    pairs = HEADS // 2
    width = 2 * HEAD_DIM
    col = lambda shift: pl.BlockSpec((rows, width), lambda p: (0, p + shift))
    return pl.pallas_call(
        attend_kernel,
        grid=(pairs,),
        in_specs=[
            pl.BlockSpec(memory_space=pltpu.SMEM),
            pl.BlockSpec(memory_space=pltpu.SMEM),
            col(0),
            col(pairs),
            col(2 * pairs),
            col(0),
            col(pairs),
            pl.BlockSpec((2, 3, BLOCK, BLOCK), lambda p: (p, 0, 0, 0)),
        ],
        out_specs=[col(0), pl.BlockSpec((1, 2, 2, BLOCK), lambda p: (p, 0, 0, 0))],
        out_shape=[
            jax.ShapeDtypeStruct((rows, HEADS * HEAD_DIM), LOW),
            jax.ShapeDtypeStruct((pairs, 2, 2, BLOCK), WIDE),
        ],
        scratch_shapes=[pltpu.VMEM((4, BLOCK, BLOCK), WIDE)],
        name="attend",
    )(info, far, projected, projected, projected, others, others, band)


def attend_back_kernel(
    info_ref,
    far_ref,
    q_ref,
    k_ref,
    v_ref,
    ko_ref,
    vo_ref,
    band_ref,
    out_ref,
    gout_ref,
    lse_ref,
    gq_ref,
    gown_ref,
    goth_ref,
    gband_ref,
    gfar_ref,
    gk_acc,
    gv_acc,
    band_acc,
    far_acc,
):
    core, length = info_ref[0], info_ref[1]
    pair = pl.program_id(0)
    width = 2 * HEAD_DIM
    lane = lax.broadcasted_iota(jnp.int32, (1, width), 1)
    gk_acc[...] = jnp.zeros_like(gk_acc)
    gv_acc[...] = jnp.zeros_like(gv_acc)
    band_acc[...] = jnp.zeros_like(band_acc)
    far_acc[...] = jnp.zeros_like(far_acc)
    select = jnp.where(
        lax.broadcasted_iota(jnp.int32, (8, width), 0)
        == lax.broadcasted_iota(jnp.int32, (8, width), 1) // HEAD_DIM,
        1.0,
        0.0,
    )
    for n in range(2):
        q_rows, blocks = key_blocks(core, n == 0)
        query = q_ref[pl.ds(q_rows, BLOCK), :]
        gout = gout_ref[pl.ds(q_rows, BLOCK), :]
        dots = gout.astype(WIDE) * out_ref[pl.ds(q_rows, BLOCK), :].astype(WIDE)
        deltas = lax.dot_general(
            select,
            dots,
            (((1,), (1,)), ((), ())),
            precision=lax.Precision.HIGHEST,
            preferred_element_type=WIDE,
        )
        halves = []
        for head in range(2):
            q_ones = query_with_ones(query, lane, head)
            q_low = only_head(query, lane, head)
            g_low = only_head(gout, lane, head)
            lse = lse_ref[0, n, head : head + 1, :]
            delta = deltas[head : head + 1]
            gq = jnp.zeros((width, BLOCK), WIDE)
            for side, start, slot in blocks:
                first = 2 * BLOCK * (core if side == 0 else 1 - core) + start
                keys = (k_ref, ko_ref)[side][pl.ds(start, BLOCK), :]
                values = (v_ref, vo_ref)[side][pl.ds(start, BLOCK), :]
                constant = far_ref[2 * pair + head] if slot is None else 0.0
                scores = nt(keys_with_mask(keys, lane, head, first, length, constant), q_ones)
                if slot is not None:
                    scores = scores + band_ref[head, slot]
                probs = jnp.exp(scores - lse)
                gprobs = nt(values, g_low)
                gscores = probs * (gprobs - delta)
                if slot is None:
                    part = jnp.sum(gscores.reshape(BLOCK // 8, 8, BLOCK), 0)
                    far_acc[head] = far_acc[head] + part
                else:
                    band_acc[head, slot] = band_acc[head, slot] + gscores
                gs_low = gscores.astype(LOW)
                at = pl.ds(2 * BLOCK * side + start, BLOCK)
                gv_acc[at, :] = gv_acc[at, :] + nn(probs.astype(LOW), g_low)
                gk_acc[at, :] = gk_acc[at, :] + nn(gs_low, q_low)
                gq = gq + tn(keys, gs_low)
            halves.append(gq[head * HEAD_DIM : (head + 1) * HEAD_DIM])
        gq_ref[pl.ds(q_rows, BLOCK), :] = jnp.transpose(jnp.concatenate(halves, 0)).astype(LOW)
    own = 2 * BLOCK
    gown_ref[0] = gk_acc[:own, :]
    gown_ref[1] = gv_acc[:own, :]
    goth_ref[0] = gk_acc[own:, :].astype(LOW)
    goth_ref[1] = gv_acc[own:, :].astype(LOW)
    span = 4 * BLOCK
    gap = jnp.zeros((8, BLOCK), WIDE)
    row = lax.broadcasted_iota(jnp.int32, (8, span), 0)
    for head in range(2):
        lines = jnp.zeros((8, span), WIDE)
        for g in range(BLOCK // 8):
            rows = slice(8 * g, 8 * g + 8)
            piece = jnp.concatenate(
                [band_acc[head, 0, rows], band_acc[head, 1, rows], gap, band_acc[head, 2, rows]], 1
            )
            lines = lines + (pltpu.roll(piece, span - 8 * g, 1) if g else piece)
        for bit in (1, 2, 4):
            lines = jnp.where((row & bit) != 0, pltpu.roll(lines, span - bit, 1), lines)
        gband_ref[0, head : head + 1, :] = jnp.sum(lines, 0, keepdims=True)
        gfar_ref[0, head : head + 1, :] = jnp.sum(far_acc[head], 0, keepdims=True)


def attend_back(info, far, projected, others, band, out, gout, lse):
    rows = projected.shape[0]
    pairs = HEADS // 2
    width = 2 * HEAD_DIM
    inner = HEADS * HEAD_DIM
    col = lambda shift: pl.BlockSpec((rows, width), lambda p: (0, p + shift))
    two = pl.BlockSpec((2, rows, width), lambda p: (0, 0, p))
    return pl.pallas_call(
        attend_back_kernel,
        grid=(pairs,),
        in_specs=[
            pl.BlockSpec(memory_space=pltpu.SMEM),
            pl.BlockSpec(memory_space=pltpu.SMEM),
            col(0),
            col(pairs),
            col(2 * pairs),
            col(0),
            col(pairs),
            pl.BlockSpec((2, 3, BLOCK, BLOCK), lambda p: (p, 0, 0, 0)),
            col(0),
            col(0),
            pl.BlockSpec((1, 2, 2, BLOCK), lambda p: (p, 0, 0, 0)),
        ],
        out_specs=[
            col(0),
            two,
            two,
            pl.BlockSpec((1, 2, 4 * BLOCK), lambda p: (p, 0, 0)),
            pl.BlockSpec((1, 2, BLOCK), lambda p: (p, 0, 0)),
        ],
        out_shape=[
            jax.ShapeDtypeStruct((rows, inner), LOW),
            jax.ShapeDtypeStruct((2, rows, inner), WIDE),
            jax.ShapeDtypeStruct((2, rows, inner), LOW),
            jax.ShapeDtypeStruct((pairs, 2, 4 * BLOCK), WIDE),
            jax.ShapeDtypeStruct((pairs, 2, BLOCK), WIDE),
        ],
        scratch_shapes=[
            pltpu.VMEM((4 * BLOCK, width), WIDE),
            pltpu.VMEM((4 * BLOCK, width), WIDE),
            pltpu.VMEM((2, 3, BLOCK, BLOCK), WIDE),
            pltpu.VMEM((2, 8, BLOCK), WIDE),
        ],
        name="attend_back",
    )(info, far, projected, projected, projected, others, others, band, out, gout, lse)


def store_terms(core, terms, kept_ref, sent_ref, at):
    for own in range(2):

        @pl.when(core == own)
        def _(own=own):
            kept_ref[at] = terms[:, own].astype(LOW)
            sent_ref[at] = terms[:, 1 - own].astype(LOW)


def mlp_terms_kernel(
    info_ref, x_ref, gate_ref, up_ref, hidden_ref, gout_ref, kept_ref, sent_ref, turned_ref
):
    core = info_ref[0]
    step = pl.program_id(0)
    owners, blocks, share, width = kept_ref.shape
    tail = blocks // 3

    @pl.when(step == 0)
    def _():
        turned_ref[...] = jnp.transpose(x_ref[...])

    for part, gin_ref in enumerate((gate_ref, up_ref)):

        @pl.when(step // tail == part)
        def _(gin_ref=gin_ref):
            terms = nn(turned_ref[...], gin_ref[...]).reshape(owners, 2, share, width)
            store_terms(core, terms, kept_ref, sent_ref, (slice(None), step))

    @pl.when(step >= 2 * tail)
    def _():
        few = owners // tail
        terms = tn(hidden_ref[...], gout_ref[...]).reshape(few, 2, tail, share, width)
        at = (pl.ds((step - 2 * tail) * few, few), slice(2 * tail, blocks))
        store_terms(core, terms, kept_ref, sent_ref, at)


def mlp_terms(info, x, gate, up, hidden, gout, owners, share):
    rows, width = x.shape
    tail = hidden.shape[1] // width
    shape = jax.ShapeDtypeStruct((owners, 3 * tail, share, width), LOW)
    whole = pl.BlockSpec((rows, width), lambda j: (0, 0))
    out = pl.BlockSpec(shape.shape, lambda j: (0, 0, 0, 0))
    turn = lambda part: pl.BlockSpec(
        (rows, width), lambda j: (0, jnp.minimum(jnp.maximum(j - part * tail, 0), tail - 1))
    )
    return pl.pallas_call(
        mlp_terms_kernel,
        grid=(3 * tail,),
        in_specs=[pl.BlockSpec(memory_space=pltpu.SMEM), whole, turn(0), turn(1), turn(2), whole],
        out_specs=[out, out],
        out_shape=[shape, shape],
        scratch_shapes=[pltpu.VMEM((width, rows), LOW)],
        name="mlp_terms",
    )(info, x, gate, up, hidden, gout)


def attn_terms_kernel(
    info_ref,
    mixed_ref,
    gjoin_ref,
    norm_ref,
    gquery_ref,
    gkv_ref,
    att_ref,
    gmid_ref,
    small_ref,
    kept_ref,
    sent_ref,
):
    core = info_ref[0]
    owners, blocks, share, width = kept_ref.shape

    def put(at, turned, right):
        terms = nn(turned, right).reshape(owners, 2, share, width)
        store_terms(core, terms, kept_ref, sent_ref, (slice(None), at))

    put(0, jnp.transpose(mixed_ref[...]), gjoin_ref[...])
    turned = jnp.transpose(norm_ref[...])
    put(1, turned, gquery_ref[...])
    put(2, turned, gkv_ref[0])
    put(3, turned, gkv_ref[1])
    put(4, jnp.transpose(att_ref[...]), gmid_ref[...])
    small = jnp.broadcast_to(small_ref[...].astype(LOW)[None], (owners, share, width))
    kept_ref[:, 5] = small
    sent_ref[:, 5] = small


def attn_terms(info, mixed, gjoin, norm, gquery, gkv, att, gmid, small, owners, share):
    width = mixed.shape[1]
    shape = jax.ShapeDtypeStruct((owners, 6, share, width), LOW)
    vmem = pl.BlockSpec(memory_space=pltpu.VMEM)
    return pl.pallas_call(
        attn_terms_kernel,
        in_specs=[pl.BlockSpec(memory_space=pltpu.SMEM)] + [vmem] * 8,
        out_specs=[vmem, vmem],
        out_shape=[shape, shape],
        name="attn_terms",
    )(info, mixed, gjoin, norm, gquery, gkv, att, gmid, small)


def pack_kernel(
    info_ref,
    lengths_ref,
    taps_ref,
    bias_ref,
    join_ref,
    join_bias_ref,
    gain_attn_ref,
    attn_in_ref,
    attn_out_ref,
    position_ref,
    gain_mlp_ref,
    mlp_in_ref,
    mlp_out_ref,
    *refs,
):
    small_ref = refs[-1]
    device = info_ref[0]
    layers, share, width = join_ref.shape
    lane = lax.broadcasted_iota(jnp.int32, (share, width), 1)
    item = lax.broadcasted_iota(jnp.int32, (share, width), 0)
    spread = jnp.where(lane == device * share + item, 1.0, 0.0).astype(LOW)
    place = lane[:1] - device * share - HEADS
    extra = jnp.zeros((1, width), WIDE)
    for m in range(lengths_ref.shape[0]):
        whole, rest = lengths_ref[m] // 32, lengths_ref[m] % 32
        extra = extra + jnp.where(place == 2 * m, whole, jnp.where(place == 2 * m + 1, rest, 0)).astype(WIDE)
    for l in range(layers):
        small_ref[0:9] = tn(taps_ref[:, l], spread)
        small_ref[9:12] = tn(bias_ref[:, l], spread)
        small_ref[12:13] = nn(join_bias_ref[l : l + 1], spread)
        small_ref[13:14] = nn(gain_attn_ref[l : l + 1], spread)
        small_ref[14:15] = nn(gain_mlp_ref[l : l + 1], spread)
        small_ref[15:16] = nn(position_ref[l : l + 1], spread[:HEADS]) + extra
        first = [join_ref[l]] + [attn_in_ref[l, c] for c in range(3)] + [small_ref[...].astype(LOW)]
        later = [attn_out_ref[l], mlp_in_ref[l, 0], mlp_in_ref[l, 1]] + [
            mlp_out_ref[l, a * share : (a + 1) * share] for a in range(mlp_out_ref.shape[1] // share)
        ]
        for out_ref, pieces in ((refs[2 * l], first), (refs[2 * l + 1], later)):
            cursor = 0
            for piece in pieces:
                out_ref[:, cursor : cursor + piece.shape[1]] = piece
                cursor += piece.shape[1]


def pack(info, lengths, arrays, share):
    layers, width = arrays[2].shape[0], arrays[2].shape[2]
    quarters = arrays[-2].shape[3] // width
    first, rest = 5 * width, (1 + 3 * quarters) * width
    smem = pl.BlockSpec(memory_space=pltpu.SMEM)
    vmem = pl.BlockSpec(memory_space=pltpu.VMEM)
    return pl.pallas_call(
        pack_kernel,
        in_specs=[smem, smem] + [vmem] * len(arrays),
        out_specs=[vmem] * (2 * layers),
        out_shape=[jax.ShapeDtypeStruct((share, span), LOW) for span in (first, rest)] * layers,
        scratch_shapes=[pltpu.VMEM((share, width), WIDE)],
        name="pack",
    )(info, lengths, *arrays)


def tie(*values):
    return lax.optimization_barrier(values)


def chip_body(
    byte_states,
    teacher,
    lengths,
    conv_taps,
    conv_bias,
    join_weight,
    join_bias,
    gain_attn,
    attn_in_weight,
    attn_out_weight,
    position_bias,
    gain_mlp,
    mlp_in_weight,
    mlp_out_weight,
):
    layer_count = conv_taps.shape[0]
    model_width = byte_states.shape[3]
    slot_rows = byte_states.shape[2]
    rows = 2 * slot_rows
    hidden_width = mlp_in_weight.shape[3]
    quarters = hidden_width // model_width
    seqs, zs, cores = (lax.axis_size(name) for name in ALL)
    devices = seqs * zs * cores
    share = model_width // devices
    s_at, z_at, c_at = (lax.axis_index(name) for name in ALL)
    device_at = (s_at * zs + z_at) * cores + c_at

    def number(s, z, c):
        return (s * zs + z) * cores + c

    places = [(s, z, c) for s in range(seqs) for z in range(zs) for c in range(cores)]
    swap = [(number(s, z, c), number(s, z, 1 - c)) for s, z, c in places]
    routes = [
        [(number(s, z, c), number(2 * (s % 2 if turn == 0 else 1 - s % 2) + c, z, s // 2)) for s, z, c in places]
        for turn in range(2)
    ]
    back_routes = [[(b, a) for a, b in route] for route in routes]

    def to_chips(block):
        odd, high = s_at % 2, s_at // 2
        first, second = (
            lax.ppermute(jnp.where(odd == turn, block[0], block[1]), ALL, routes[turn]) for turn in range(2)
        )
        return jnp.concatenate(
            [jnp.where(high == 0, first, second), jnp.where(high == 0, second, first)], 0
        )

    def leave(block):
        high = s_at // 2
        halves = (block[:slot_rows], block[slot_rows:])
        return [
            lax.ppermute(jnp.where(high == turn, halves[0], halves[1]), ALL, back_routes[turn])
            for turn in range(2)
        ]

    def arrive(pieces):
        first, second = pieces
        odd = s_at % 2
        whole = jnp.stack([jnp.where(odd == 0, first, second), jnp.where(odd == 0, second, first)])
        return whole.astype(WIDE)[:, None]

    def trade(block):
        return lax.ppermute(block, ALL, swap)

    to_high = [(number(s, z, 0), number(s, z, 1)) for s, z, c in places if c == 0]
    to_low = [(b, a) for a, b in to_high]

    lanes = jnp.arange(model_width)
    lane_owner, lane_item = lanes // share, lanes % share
    every_layer = range(layer_count)
    packed = pack(
        device_at.astype(jnp.int32).reshape(1),
        lengths.reshape(-1),
        (
            conv_taps.transpose(2, 0, 1),
            conv_bias.transpose(2, 0, 1),
            join_weight,
            join_bias,
            gain_attn,
            attn_in_weight,
            attn_out_weight,
            position_bias,
            gain_mlp,
            mlp_in_weight,
            mlp_out_weight,
        ),
        share,
    )

    def moved(block, name, change):
        def target(s, z, c):
            return number(s ^ change, z, c) if name == "seq" else number(s, z ^ change, c)

        return lax.ppermute(block, ALL, [(number(s, z, c), target(s, z, c)) for s, z, c in places])

    def spread_out(block, name, at, size):
        whole = jnp.zeros((size,) + block.shape, block.dtype)
        pieces = [block] + [moved(block, name, change) for change in range(1, size)]
        for change, piece in enumerate(pieces):
            whole = lax.dynamic_update_index_in_dim(whole, piece, at ^ change, 0)
        return whole

    def pair_up(block):
        other = trade(block)
        return jnp.stack(
            [jnp.where(c_at == 0, block, other), jnp.where(c_at == 0, other, block)], 2
        ).reshape(model_width, -1)

    def split_halves(kept, arrived):
        shape = (seqs, zs) + kept.shape[1:]
        return kept.reshape(shape), arrived.reshape(shape)

    def plane_terms(kept, arrived):
        kept, arrived = split_halves(kept, arrived)
        pick = lambda whole, s: lax.dynamic_index_in_dim(whole, s, 0, False).astype(WIDE)
        return [
            (pick(kept, s_at ^ change) + pick(arrived, s_at ^ change)).astype(LOW)
            for change in range(seqs)
        ]

    def line_terms(pieces):
        total = finish(pieces).astype(LOW)
        return [lax.dynamic_index_in_dim(total, z_at ^ change, 0, False) for change in range(zs)]

    def send(name, terms):
        return [moved(part, name, change) if change else part for change, part in enumerate(terms)]

    def finish(pieces):
        return sum(piece.astype(WIDE) for piece in pieces)

    early, behind = spread_out(packed[0], "z", z_at, zs), packed[2]
    early, behind = tie(early, behind)
    early, behind = spread_out(early, "seq", s_at, seqs), spread_out(behind, "z", z_at, zs)
    early, behind = tie(early, behind)
    early = [pair_up(early), spread_out(behind, "seq", s_at, seqs)]
    later = [lax.all_gather(packed[2 * l + 1], ALL, axis=0, tiled=True) for l in every_layer]

    def unpack_first(first):
        small = jnp.sum(first[:, 4 * model_width :].reshape(devices, share, model_width).astype(WIDE), 0)
        return dict(
            join=first[:, :model_width],
            attn_in=first[:, model_width : 4 * model_width],
            taps=jnp.stack(
                [
                    small[5],
                    small[2] + small[6],
                    small[0] + small[3] + small[7],
                    small[1] + small[4] + small[8],
                ]
            ),
            bias=small[9] + small[10] + small[11],
            join_bias=small[12],
            gain_attn=small[13],
            gain_mlp=small[14],
            last=small[15],
        )

    def unpack_rest(rest):
        outward = rest[:, (1 + 2 * quarters) * model_width :].reshape(devices, share, quarters, model_width)
        return dict(
            attn_out=rest[:, :model_width],
            gate=rest[:, model_width : model_width + hidden_width],
            up=rest[:, model_width + hidden_width : model_width + 2 * hidden_width],
            mlp_out=outward.transpose(0, 2, 1, 3).reshape(hidden_width, model_width),
        )

    weights = [unpack_first(early[0])]
    state = to_chips(byte_states[:, 0]).astype(WIDE)
    target = to_chips(teacher[:, 0])

    counts = weights[0]["last"]
    scale = jnp.where((lane_item >= HEADS) & (lane_item < HEADS + 4), jnp.where(lane_item % 2 == 0, 32.0, 1.0), 0.0)
    total_valid = jnp.sum(jnp.where(lane_owner < zs * cores, counts * scale, 0.0))
    mine = (lane_owner == z_at * cores + s_at % 2) & ((lane_item - HEADS) // 2 == s_at // 2)
    length = jnp.sum(jnp.where(mine, counts * scale, 0.0)).astype(jnp.int32)
    info = jnp.stack([c_at.astype(jnp.int32), length])
    row_valid = (rows * c_at + jnp.arange(rows) < length)[:, None]

    offsets = -((jnp.arange(4 * BLOCK) + 2 * BLOCK) % (4 * BLOCK) - 2 * BLOCK)
    in_bucket = (lane_owner[:, None] == bucket_ids(offsets)[None, :]).astype(LOW)
    of_head = (lane_item[None, :] == jnp.arange(HEADS)[:, None]).astype(WIDE)
    far_bucket = (lane_owner == jnp.where(c_at == 0, 31, 15)).astype(WIDE)

    def normed(values, gain):
        inverse = lax.rsqrt(jnp.mean(values * values, -1, keepdims=True) + eps)
        return (values * inverse * gain).astype(LOW)

    def normed_back(grad, values, gain):
        inverse = lax.rsqrt(jnp.mean(values * values, -1, keepdims=True) + eps)
        unit = values * inverse
        scaled = grad * gain
        grad_in = inverse * (scaled - unit * jnp.mean(scaled * unit, -1, keepdims=True))
        return grad_in, jnp.sum(grad * unit, 0)

    kept = []
    for l in range(layer_count):
        w = weights[l]
        low_state = state.astype(LOW)
        prior = lax.ppermute(low_state[rows - 8 :], ALL, to_high)[5:]
        extended = jnp.concatenate([prior, low_state], 0).astype(WIDE)
        mixed = w["bias"] + sum(w["taps"][k] * extended[k : k + rows] for k in range(4))
        mixed = mixed.astype(LOW)
        joined = state + nn(mixed, w["join"]) + w["join_bias"]
        norm_a = normed(joined, w["gain_attn"])
        projected = nn(norm_a, w["attn_in"]).astype(LOW)
        others = trade(projected[:, HEADS * HEAD_DIM :])
        line = jnp.dot(
            (of_head * w["last"]).astype(LOW), in_bucket, preferred_element_type=WIDE
        )
        far = jnp.sum(of_head * (w["last"] * far_bucket), 1)
        band = build_band(line)
        attended, lse = attend(info, far, projected, others, band)
        if l + 1 < layer_count:
            attended, lse, later[l], early[l + 1], target = tie(
                attended, lse, later[l], early[l + 1], target
            )
            weights.append(unpack_first(pair_up(early[l + 1])))
        else:
            attended, lse, later[l] = tie(attended, lse, later[l])
        w.update(unpack_rest(later[l]))
        mid = joined + nn(attended, w["attn_out"])
        norm_m = normed(mid, w["gain_mlp"])
        gate = nn(norm_m, w["gate"])
        up = nn(norm_m, w["up"])
        hidden = (jax.nn.gelu(gate, approximate=True) * up).astype(LOW)
        state = mid + nn(hidden, w["mlp_out"])
        kept.append(
            (extended, mixed, joined, norm_a, projected, others, far, band, attended, lse, mid, norm_m, gate, up, hidden)
        )

    activations = leave(state)
    diff = jnp.where(row_valid, state - target.astype(WIDE), 0.0)
    squares = jnp.sum(diff * diff, 0)
    grad = 2.0 * diff / (total_valid * model_width)
    owners = seqs * zs
    mlp_done, attn_done = [None] * layer_count, [None] * layer_count
    mlp_way = attn_way = None
    for l in reversed(every_layer):
        w = weights[l]
        (extended, mixed, joined, norm_a, projected, others, far, band, attended, lse, mid, norm_m, gate, up, hidden) = kept[l]
        g_low = grad.astype(LOW)
        g_hidden = nt(g_low, w["mlp_out"])
        unused, gelu_back = jax.vjp(gated_unit, gate, up)
        g_gate, g_up = (part.astype(LOW) for part in gelu_back(g_hidden))
        g_norm = nt(g_gate, w["gate"]) + nt(g_up, w["up"])
        g_mid, g_gain_mlp = normed_back(g_norm, mid, w["gain_mlp"])
        g_mid = grad + g_mid
        if mlp_way is not None:
            g_mid, g_gate, g_up, mlp_way, attn_way = tie(g_mid, g_gate, g_up, mlp_way, attn_way)
            line, plane = line_terms(mlp_way), plane_terms(*attn_way)
            g_mid, g_gate, g_up, line, plane = tie(g_mid, g_gate, g_up, line, plane)
            mlp_way, attn_way = send("z", line), send("seq", plane)
        mlp_kept, mlp_sent = mlp_terms(info, norm_m, g_gate, g_up, hidden, g_low, owners, share)
        g_mid, mlp_kept, mlp_sent = tie(g_mid, mlp_kept, mlp_sent)
        mlp_half = (mlp_kept, trade(mlp_sent))
        g_mid_low = g_mid.astype(LOW)
        g_att = nt(g_mid_low, w["attn_out"]).astype(LOW)
        back = attend_back(info, far, projected, others, band, attended, g_att, lse)
        if mlp_way is None:
            back, mlp_half, activations = tie(back, mlp_half, activations)
        else:
            back, mlp_half, mlp_way, attn_way = tie(back, mlp_half, mlp_way, attn_way)
            mlp_done[l + 1] = finish(mlp_way)
            line = line_terms(attn_way)
        plane = plane_terms(*mlp_half)
        if mlp_way is None:
            back, plane = tie(back, plane)
        else:
            back, plane, line = tie(back, plane, line)
            attn_way = send("z", line)
        mlp_half = send("seq", plane)
        g_query, g_own, g_other, g_band, g_far = back
        g_kv = (g_own + trade(g_other).astype(WIDE)).astype(LOW)
        g_norm = sum(
            nt(part, w["attn_in"][:, c * model_width : (c + 1) * model_width])
            for c, part in enumerate((g_query, g_kv[0], g_kv[1]))
        )
        g_joined, g_gain_attn = normed_back(g_norm, joined, w["gain_attn"])
        g_joined = g_mid + g_joined
        g_join_low = g_joined.astype(LOW)
        g_join_bias = jnp.sum(g_join_low.astype(WIDE), 0)
        g_mixed = nt(g_join_low, w["join"]).astype(LOW).astype(WIDE)
        g_taps = [jnp.sum(g_mixed * extended[k : k + rows], 0) for k in range(4)]
        g_bias = jnp.sum(g_mixed, 0)
        head_rows = [
            sum(w["taps"][k] * g_mixed[r - k : r - k + 1] for k in range(r + 1)) for r in range(3)
        ]
        beyond = lax.ppermute(
            jnp.concatenate(head_rows + [jnp.zeros((5, model_width), WIDE)], 0), ALL, to_low
        )
        padded = jnp.concatenate([g_mixed, jnp.zeros((3, model_width), WIDE)], 0)
        g_state = sum(w["taps"][k] * padded[3 - k : 3 - k + rows] for k in range(4))
        tail = jnp.concatenate([jnp.zeros((rows - 8, model_width), WIDE), jnp.zeros((5, model_width), WIDE), beyond[:3]], 0)
        grad = g_joined + g_state + tail

        by_lane = jnp.dot(
            g_band.reshape(HEADS, -1),
            in_bucket.T.astype(WIDE),
            precision=lax.Precision.HIGHEST,
            preferred_element_type=WIDE,
        )
        g_far = jnp.sum(g_far.reshape(HEADS, -1), 1)[:, None]
        g_last = jnp.sum(of_head * (by_lane + g_far * far_bucket), 0)
        small = jnp.stack(
            g_taps
            + [g_bias, g_join_bias, g_gain_attn, g_gain_mlp, g_last, squares]
            + [jnp.zeros((model_width,), WIDE)] * (share - 10)
        )
        attn_kept, attn_sent = attn_terms(
            info, mixed, g_join_low, norm_a, g_query, g_kv, attended, g_mid_low, small, owners, share
        )
        grad, attn_kept, attn_sent = tie(grad, attn_kept, attn_sent)
        if attn_way is not None:
            attn_done[l + 1] = finish(attn_way)
        mlp_way, attn_way = mlp_half, (attn_kept, trade(attn_sent))

    mlp_way, attn_way = tie(mlp_way, attn_way)
    line, plane = line_terms(mlp_way), plane_terms(*attn_way)
    line, plane = tie(line, plane)
    attn_way, mlp_way = send("seq", plane), send("z", line)
    grad, attn_way = tie(grad.astype(LOW), attn_way)
    attn_way = send("z", line_terms(attn_way))
    input_grad = leave(grad)
    mlp_done[0], attn_done[0] = finish(mlp_way), finish(attn_way)
    owned = [
        jnp.concatenate([attn_done[l][:5], mlp_done[l], attn_done[l][5:]], 0) for l in every_layer
    ]
    small = [lax.dynamic_slice_in_dim(part[-1], device_at * share, share, 1) for part in owned]
    stack = lambda pick: jnp.stack([pick(l) for l in range(layer_count)])
    taps_at = (2, 3, 1, 2, 3, 0, 1, 2, 3)
    loss = jnp.sum(owned[-1][-1][9]) / (total_valid * model_width)
    inward = lambda part: part.transpose(1, 0, 2).reshape(share, hidden_width)
    return (
        arrive(activations),
        loss,
        arrive(input_grad),
        stack(lambda l: jnp.stack([small[l][k] for k in taps_at])),
        stack(lambda l: jnp.broadcast_to(small[l][4], (3, share))),
        stack(lambda l: owned[l][0]),
        stack(lambda l: small[l][5]),
        stack(lambda l: small[l][6]),
        stack(lambda l: owned[l][1:4]),
        stack(lambda l: owned[l][4]),
        stack(lambda l: small[l][8][:HEADS]),
        stack(lambda l: small[l][7]),
        stack(
            lambda l: jnp.stack(
                [inward(owned[l][5 : 5 + quarters]), inward(owned[l][5 + quarters : 5 + 2 * quarters])]
            )
        ),
        stack(lambda l: owned[l][5 + 2 * quarters : 5 + 3 * quarters].reshape(-1, model_width)),
    )


def chip_plan(mesh):
    grid = Mesh(
        mesh.devices.reshape(mesh.shape["seq"], mesh.shape["batch"] // 2, 2),
        ALL,
    )
    batch = ("z", "core")
    in_specs = (
        P(None, batch, "seq", None),
        P(None, batch, "seq", None),
        P(None, batch),
        P(None, None, ALL),
        P(None, None, ALL),
        P(None, ALL, None),
        P(None, ALL),
        P(None, ALL),
        P(None, None, ALL, None),
        P(None, ALL, None),
        P(None, ALL),
        P(None, ALL),
        P(None, None, ALL, None),
        P(None, ALL, None),
    )
    out_specs = (in_specs[0], P(), in_specs[0]) + in_specs[3:]
    return jax.shard_map(chip_body, mesh=grid, in_specs=in_specs, out_specs=out_specs, check_vma=False)


def shared_plan(mesh):
    in_specs = (
        P(None, "batch", "seq", None),
        P(None, "batch", "seq", None),
        P(None, "batch"),
        P(None, None, ("seq", "batch")),
        P(None, None, ("seq", "batch")),
        P(None, ("seq", "batch"), None),
        P(None, ("seq", "batch")),
        P(None, ("seq", "batch")),
        P(None, None, ("seq", "batch"), None),
        P(None, ("seq", "batch"), None),
        P(None, ("seq", "batch")),
        P(None, ("seq", "batch")),
        P(None, None, ("seq", "batch"), None),
        P(None, ("seq", "batch"), None),
    )
    out_specs = (
        P(None, "batch", "seq", None),
        P(),
        P(None, "batch", "seq", None),
        P(None, None, ("seq", "batch")),
        P(None, None, ("seq", "batch")),
        P(None, ("seq", "batch"), None),
        P(None, ("seq", "batch")),
        P(None, ("seq", "batch")),
        P(None, None, ("seq", "batch"), None),
        P(None, ("seq", "batch"), None),
        P(None, ("seq", "batch")),
        P(None, ("seq", "batch")),
        P(None, None, ("seq", "batch"), None),
        P(None, ("seq", "batch"), None),
    )
    return jax.shard_map(body, mesh=mesh, in_specs=in_specs, out_specs=out_specs, check_vma=False)


def solution(mesh):
    shared = shared_plan(mesh)

    def run(*arrays):
        sequences = arrays[0].shape[0] * arrays[0].shape[1]
        one_per_chip = 2 * sequences == mesh.devices.size and 2 * arrays[0].shape[0] == mesh.shape["seq"]
        two_layers = arrays[3].shape[0] == 2
        lanes_fit = arrays[5].shape[1] == 16 * mesh.devices.size and arrays[0].shape[2] == 4 * BLOCK
        plan = chip_plan(mesh) if one_per_chip and lanes_fit and two_layers else shared
        return plan(*arrays)

    return run
```

```python
import jax
import jax.numpy as jnp
from jax import lax
from jax.experimental import pallas as pl
from jax.experimental.pallas import tpu as pltpu
from jax.sharding import Mesh
from jax.sharding import PartitionSpec as P

HEADS = 8
HEAD_DIM = 64
BUCKETS = 32


eps = 1e-06
bounds = (12, 16, 23, 32, 46, 64, 91)
windows = ((2, 0), (3, 2), (4, 5))


def passed_along(block, axis, distance):
    devices = range(lax.axis_size(axis))
    route = [(i - distance, i) for i in devices if i - distance in devices]
    return lax.ppermute(block, axis, route)


def bucket_ids(offsets):
    magnitude = jnp.abs(offsets)
    far_ids = 8 + sum(((magnitude >= bound_value).astype(jnp.int32) for bound_value in bounds))
    near_ids = jnp.where(magnitude < 8, magnitude, far_ids)
    return jnp.where(offsets > 0, 16, 0) + near_ids


def rms_norm(values, gain):
    return values * lax.rsqrt(jnp.mean(values * values, -1, keepdims=True) + eps) * gain


def conv_sum(extended, tap_rows, biases, row_count):
    total = jnp.zeros((row_count, extended.shape[1]), jnp.float32) + jnp.sum(biases, 0)
    for window, offset in windows:
        for tap_index in range(window):
            first_row = 4 - window + tap_index
            total = (
                total + tap_rows[offset + tap_index] * extended[first_row : first_row + row_count]
            )
    return total


def project(left, right):
    return jnp.dot(left, right, preferred_element_type=jnp.float32)


def project_left(left, right):
    return lax.dot_general(
        left, right, (((0,), (0,)), ((), ())), preferred_element_type=jnp.float32
    )


def project_right(left, right):
    return lax.dot_general(
        left, right, (((1,), (1,)), ((), ())), preferred_element_type=jnp.float32
    )


def score_block(query, keys_all, pos_table, one_hot_ids, key_valid):
    query_heads = query.reshape(query.shape[0], HEADS, HEAD_DIM)
    key_heads = keys_all.reshape(keys_all.shape[0], HEADS, HEAD_DIM)
    rel_bias = jnp.einsum(
        "slb,bh->hsl",
        one_hot_ids,
        pos_table.reshape(BUCKETS, HEADS),
        preferred_element_type=jnp.float32,
    )
    scores = (
        jnp.einsum("shd,lhd->hsl", query_heads, key_heads, preferred_element_type=jnp.float32)
        + rel_bias
    )
    return jnp.where(key_valid[None, None, :], scores, -1e30)


def layer_forward(state, weights, one_hot_ids, key_valid):
    (
        tap_rows,
        biases,
        join_matrix,
        join_shift,
        gain_first,
        attn_in,
        attn_out,
        pos_table,
        gain_second,
        mlp_in,
        mlp_out,
    ) = weights
    row_count = state.shape[0]
    rounded_in = state.astype(jnp.bfloat16)
    prior_rows = passed_along(rounded_in[row_count - 3 :], "seq", 1)
    extended = jnp.concatenate([prior_rows, rounded_in], 0).astype(jnp.float32)
    mixed = conv_sum(
        extended, tap_rows.astype(jnp.float32), biases.astype(jnp.float32), row_count
    ).astype(jnp.bfloat16)
    joined = state + project(mixed, join_matrix) + join_shift.astype(jnp.float32)
    normed = rms_norm(joined, gain_first.astype(jnp.float32)).astype(jnp.bfloat16)
    projected = jnp.einsum(
        "sd,cdi->csi", normed, attn_in, preferred_element_type=jnp.float32
    ).astype(jnp.bfloat16)
    keys_all, values_all = (
        lax.all_gather(projected[1], "seq", axis=0, tiled=True),
        lax.all_gather(projected[2], "seq", axis=0, tiled=True),
    )
    scores = score_block(projected[0], keys_all, pos_table, one_hot_ids, key_valid)
    row_max = jnp.max(scores, -1, keepdims=True)
    log_total = row_max + jnp.log(jnp.sum(jnp.exp(scores - row_max), -1, keepdims=True))
    probs = jnp.exp(scores - log_total)
    value_heads = values_all.reshape(values_all.shape[0], HEADS, HEAD_DIM)
    attended = jnp.einsum(
        "hsl,lhd->shd", probs.astype(jnp.bfloat16), value_heads, preferred_element_type=jnp.float32
    )
    attended = attended.reshape(row_count, -1).astype(jnp.bfloat16)
    mid_state = joined + project(attended, attn_out)
    normed_mid = rms_norm(mid_state, gain_second.astype(jnp.float32)).astype(jnp.bfloat16)
    gate_up = jnp.einsum("sd,cdf->csf", normed_mid, mlp_in, preferred_element_type=jnp.float32)
    hidden = (jax.nn.gelu(gate_up[0], approximate=True) * gate_up[1]).astype(jnp.bfloat16)
    out_state = mid_state + project(hidden, mlp_out)
    saved = (
        extended,
        mixed,
        joined,
        normed,
        projected,
        keys_all,
        values_all,
        log_total,
        attended,
        mid_state,
        normed_mid,
        gate_up,
        hidden,
    )
    return (out_state, saved)


def gated_unit(gate_in, up_in):
    return jax.nn.gelu(gate_in, approximate=True) * up_in


def layer_backward(grad_out, saved, weights, one_hot_ids, key_valid):
    (
        tap_rows,
        biases,
        join_matrix,
        join_shift,
        gain_first,
        attn_in,
        attn_out,
        pos_table,
        gain_second,
        mlp_in,
        mlp_out,
    ) = weights
    (
        extended,
        mixed,
        joined,
        normed,
        projected,
        keys_all,
        values_all,
        log_total,
        attended,
        mid_state,
        normed_mid,
        gate_up,
        hidden,
    ) = saved
    row_count = grad_out.shape[0]
    model_width = grad_out.shape[1]
    grad_branch = grad_out.astype(jnp.bfloat16)
    grad_mlp_out = project_left(hidden, grad_branch)
    grad_hidden = project_right(grad_branch, mlp_out)
    unused_value, gelu_back = jax.vjp(gated_unit, gate_up[0], gate_up[1])
    grad_gate, grad_up = gelu_back(grad_hidden)
    grad_gate_up = jnp.stack([grad_gate, grad_up]).astype(jnp.bfloat16)
    grad_mlp_in = jnp.einsum(
        "sd,csf->cdf", normed_mid, grad_gate_up, preferred_element_type=jnp.float32
    )
    grad_normed_mid = jnp.einsum(
        "csf,cdf->sd", grad_gate_up, mlp_in, preferred_element_type=jnp.float32
    )
    unused_mid, mid_back = jax.vjp(rms_norm, mid_state, gain_second.astype(jnp.float32))
    grad_mid_part, grad_gain_second = mid_back(grad_normed_mid)
    grad_mid = grad_out + grad_mid_part
    grad_attn = grad_mid.astype(jnp.bfloat16)
    grad_attn_out = project_left(attended, grad_attn)
    grad_attended = (
        project_right(grad_attn, attn_out).astype(jnp.bfloat16).reshape(row_count, HEADS, HEAD_DIM)
    )
    query = projected[0]
    scores = score_block(query, keys_all, pos_table, one_hot_ids, key_valid)
    probs = jnp.exp(scores - log_total)
    value_heads = values_all.reshape(values_all.shape[0], HEADS, HEAD_DIM)
    key_heads = keys_all.reshape(keys_all.shape[0], HEADS, HEAD_DIM)
    query_heads = query.reshape(row_count, HEADS, HEAD_DIM)
    grad_probs = jnp.einsum(
        "shd,lhd->hsl", grad_attended, value_heads, preferred_element_type=jnp.float32
    )
    row_delta = jnp.sum(probs * grad_probs, -1, keepdims=True)
    grad_scores = (probs * (grad_probs - row_delta)).astype(jnp.bfloat16)
    grad_table = jnp.einsum(
        "slb,hsl->bh", one_hot_ids, grad_scores, preferred_element_type=jnp.float32
    ).reshape(-1)
    grad_query = jnp.einsum(
        "hsl,lhd->shd", grad_scores, key_heads, preferred_element_type=jnp.float32
    ).reshape(row_count, -1)
    grad_values_all = jnp.einsum(
        "hsl,shd->lhd",
        probs.astype(jnp.bfloat16),
        grad_attended,
        preferred_element_type=jnp.float32,
    )
    grad_keys_all = jnp.einsum(
        "hsl,shd->lhd", grad_scores, query_heads, preferred_element_type=jnp.float32
    )
    key_total = grad_keys_all.shape[0]
    grad_key, grad_value = (
        lax.psum_scatter(
            grad_keys_all.reshape(key_total, -1).astype(jnp.bfloat16),
            "seq",
            scatter_dimension=0,
            tiled=True,
        ).astype(jnp.float32),
        lax.psum_scatter(
            grad_values_all.reshape(key_total, -1).astype(jnp.bfloat16),
            "seq",
            scatter_dimension=0,
            tiled=True,
        ).astype(jnp.float32),
    )
    grad_projected = jnp.stack([grad_query, grad_key, grad_value]).astype(jnp.bfloat16)
    grad_attn_in = jnp.einsum(
        "sd,csi->cdi", normed, grad_projected, preferred_element_type=jnp.float32
    )
    grad_normed = jnp.einsum(
        "csi,cdi->sd", grad_projected, attn_in, preferred_element_type=jnp.float32
    )
    unused_joined, joined_back = jax.vjp(rms_norm, joined, gain_first.astype(jnp.float32))
    grad_joined_part, grad_gain_first = joined_back(grad_normed)
    grad_joined = grad_mid + grad_joined_part
    grad_join = grad_joined.astype(jnp.bfloat16)
    grad_join_matrix = project_left(mixed, grad_join)
    grad_join_shift = jnp.sum(grad_join.astype(jnp.float32), 0)
    grad_mixed = project_right(grad_join, join_matrix).astype(jnp.bfloat16).astype(jnp.float32)
    grad_biases = jnp.broadcast_to(jnp.sum(grad_mixed, 0), (3, model_width))
    tap_float = tap_rows.astype(jnp.float32)
    grad_taps = [None] * 9
    grad_extended = jnp.zeros((row_count + 3, model_width), jnp.float32)
    for window, offset in windows:
        for tap_index in range(window):
            first_row = 4 - window + tap_index
            grad_taps[offset + tap_index] = jnp.sum(
                grad_mixed * extended[first_row : first_row + row_count], 0
            )
            grad_extended = grad_extended + jnp.pad(
                tap_float[offset + tap_index] * grad_mixed, ((first_row, 3 - first_row), (0, 0))
            )
    back_rows = passed_along(grad_extended[:3], "seq", -1)
    grad_in = grad_joined + grad_extended[3:] + jnp.pad(back_rows, ((row_count - 3, 0), (0, 0)))
    layer_grads = (
        jnp.stack(grad_taps),
        grad_biases,
        grad_join_matrix,
        grad_join_shift,
        grad_gain_first,
        grad_attn_in,
        grad_attn_out,
        grad_table,
        grad_gain_second,
        grad_mlp_in,
        grad_mlp_out,
    )
    return (grad_in, layer_grads)


def body(
    byte_states,
    teacher,
    lengths,
    conv_taps,
    conv_bias,
    join_weight,
    join_bias,
    gain_attn,
    attn_in_weight,
    attn_out_weight,
    position_bias,
    gain_mlp,
    mlp_in_weight,
    mlp_out_weight,
):
    layer_count = conv_taps.shape[0]
    micro_count = byte_states.shape[0]
    row_count = byte_states.shape[2]
    model_width = byte_states.shape[3]
    seq_total = row_count * lax.axis_size("seq")
    positions = lax.axis_index("seq") * row_count + jnp.arange(row_count)
    key_positions = jnp.arange(seq_total)
    bucket_grid = bucket_ids(key_positions[None, :] - positions[:, None])
    one_hot_ids = (bucket_grid[:, :, None] == jnp.arange(BUCKETS)[None, None, :]).astype(
        jnp.bfloat16
    )
    total_valid = lax.psum(jnp.sum(lengths.astype(jnp.float32)), "batch")
    sums = [None] * layer_count
    out_rows = []
    grad_rows = []
    local_squares = jnp.zeros((), jnp.float32)
    for batch_index in range(micro_count):
        state = byte_states[batch_index, 0].astype(jnp.float32)
        length = lengths[batch_index, 0]
        key_valid = key_positions < length
        row_valid = positions < length
        kept = []
        for layer_index in range(layer_count):
            weights = (
                lax.all_gather(conv_taps[layer_index], ("seq", "batch"), axis=1, tiled=True),
                lax.all_gather(conv_bias[layer_index], ("seq", "batch"), axis=1, tiled=True),
                lax.all_gather(join_weight[layer_index], ("seq", "batch"), axis=0, tiled=True),
                lax.all_gather(join_bias[layer_index], ("seq", "batch"), axis=0, tiled=True),
                lax.all_gather(gain_attn[layer_index], ("seq", "batch"), axis=0, tiled=True),
                lax.all_gather(attn_in_weight[layer_index], ("seq", "batch"), axis=1, tiled=True),
                lax.all_gather(attn_out_weight[layer_index], ("seq", "batch"), axis=0, tiled=True),
                lax.all_gather(position_bias[layer_index], ("seq", "batch"), axis=0, tiled=True),
                lax.all_gather(gain_mlp[layer_index], ("seq", "batch"), axis=0, tiled=True),
                lax.all_gather(mlp_in_weight[layer_index], ("seq", "batch"), axis=1, tiled=True),
                lax.all_gather(mlp_out_weight[layer_index], ("seq", "batch"), axis=0, tiled=True),
            )
            state, saved = layer_forward(state, weights, one_hot_ids, key_valid)
            kept.append(saved)
        out_rows.append(state)
        diff = jnp.where(
            row_valid[:, None], state - teacher[batch_index, 0].astype(jnp.float32), 0.0
        )
        local_squares = local_squares + jnp.sum(diff * diff)
        grad_state = 2.0 * diff / (total_valid * model_width)
        for layer_index in reversed(range(layer_count)):
            weights = (
                lax.all_gather(conv_taps[layer_index], ("seq", "batch"), axis=1, tiled=True),
                lax.all_gather(conv_bias[layer_index], ("seq", "batch"), axis=1, tiled=True),
                lax.all_gather(join_weight[layer_index], ("seq", "batch"), axis=0, tiled=True),
                lax.all_gather(join_bias[layer_index], ("seq", "batch"), axis=0, tiled=True),
                lax.all_gather(gain_attn[layer_index], ("seq", "batch"), axis=0, tiled=True),
                lax.all_gather(attn_in_weight[layer_index], ("seq", "batch"), axis=1, tiled=True),
                lax.all_gather(attn_out_weight[layer_index], ("seq", "batch"), axis=0, tiled=True),
                lax.all_gather(position_bias[layer_index], ("seq", "batch"), axis=0, tiled=True),
                lax.all_gather(gain_mlp[layer_index], ("seq", "batch"), axis=0, tiled=True),
                lax.all_gather(mlp_in_weight[layer_index], ("seq", "batch"), axis=1, tiled=True),
                lax.all_gather(mlp_out_weight[layer_index], ("seq", "batch"), axis=0, tiled=True),
            )
            grad_state, layer_grads = layer_backward(
                grad_state, kept[layer_index], weights, one_hot_ids, key_valid
            )
            if sums[layer_index] is None:
                sums[layer_index] = layer_grads
            else:
                sums[layer_index] = jax.tree.map(jnp.add, sums[layer_index], layer_grads)
        grad_rows.append(grad_state)
    loss = lax.psum(local_squares, ("seq", "batch")) / (total_valid * model_width)
    stacked_grads = tuple(
        (
            jnp.stack([sums[layer_index][member] for layer_index in range(layer_count)])
            for member in range(11)
        )
    )
    (
        grad_taps,
        grad_biases,
        grad_join_matrix,
        grad_join_shift,
        grad_gain_first,
        grad_attn_in,
        grad_attn_out,
        grad_table,
        grad_gain_second,
        grad_mlp_in,
        grad_mlp_out,
    ) = stacked_grads
    owned = (
        lax.psum_scatter(grad_taps, ("seq", "batch"), scatter_dimension=2, tiled=True),
        lax.psum_scatter(grad_biases, ("seq", "batch"), scatter_dimension=2, tiled=True),
        lax.psum_scatter(grad_join_matrix, ("seq", "batch"), scatter_dimension=1, tiled=True),
        lax.psum_scatter(grad_join_shift, ("seq", "batch"), scatter_dimension=1, tiled=True),
        lax.psum_scatter(grad_gain_first, ("seq", "batch"), scatter_dimension=1, tiled=True),
        lax.psum_scatter(grad_attn_in, ("seq", "batch"), scatter_dimension=2, tiled=True),
        lax.psum_scatter(grad_attn_out, ("seq", "batch"), scatter_dimension=1, tiled=True),
        lax.psum_scatter(grad_table, ("seq", "batch"), scatter_dimension=1, tiled=True),
        lax.psum_scatter(grad_gain_second, ("seq", "batch"), scatter_dimension=1, tiled=True),
        lax.psum_scatter(grad_mlp_in, ("seq", "batch"), scatter_dimension=2, tiled=True),
        lax.psum_scatter(grad_mlp_out, ("seq", "batch"), scatter_dimension=1, tiled=True),
    )
    activations = jnp.stack(out_rows)[:, None]
    input_grad = jnp.stack(grad_rows)[:, None]
    return (
        activations,
        loss,
        input_grad,
        owned[0],
        owned[1],
        owned[2],
        owned[3],
        owned[4],
        owned[5],
        owned[6],
        owned[7],
        owned[8],
        owned[9],
        owned[10],
    )


ALL = ("seq", "z", "core")
LOW = jnp.bfloat16
WIDE = jnp.float32
BLOCK = 256
SHARE = 16
MASKED = -1e30


def nt(left, right):
    return lax.dot_general(left, right, (((1,), (1,)), ((), ())), preferred_element_type=WIDE)


def nn(left, right):
    return lax.dot_general(left, right, (((1,), (0,)), ((), ())), preferred_element_type=WIDE)


def tn(left, right):
    return lax.dot_general(left, right, (((0,), (0,)), ((), ())), preferred_element_type=WIDE)


def band_kernel(line_ref, band_ref):
    wide = jnp.broadcast_to(line_ref[0], (BLOCK, 4 * BLOCK))
    rolled = pltpu.roll(wide, 0, 1, stride=1, stride_axis=0)
    band_ref[0, 0] = rolled[:, :BLOCK]
    band_ref[0, 1] = rolled[:, BLOCK : 2 * BLOCK]
    band_ref[0, 2] = rolled[:, 3 * BLOCK :]


def build_band(line):
    return pl.pallas_call(
        band_kernel,
        grid=(HEADS,),
        in_specs=[pl.BlockSpec((1, 1, 4 * BLOCK), lambda h: (h, 0, 0))],
        out_specs=pl.BlockSpec((1, 3, BLOCK, BLOCK), lambda h: (h, 0, 0, 0)),
        out_shape=jax.ShapeDtypeStruct((HEADS, 3, BLOCK, BLOCK), WIDE),
        name="bias_band",
    )(line.reshape(HEADS, 1, 4 * BLOCK))


def key_blocks(core, near):
    near_rows = pl.multiple_of(BLOCK * (1 - core), BLOCK)
    far_rows = pl.multiple_of(BLOCK * core, BLOCK)
    below, above = 1 + core, 2 - core
    if near:
        return near_rows, ((0, near_rows, 0), (0, far_rows, below), (1, far_rows, above), (1, near_rows, None))
    return far_rows, ((0, far_rows, 0), (0, near_rows, above), (1, far_rows, None), (1, near_rows, None))


def keys_with_mask(block, lane, head, first_position, length, constant):
    rows = first_position + lax.broadcasted_iota(jnp.int32, (BLOCK, 1), 0)
    mask = jnp.where(rows < length, 0.0, MASKED)
    spare = (1 - head) * HEAD_DIM
    extra = jnp.where(lane == spare, mask, jnp.where(lane == spare + 1, constant, 0.0))
    return jnp.where(lane // HEAD_DIM == head, block.astype(WIDE), extra).astype(LOW)


def query_with_ones(block, lane, head):
    spare = (1 - head) * HEAD_DIM
    extra = jnp.where((lane == spare) | (lane == spare + 1), 1.0, 0.0)
    return jnp.where(lane // HEAD_DIM == head, block.astype(WIDE), extra).astype(LOW)


def only_head(block, lane, head):
    return jnp.where(lane // HEAD_DIM == head, block.astype(WIDE), 0.0).astype(LOW)


def attend_kernel(
    info_ref, far_ref, q_ref, k_ref, v_ref, ko_ref, vo_ref, band_ref, out_ref, lse_ref, score_ref
):
    core, length = info_ref[0], info_ref[1]
    pair = pl.program_id(0)
    lane = lax.broadcasted_iota(jnp.int32, (1, 2 * HEAD_DIM), 1)
    for n in range(2):
        q_rows, blocks = key_blocks(core, n == 0)
        query = q_ref[pl.ds(q_rows, BLOCK), :]
        halves = []
        for head in range(2):
            q_low = query_with_ones(query, lane, head)
            top = None
            for b, (side, start, slot) in enumerate(blocks):
                first = 2 * BLOCK * (core if side == 0 else 1 - core) + start
                keys = (k_ref, ko_ref)[side][pl.ds(start, BLOCK), :]
                constant = far_ref[2 * pair + head] if slot is None else 0.0
                scores = nt(keys_with_mask(keys, lane, head, first, length, constant), q_low)
                if slot is not None:
                    scores = scores + band_ref[head, slot]
                score_ref[b] = scores
                block_top = jnp.max(scores, 0, keepdims=True)
                top = block_top if top is None else jnp.maximum(top, block_top)
            total = jnp.zeros((1, BLOCK), WIDE)
            mixed = jnp.zeros((2 * HEAD_DIM, BLOCK), WIDE)
            for b, (side, start, slot) in enumerate(blocks):
                weights = jnp.exp(score_ref[b] - top)
                total = total + jnp.sum(weights, 0, keepdims=True)
                values = (v_ref, vo_ref)[side][pl.ds(start, BLOCK), :]
                mixed = mixed + tn(values, weights.astype(LOW))
            lse_ref[0, n, head : head + 1, :] = top + jnp.log(total)
            halves.append((mixed / total)[head * HEAD_DIM : (head + 1) * HEAD_DIM])
        out_ref[pl.ds(q_rows, BLOCK), :] = jnp.transpose(jnp.concatenate(halves, 0)).astype(LOW)


def attend(info, far, projected, others, band):
    rows = projected.shape[0]
    pairs = HEADS // 2
    width = 2 * HEAD_DIM
    col = lambda shift: pl.BlockSpec((rows, width), lambda p: (0, p + shift))
    return pl.pallas_call(
        attend_kernel,
        grid=(pairs,),
        in_specs=[
            pl.BlockSpec(memory_space=pltpu.SMEM),
            pl.BlockSpec(memory_space=pltpu.SMEM),
            col(0),
            col(pairs),
            col(2 * pairs),
            col(0),
            col(pairs),
            pl.BlockSpec((2, 3, BLOCK, BLOCK), lambda p: (p, 0, 0, 0)),
        ],
        out_specs=[col(0), pl.BlockSpec((1, 2, 2, BLOCK), lambda p: (p, 0, 0, 0))],
        out_shape=[
            jax.ShapeDtypeStruct((rows, HEADS * HEAD_DIM), LOW),
            jax.ShapeDtypeStruct((pairs, 2, 2, BLOCK), WIDE),
        ],
        scratch_shapes=[pltpu.VMEM((4, BLOCK, BLOCK), WIDE)],
        name="attend",
    )(info, far, projected, projected, projected, others, others, band)


def attend_back_kernel(
    info_ref,
    far_ref,
    q_ref,
    k_ref,
    v_ref,
    ko_ref,
    vo_ref,
    band_ref,
    out_ref,
    gout_ref,
    lse_ref,
    *refs,
):
    gq_ref, gown_ref, goth_ref, gband_ref, gfar_ref, gk_acc, gv_acc, band_acc, far_acc = refs[-9:]
    core, length, first_pair = info_ref[0], info_ref[1], info_ref[2]
    pair = first_pair + pl.program_id(0)
    width = 2 * HEAD_DIM
    lane = lax.broadcasted_iota(jnp.int32, (1, width), 1)
    gk_acc[...] = jnp.zeros_like(gk_acc)
    gv_acc[...] = jnp.zeros_like(gv_acc)
    band_acc[...] = jnp.zeros_like(band_acc)
    far_acc[...] = jnp.zeros_like(far_acc)
    select = jnp.where(
        lax.broadcasted_iota(jnp.int32, (8, width), 0)
        == lax.broadcasted_iota(jnp.int32, (8, width), 1) // HEAD_DIM,
        1.0,
        0.0,
    )
    for n in range(2):
        q_rows, blocks = key_blocks(core, n == 0)
        query = q_ref[pl.ds(q_rows, BLOCK), :]
        gout = gout_ref[pl.ds(q_rows, BLOCK), :]
        dots = gout.astype(WIDE) * out_ref[pl.ds(q_rows, BLOCK), :].astype(WIDE)
        deltas = lax.dot_general(
            select,
            dots,
            (((1,), (1,)), ((), ())),
            precision=lax.Precision.HIGHEST,
            preferred_element_type=WIDE,
        )
        halves = []
        for head in range(2):
            q_ones = query_with_ones(query, lane, head)
            q_low = only_head(query, lane, head)
            g_low = only_head(gout, lane, head)
            lse = lse_ref[0, n, head : head + 1, :]
            delta = deltas[head : head + 1]
            gq = jnp.zeros((width, BLOCK), WIDE)
            for side, start, slot in blocks:
                first = 2 * BLOCK * (core if side == 0 else 1 - core) + start
                keys = (k_ref, ko_ref)[side][pl.ds(start, BLOCK), :]
                values = (v_ref, vo_ref)[side][pl.ds(start, BLOCK), :]
                constant = far_ref[2 * pair + head] if slot is None else 0.0
                scores = nt(keys_with_mask(keys, lane, head, first, length, constant), q_ones)
                if slot is not None:
                    scores = scores + band_ref[head, slot]
                probs = jnp.exp(scores - lse)
                gprobs = nt(values, g_low)
                gscores = probs * (gprobs - delta)
                if slot is None:
                    part = jnp.sum(gscores.reshape(BLOCK // 8, 8, BLOCK), 0)
                    far_acc[head] = far_acc[head] + part
                else:
                    band_acc[head, slot] = band_acc[head, slot] + gscores
                gs_low = gscores.astype(LOW)
                at = pl.ds(2 * BLOCK * side + start, BLOCK)
                gv_acc[at, :] = gv_acc[at, :] + nn(probs.astype(LOW), g_low)
                gk_acc[at, :] = gk_acc[at, :] + nn(gs_low, q_low)
                gq = gq + tn(keys, gs_low)
            halves.append(gq[head * HEAD_DIM : (head + 1) * HEAD_DIM])
        gq_ref[pl.ds(q_rows, BLOCK), :] = jnp.transpose(jnp.concatenate(halves, 0)).astype(LOW)
    own = 2 * BLOCK
    gown_ref[0] = gk_acc[:own, :]
    gown_ref[1] = gv_acc[:own, :]
    goth_ref[0] = gk_acc[own:, :].astype(LOW)
    goth_ref[1] = gv_acc[own:, :].astype(LOW)
    span = 4 * BLOCK
    gap = jnp.zeros((8, BLOCK), WIDE)
    row = lax.broadcasted_iota(jnp.int32, (8, span), 0)
    for head in range(2):
        lines = jnp.zeros((8, span), WIDE)
        for g in range(BLOCK // 8):
            rows = slice(8 * g, 8 * g + 8)
            piece = jnp.concatenate(
                [band_acc[head, 0, rows], band_acc[head, 1, rows], gap, band_acc[head, 2, rows]], 1
            )
            lines = lines + (pltpu.roll(piece, span - 8 * g, 1) if g else piece)
        for bit in (1, 2, 4):
            lines = jnp.where((row & bit) != 0, pltpu.roll(lines, span - bit, 1), lines)
        gband_ref[0, head : head + 1, :] = jnp.sum(lines, 0, keepdims=True)
        gfar_ref[0, head : head + 1, :] = jnp.sum(far_acc[head], 0, keepdims=True)


def attend_back(info, far, projected, others, band, out, gout, lse, part, before=()):
    rows = projected.shape[0]
    pairs = HEADS // 2
    width = 2 * HEAD_DIM
    inner = HEADS * HEAD_DIM
    first = part * pairs // 2
    col = lambda shift: pl.BlockSpec((rows, width), lambda p: (0, first + p + shift))
    two = pl.BlockSpec((2, rows, width), lambda p: (0, 0, first + p))
    own = lambda *block: pl.BlockSpec(
        (block[0],) + block[1:], lambda p: (first + p,) + (0,) * (len(block) - 1)
    )
    info = jnp.concatenate([info, jnp.full((1,), first, jnp.int32)])
    return pl.pallas_call(
        attend_back_kernel,
        grid=(pairs // 2,),
        in_specs=[
            pl.BlockSpec(memory_space=pltpu.SMEM),
            pl.BlockSpec(memory_space=pltpu.SMEM),
            col(0),
            col(pairs),
            col(2 * pairs),
            col(0),
            col(pairs),
            own(2, 3, BLOCK, BLOCK),
            col(0),
            col(0),
            own(1, 2, 2, BLOCK),
        ]
        + [pl.BlockSpec(memory_space=pl.ANY)] * len(before),
        out_specs=[col(0), two, two, own(1, 2, 4 * BLOCK), own(1, 2, BLOCK)],
        out_shape=[
            jax.ShapeDtypeStruct((rows, inner), LOW),
            jax.ShapeDtypeStruct((2, rows, inner), WIDE),
            jax.ShapeDtypeStruct((2, rows, inner), LOW),
            jax.ShapeDtypeStruct((pairs, 2, 4 * BLOCK), WIDE),
            jax.ShapeDtypeStruct((pairs, 2, BLOCK), WIDE),
        ],
        input_output_aliases={11 + at: at for at in range(len(before))},
        scratch_shapes=[
            pltpu.VMEM((4 * BLOCK, width), WIDE),
            pltpu.VMEM((4 * BLOCK, width), WIDE),
            pltpu.VMEM((2, 3, BLOCK, BLOCK), WIDE),
            pltpu.VMEM((2, 8, BLOCK), WIDE),
        ],
        name="attend_back",
    )(info, far, projected, projected, projected, others, others, band, out, gout, lse, *before)


def store_terms(core, terms, kept_ref, sent_ref, at):
    for own in range(2):

        @pl.when(core == own)
        def _(own=own):
            kept_ref[at] = terms[:, own].astype(LOW)
            sent_ref[at] = terms[:, 1 - own].astype(LOW)


def unit_rows(values):
    inverse = lax.rsqrt(jnp.mean(values * values, -1, keepdims=True) + eps)
    return values * inverse, inverse


def normed(values, gain):
    return (unit_rows(values)[0] * gain).astype(LOW)


def normed_back(grad, values, gain):
    unit, inverse = unit_rows(values)
    scaled = grad * gain
    grad_in = inverse * (scaled - unit * jnp.mean(scaled * unit, -1, keepdims=True))
    return grad_in, jnp.sum(grad * unit, 0, keepdims=True)


def outward_chunk(block, share, width):
    owners = block.shape[0] // share
    parts = [
        block[:, at * width : (at + 1) * width].reshape(owners, 1, share, width)
        for at in range(block.shape[1] // width)
    ]
    return jnp.concatenate(parts, 1).reshape(-1, width)


ROOT = 0.7978845608028654
CUBIC = 0.044715


def mlp_kernel(att_ref, joined_ref, gain_ref, ao_ref, gate_ref, up_ref, out_ref, mid_ref, norm_ref, state_ref):
    width = att_ref.shape[1]

    @pl.when(pl.program_id(0) == 0)
    def _():
        mid = joined_ref[...] + nn(att_ref[...], ao_ref[...])
        mid_ref[...] = mid
        norm_ref[...] = normed(mid, gain_ref[...])
        state_ref[...] = mid

    norm = norm_ref[...]
    gate = nn(norm, gate_ref[...])
    turn = jnp.tanh(ROOT * (gate + CUBIC * gate * gate * gate))
    hidden = 0.5 * gate * (1.0 + turn) * nn(norm, up_ref[...])
    outward = outward_chunk(out_ref[...], SHARE, width)
    state_ref[...] += nn(hidden.astype(LOW), outward)


def rest_specs(width, quarters, layers, l):
    start = layers * quarters + l * (2 * quarters + 1)
    column = lambda first, moves: pl.BlockSpec(
        (width, width), lambda j: (0, start + first + j) if moves else (0, start + first)
    )
    return [
        column(0, False),
        column(1, True),
        column(1 + quarters, True),
        pl.BlockSpec((width // quarters, quarters * width), lambda j: (j, l)),
    ]


def mlp_forward(attended, joined, gain, rest, quarters, layers, l):
    rows, width = joined.shape
    whole = pl.BlockSpec((rows, width), lambda j: (0, 0))
    return pl.pallas_call(
        mlp_kernel,
        grid=(quarters,),
        in_specs=[whole, whole, pl.BlockSpec((1, width), lambda j: (0, 0))]
        + rest_specs(width, quarters, layers, l),
        out_specs=[whole] * 3,
        out_shape=[
            jax.ShapeDtypeStruct((rows, width), WIDE),
            jax.ShapeDtypeStruct((rows, width), LOW),
            jax.ShapeDtypeStruct((rows, width), WIDE),
        ],
        name="mlp",
    )(attended, joined, gain.reshape(1, width), rest, rest, rest, rest)


def mlp_back_kernel(
    info_ref,
    grad_ref,
    norm_ref,
    mid_ref,
    gain_ref,
    ao_ref,
    gate_ref,
    up_ref,
    out_ref,
    gmid_ref,
    gmid_low_ref,
    gatt_ref,
    ggain_ref,
    kept_ref,
    sent_ref,
    turned_ref,
    low_ref,
    gnorm_ref,
):
    core = info_ref[0]
    step = pl.program_id(0)
    owners, blocks, share, width = kept_ref.shape
    quarters = blocks // 3

    @pl.when(step == 0)
    def _():
        turned_ref[...] = jnp.transpose(norm_ref[...])
        low_ref[...] = grad_ref[...].astype(LOW)
        gnorm_ref[...] = jnp.zeros_like(gnorm_ref)

    norm, low = norm_ref[...], low_ref[...]
    gate, up = nn(norm, gate_ref[...]), nn(norm, up_ref[...])
    square = gate * gate
    turn = jnp.tanh(ROOT * gate * (1.0 + CUBIC * square))
    half = 0.5 * (1.0 + turn)
    slope = half + 0.5 * ROOT * gate * (1.0 - turn * turn) * (1.0 + 3.0 * CUBIC * square)
    bent = half * gate
    g_hidden = nt(low, outward_chunk(out_ref[...], share, width))
    g_gate = (g_hidden * up * slope).astype(LOW)
    g_up = (g_hidden * bent).astype(LOW)
    hidden = (bent * up).astype(LOW)
    every = slice(None)
    for at, part in ((step, g_gate), (step + quarters, g_up)):
        terms = nn(turned_ref[...], part).reshape(owners, 2, share, width)
        store_terms(core, terms, kept_ref, sent_ref, (every, at))
    few = owners // quarters
    terms = tn(hidden, low).reshape(few, 2, quarters, share, width)
    at = (pl.ds(step * few, few), slice(2 * quarters, blocks))
    store_terms(core, terms, kept_ref, sent_ref, at)
    gnorm_ref[...] += nt(g_gate, gate_ref[...]) + nt(g_up, up_ref[...])

    @pl.when(step == quarters - 1)
    def _():
        part, ggain_ref[...] = normed_back(gnorm_ref[...], mid_ref[...], gain_ref[...])
        g_mid = grad_ref[...] + part
        gmid_ref[...] = g_mid
        g_low = g_mid.astype(LOW)
        gmid_low_ref[...] = g_low
        gatt_ref[...] = nt(g_low, ao_ref[...]).astype(LOW)


def mlp_back(info, grad, norm, mid, gain, rest, quarters, layers, l, owners, share):
    rows, width = grad.shape
    shape = jax.ShapeDtypeStruct((owners, 3 * quarters, share, width), LOW)
    whole = pl.BlockSpec((rows, width), lambda j: (0, 0))
    line = pl.BlockSpec((1, width), lambda j: (0, 0))
    out = pl.BlockSpec(shape.shape, lambda j: (0, 0, 0, 0))
    return pl.pallas_call(
        mlp_back_kernel,
        grid=(quarters,),
        in_specs=[pl.BlockSpec(memory_space=pltpu.SMEM), whole, whole, whole, line]
        + rest_specs(width, quarters, layers, l),
        out_specs=[whole, whole, whole, line, out, out],
        out_shape=[
            jax.ShapeDtypeStruct((rows, width), WIDE),
            jax.ShapeDtypeStruct((rows, width), LOW),
            jax.ShapeDtypeStruct((rows, width), LOW),
            jax.ShapeDtypeStruct((1, width), WIDE),
            shape,
            shape,
        ],
        scratch_shapes=[
            pltpu.VMEM((width, rows), LOW),
            pltpu.VMEM((rows, width), LOW),
            pltpu.VMEM((rows, width), WIDE),
        ],
        name="mlp_back",
    )(info, grad, norm, mid, gain.reshape(1, width), rest, rest, rest, rest)


def attn_terms_kernel(
    info_ref,
    mixed_ref,
    gjoin_ref,
    norm_ref,
    gquery_ref,
    gkv_ref,
    att_ref,
    gmid_ref,
    small_ref,
    kept_ref,
    sent_ref,
):
    core = info_ref[0]
    owners, blocks, share, width = kept_ref.shape

    def put(at, turned, right):
        terms = nn(turned, right).reshape(owners, 2, share, width)
        store_terms(core, terms, kept_ref, sent_ref, (slice(None), at))

    put(0, jnp.transpose(mixed_ref[...]), gjoin_ref[...])
    turned = jnp.transpose(norm_ref[...])
    put(1, turned, gquery_ref[...])
    put(2, turned, gkv_ref[0])
    put(3, turned, gkv_ref[1])
    put(4, jnp.transpose(att_ref[...]), gmid_ref[...])
    small = jnp.broadcast_to(small_ref[...].astype(LOW)[None], (owners, share, width))
    kept_ref[:, 5] = small
    sent_ref[:, 5] = small


def attn_terms(info, mixed, gjoin, norm, gquery, gkv, att, gmid, small, owners, share):
    width = mixed.shape[1]
    shape = jax.ShapeDtypeStruct((owners, 6, share, width), LOW)
    vmem = pl.BlockSpec(memory_space=pltpu.VMEM)
    return pl.pallas_call(
        attn_terms_kernel,
        in_specs=[pl.BlockSpec(memory_space=pltpu.SMEM)] + [vmem] * 8,
        out_specs=[vmem, vmem],
        out_shape=[shape, shape],
        name="attn_terms",
    )(info, mixed, gjoin, norm, gquery, gkv, att, gmid, small)


def pack_kernel(
    info_ref,
    lengths_ref,
    taps_ref,
    bias_ref,
    join_ref,
    join_bias_ref,
    gain_attn_ref,
    attn_in_ref,
    attn_out_ref,
    position_ref,
    gain_mlp_ref,
    mlp_in_ref,
    mlp_out_ref,
    *refs,
):
    small_ref = refs[-1]
    device = info_ref[0]
    layers, share, width = join_ref.shape
    lane = lax.broadcasted_iota(jnp.int32, (share, width), 1)
    item = lax.broadcasted_iota(jnp.int32, (share, width), 0)
    spread = jnp.where(lane == device * share + item, 1.0, 0.0).astype(LOW)
    place = lane[:1] - device * share - HEADS
    extra = jnp.zeros((1, width), WIDE)
    for m in range(lengths_ref.shape[0]):
        whole, rest = lengths_ref[m] // 32, lengths_ref[m] % 32
        extra = extra + jnp.where(place == 2 * m, whole, jnp.where(place == 2 * m + 1, rest, 0)).astype(WIDE)
    for l in range(layers):
        small_ref[0:9] = nn(taps_ref[:, l], spread)
        small_ref[9:12] = nn(bias_ref[:, l], spread)
        small_ref[12:13] = nn(join_bias_ref[l : l + 1], spread)
        small_ref[13:14] = nn(gain_attn_ref[l : l + 1], spread)
        small_ref[14:15] = nn(gain_mlp_ref[l : l + 1], spread)
        small_ref[15:16] = nn(position_ref[l : l + 1], spread[:HEADS]) + extra
        first = [join_ref[l]] + [attn_in_ref[l, c] for c in range(3)] + [small_ref[...].astype(LOW)]
        outward = [mlp_out_ref[l, a * share : (a + 1) * share] for a in range(mlp_out_ref.shape[1] // share)]
        inward = [attn_out_ref[l], mlp_in_ref[l, 0], mlp_in_ref[l, 1]]
        out_width = mlp_out_ref.shape[1] // share * width
        in_width = width + 2 * mlp_in_ref.shape[3]
        places = (
            (refs[l], 0, first),
            (refs[layers], l * out_width, outward),
            (refs[layers], layers * out_width + l * in_width, inward),
        )
        for out_ref, cursor, pieces in places:
            for piece in pieces:
                out_ref[:, cursor : cursor + piece.shape[1]] = piece
                cursor += piece.shape[1]


def pack(info, lengths, arrays, share):
    layers, width = arrays[2].shape[0], arrays[2].shape[2]
    quarters = arrays[-2].shape[3] // width
    first, rest = 5 * width, (1 + 3 * quarters) * width
    smem = pl.BlockSpec(memory_space=pltpu.SMEM)
    vmem = pl.BlockSpec(memory_space=pltpu.VMEM)
    return pl.pallas_call(
        pack_kernel,
        in_specs=[smem, smem] + [vmem] * len(arrays),
        out_specs=[vmem] * (layers + 1),
        out_shape=[
            jax.ShapeDtypeStruct((share, span), LOW) for span in [first] * layers + [layers * rest]
        ],
        scratch_shapes=[pltpu.VMEM((share, width), WIDE)],
        name="pack",
    )(info, lengths, *arrays)


def collected_kernel(device_ref, inverse_ref, *refs):
    device = device_ref[0]
    inputs, outputs = refs[:16], refs[16:]
    join_ref, attn_in_ref, attn_out_ref, mlp_in_ref, mlp_out_ref, loss_ref = outputs[:6]
    taps_ref, bias_ref, join_bias_ref, gain_attn_ref, gain_mlp_ref, position_ref = outputs[6:]
    share, width = join_ref.shape[1:]
    quarters = mlp_in_ref.shape[3] // width
    lane = lax.broadcasted_iota(jnp.int32, (share, width), 1)
    item = lax.broadcasted_iota(jnp.int32, (share, width), 0)
    own = jnp.where(lane == device * share + item, 1.0, 0.0)

    def total(pieces, at):
        return sum(piece[at].astype(WIDE) for piece in pieces)

    for l in range(2):
        mlp, attn = inputs[8 * l : 8 * l + 4], inputs[8 * l + 4 : 8 * l + 8]
        join_ref[l] = total(attn, 0)
        for c in range(3):
            attn_in_ref[l, c] = total(attn, 1 + c)
        attn_out_ref[l] = total(attn, 4)
        for c in range(2):
            for a in range(quarters):
                mlp_in_ref[l, c, :, a * width : (a + 1) * width] = total(mlp, c * quarters + a)
        for a in range(quarters):
            mlp_out_ref[l, a * share : (a + 1) * share] = total(mlp, 2 * quarters + a)
        small = total(attn, 5)
        small_own = lax.dot_general(
            small,
            own,
            (((1,), (1,)), ((), ())),
            precision=lax.Precision.HIGHEST,
            preferred_element_type=WIDE,
        )
        line = slice(l, l + 1)
        for at, tap in enumerate((2, 3, 1, 2, 3, 0, 1, 2, 3)):
            taps_ref[at, line] = small_own[tap : tap + 1]
        for at in range(3):
            bias_ref[at, line] = small_own[4:5]
        for at, out_ref in enumerate((join_bias_ref, gain_attn_ref, gain_mlp_ref)):
            out_ref[line] = small_own[5 + at : 6 + at]
        position_ref[line] = small_own[8:9, :HEADS]
        if l == 1:
            loss_ref[...] = jnp.sum(small[9:10], 1, keepdims=True) * inverse_ref[0]


def collected(device, inverse, layers, quarters):
    pieces = [piece for mlp, attn in layers for piece in list(mlp) + list(attn)]
    share, width = pieces[0].shape[1:]
    count = len(layers)
    shapes = [
        (count, share, width),
        (count, 3, share, width),
        (count, share, width),
        (count, 2, share, quarters * width),
        (count, quarters * share, width),
        (1, 1),
        (9, count, share),
        (3, count, share),
        (count, share),
        (count, share),
        (count, share),
        (count, HEADS),
    ]
    vmem = pl.BlockSpec(memory_space=pltpu.VMEM)
    return pl.pallas_call(
        collected_kernel,
        in_specs=[pl.BlockSpec(memory_space=pltpu.SMEM)] * 2 + [vmem] * len(pieces),
        out_specs=[vmem] * len(shapes),
        out_shape=[jax.ShapeDtypeStruct(shape, WIDE) for shape in shapes],
        name="collected",
    )(device, inverse, *pieces)


def tie(*values):
    return lax.optimization_barrier(values)


def chip_body(
    byte_states,
    teacher,
    lengths,
    conv_taps,
    conv_bias,
    join_weight,
    join_bias,
    gain_attn,
    attn_in_weight,
    attn_out_weight,
    position_bias,
    gain_mlp,
    mlp_in_weight,
    mlp_out_weight,
):
    layer_count = conv_taps.shape[0]
    model_width = byte_states.shape[3]
    slot_rows = byte_states.shape[2]
    rows = 2 * slot_rows
    hidden_width = mlp_in_weight.shape[3]
    quarters = hidden_width // model_width
    seqs, zs, cores = (lax.axis_size(name) for name in ALL)
    devices = seqs * zs * cores
    share = SHARE
    s_at, z_at, c_at = (lax.axis_index(name) for name in ALL)
    device_at = (s_at * zs + z_at) * cores + c_at

    def number(s, z, c):
        return (s * zs + z) * cores + c

    places = [(s, z, c) for s in range(seqs) for z in range(zs) for c in range(cores)]
    swap = [(number(s, z, c), number(s, z, 1 - c)) for s, z, c in places]
    routes = [
        [(number(s, z, c), number(2 * (s % 2 if turn == 0 else 1 - s % 2) + c, z, s // 2)) for s, z, c in places]
        for turn in range(2)
    ]
    back_routes = [[(b, a) for a, b in route] for route in routes]

    def to_chips(block):
        odd, high = s_at % 2, s_at // 2
        first, second = (
            lax.ppermute(jnp.where(odd == turn, block[0], block[1]), ALL, routes[turn]) for turn in range(2)
        )
        return jnp.concatenate(
            [jnp.where(high == 0, first, second), jnp.where(high == 0, second, first)], 0
        )

    def leave(block):
        high = s_at // 2
        halves = (block[:slot_rows], block[slot_rows:])
        return [
            lax.ppermute(jnp.where(high == turn, halves[0], halves[1]), ALL, back_routes[turn])
            for turn in range(2)
        ]

    def arrive(pieces):
        first, second = pieces
        odd = s_at % 2
        whole = jnp.stack([jnp.where(odd == 0, first, second), jnp.where(odd == 0, second, first)])
        return whole.astype(WIDE)[:, None]

    def trade(block):
        return lax.ppermute(block, ALL, swap)

    to_high = [(number(s, z, 0), number(s, z, 1)) for s, z, c in places if c == 0]
    to_low = [(b, a) for a, b in to_high]

    lanes = jnp.arange(model_width)
    lane_owner, lane_item = lanes // share, lanes % share
    every_layer = range(layer_count)
    packed = pack(
        device_at.astype(jnp.int32).reshape(1),
        lengths.reshape(-1),
        (
            conv_taps.transpose(1, 0, 2),
            conv_bias.transpose(1, 0, 2),
            join_weight,
            join_bias,
            gain_attn,
            attn_in_weight,
            attn_out_weight,
            position_bias,
            gain_mlp,
            mlp_in_weight,
            mlp_out_weight,
        ),
        share,
    )

    def moved(block, name, change):
        def target(s, z, c):
            return number(s ^ change, z, c) if name == "seq" else number(s, z ^ change, c)

        return lax.ppermute(block, ALL, [(number(s, z, c), target(s, z, c)) for s, z, c in places])

    def spread_out(block, name, at, size):
        whole = jnp.zeros((size,) + block.shape, block.dtype)
        pieces = [block] + [moved(block, name, change) for change in range(1, size)]
        for change, piece in enumerate(pieces):
            whole = lax.dynamic_update_index_in_dim(whole, piece, at ^ change, 0)
        return whole

    def pair_up(block):
        other = trade(block)
        return jnp.stack(
            [jnp.where(c_at == 0, block, other), jnp.where(c_at == 0, other, block)], 2
        ).reshape(model_width, -1)

    def split_halves(kept, arrived):
        shape = (seqs, zs) + kept.shape[1:]
        return kept.reshape(shape), arrived.reshape(shape)

    def plane_terms(kept, arrived):
        kept, arrived = split_halves(kept, arrived)
        pick = lambda whole, s: lax.dynamic_index_in_dim(whole, s, 0, False).astype(WIDE)
        return [
            (pick(kept, s_at ^ change) + pick(arrived, s_at ^ change)).astype(LOW)
            for change in range(seqs)
        ]

    def line_terms(pieces):
        total = finish(pieces).astype(LOW)
        return [lax.dynamic_index_in_dim(total, z_at ^ change, 0, False) for change in range(zs)]

    def send(name, terms):
        return [moved(part, name, change) if change else part for change, part in enumerate(terms)]

    def finish(pieces):
        return sum(piece.astype(WIDE) for piece in pieces)

    early, behind = spread_out(packed[0], "z", z_at, zs), packed[1]
    early = spread_out(early, "seq", s_at, seqs)
    early, behind = tie(early, behind)
    early = [pair_up(early), spread_out(spread_out(behind, "z", z_at, zs), "seq", s_at, seqs)]
    later = lax.all_gather(packed[2], ALL, axis=0, tiled=True)

    def unpack_first(first):
        small = jnp.sum(first[:, 4 * model_width :].reshape(devices, share, model_width).astype(WIDE), 0)
        return dict(
            join=first[:, :model_width],
            attn_in=first[:, model_width : 4 * model_width],
            taps=jnp.stack(
                [
                    small[5],
                    small[2] + small[6],
                    small[0] + small[3] + small[7],
                    small[1] + small[4] + small[8],
                ]
            ),
            bias=small[9] + small[10] + small[11],
            join_bias=small[12],
            gain_attn=small[13],
            gain_mlp=small[14],
            last=small[15],
        )

    weights = [unpack_first(early[0])]
    state = to_chips(byte_states[:, 0]).astype(WIDE)
    target = to_chips(teacher[:, 0])

    counts = weights[0]["last"]
    scale = jnp.where((lane_item >= HEADS) & (lane_item < HEADS + 4), jnp.where(lane_item % 2 == 0, 32.0, 1.0), 0.0)
    total_valid = jnp.sum(jnp.where(lane_owner < zs * cores, counts * scale, 0.0))
    mine = (lane_owner == z_at * cores + s_at % 2) & ((lane_item - HEADS) // 2 == s_at // 2)
    length = jnp.sum(jnp.where(mine, counts * scale, 0.0)).astype(jnp.int32)
    info = jnp.stack([c_at.astype(jnp.int32), length])
    row_valid = (rows * c_at + jnp.arange(rows) < length)[:, None]

    offsets = -((jnp.arange(4 * BLOCK) + 2 * BLOCK) % (4 * BLOCK) - 2 * BLOCK)
    in_bucket = (lane_owner[:, None] == bucket_ids(offsets)[None, :]).astype(LOW)
    of_head = (lane_item[None, :] == jnp.arange(HEADS)[:, None]).astype(WIDE)
    far_bucket = (lane_owner == jnp.where(c_at == 0, 31, 15)).astype(WIDE)

    def bias_of(last):
        line = jnp.dot((of_head * last).astype(LOW), in_bucket, preferred_element_type=WIDE)
        return jnp.sum(of_head * (last * far_bucket), 1), build_band(line)

    biases = [bias_of(weights[0]["last"])]
    kept = []
    for l in range(layer_count):
        w = weights[l]
        low_state = state.astype(LOW)
        prior = lax.ppermute(low_state[rows - 8 :], ALL, to_high)[5:]
        extended = jnp.concatenate([prior, low_state], 0).astype(WIDE)
        mixed = w["bias"] + sum(w["taps"][k] * extended[k : k + rows] for k in range(4))
        mixed = mixed.astype(LOW)
        joined = state + nn(mixed, w["join"]) + w["join_bias"]
        norm_a = normed(joined, w["gain_attn"])
        projected = nn(norm_a, w["attn_in"]).astype(LOW)
        others = trade(projected[:, HEADS * HEAD_DIM :])
        far, band = biases[l]
        attended, lse = attend(info, far, projected, others, band)
        if l + 1 < layer_count:
            attended, lse, early[l + 1] = tie(attended, lse, early[l + 1])
            weights.append(unpack_first(pair_up(early[l + 1])))
            biases.append(bias_of(weights[l + 1]["last"]))
            attended, lse, later, biases[l + 1], weights[l + 1], target = tie(
                attended, lse, later, biases[l + 1], weights[l + 1], target
            )
        mid, norm_m, state = mlp_forward(attended, joined, w["gain_mlp"], later, quarters, layer_count, l)
        kept.append(
            (extended, mixed, joined, norm_a, projected, others, far, band, attended, lse, mid, norm_m)
        )

    activations = leave(state)
    diff = jnp.where(row_valid, state - target.astype(WIDE), 0.0)
    squares = jnp.sum(diff * diff, 0)
    grad = 2.0 * diff / (total_valid * model_width)
    owners = seqs * zs
    mlp_way = attn_way = None
    for l in reversed(every_layer):
        w = weights[l]
        (extended, mixed, joined, norm_a, projected, others, far, band, attended, lse, mid, norm_m) = kept[l]
        g_mid, g_mid_low, g_att, g_gain_mlp, mlp_kept, mlp_sent = mlp_back(
            info, grad, norm_m, mid, w["gain_mlp"], later, quarters, layer_count, l, owners, share
        )
        if mlp_way is None:
            g_att, mlp_kept, mlp_sent, activations = tie(g_att, mlp_kept, mlp_sent, activations)
        else:
            g_att, mlp_kept, mlp_sent, mlp_way, attn_way = tie(
                g_att, mlp_kept, mlp_sent, mlp_way, attn_way
            )
            line = line_terms(attn_way)
            g_att, line = tie(g_att, line)
            attn_way = send("z", line)
        mlp_half = (mlp_kept, trade(mlp_sent))
        attention = (info, far, projected, others, band, attended, g_att, lse)
        back = attend_back(*attention, 0)
        back, mlp_half = tie(back, mlp_half)
        plane = plane_terms(*mlp_half)
        back, plane = tie(back, plane)
        mlp_half = send("seq", plane)
        back = attend_back(*attention, 1, back)
        mlp_near = mlp_half[: seqs - 1]
        back, mlp_near = tie(back, mlp_near)
        mlp_half = mlp_near + mlp_half[seqs - 1 :]
        g_query, g_own, g_other, g_band, g_far = back
        g_kv = (g_own + trade(g_other).astype(WIDE)).astype(LOW)
        g_norm = sum(
            nt(part, w["attn_in"][:, c * model_width : (c + 1) * model_width])
            for c, part in enumerate((g_query, g_kv[0], g_kv[1]))
        )
        g_joined, g_gain_attn = normed_back(g_norm, joined, w["gain_attn"])
        g_joined = g_mid + g_joined
        g_join_low = g_joined.astype(LOW)
        g_join_bias = jnp.sum(g_join_low.astype(WIDE), 0)
        g_mixed = nt(g_join_low, w["join"]).astype(LOW).astype(WIDE)
        g_taps = [jnp.sum(g_mixed * extended[k : k + rows], 0) for k in range(4)]
        g_bias = jnp.sum(g_mixed, 0)
        head_rows = [
            sum(w["taps"][k] * g_mixed[r - k : r - k + 1] for k in range(r + 1)) for r in range(3)
        ]
        beyond = lax.ppermute(
            jnp.concatenate(head_rows + [jnp.zeros((5, model_width), WIDE)], 0), ALL, to_low
        )
        padded = jnp.concatenate([g_mixed, jnp.zeros((3, model_width), WIDE)], 0)
        g_state = sum(w["taps"][k] * padded[3 - k : 3 - k + rows] for k in range(4))
        tail = jnp.concatenate([jnp.zeros((rows - 8, model_width), WIDE), jnp.zeros((5, model_width), WIDE), beyond[:3]], 0)
        grad = g_joined + g_state + tail

        by_lane = jnp.dot(
            g_band.reshape(HEADS, -1),
            in_bucket.T.astype(WIDE),
            precision=lax.Precision.HIGHEST,
            preferred_element_type=WIDE,
        )
        g_far = jnp.sum(g_far.reshape(HEADS, -1), 1)[:, None]
        g_last = jnp.sum(of_head * (by_lane + g_far * far_bucket), 0)
        small = jnp.stack(
            g_taps
            + [g_bias, g_join_bias, g_gain_attn[0], g_gain_mlp[0], g_last, squares]
            + [jnp.zeros((model_width,), WIDE)] * (share - 10)
        )
        if l == 0:
            g_join_low, mlp_half, attn_way = tie(g_join_low, mlp_half, attn_way)
            line = line_terms(mlp_half)
            g_join_low, line = tie(g_join_low, line)
            mlp_half = send("z", line)
        attn_kept, attn_sent = attn_terms(
            info, mixed, g_join_low, norm_a, g_query, g_kv, attended, g_mid_low, small, owners, share
        )
        if l > 0:
            grad, attn_kept, attn_sent, mlp_half = tie(grad, attn_kept, attn_sent, mlp_half)
            line = line_terms(mlp_half)
            attn_arrived, line = tie(trade(attn_sent), line)
            plane = plane_terms(attn_kept, attn_arrived)
            grad, line, plane = tie(grad, line, plane)
            attn_way, mlp_way = send("seq", plane), send("z", line)

    above_mlp, above_attn = mlp_way, attn_way
    grad, attn_kept, attn_sent, above_mlp = tie(grad, attn_kept, attn_sent, above_mlp)
    attn_way = send("seq", plane_terms(attn_kept, trade(attn_sent)))
    attn_way, mlp_way = tie(attn_way, mlp_half)
    grad, attn_way, above_attn = tie(grad.astype(LOW), attn_way, above_attn)
    attn_way = send("z", line_terms(attn_way))
    input_grad = leave(grad)
    (
        g_join,
        g_attn_in,
        g_attn_out,
        g_mlp_in,
        g_mlp_out,
        loss,
        g_taps,
        g_bias,
        g_join_bias,
        g_gain_attn,
        g_gain_mlp,
        g_position,
    ) = collected(
        device_at.astype(jnp.int32).reshape(1),
        (1.0 / (total_valid * model_width)).reshape(1),
        [(mlp_way, attn_way), (above_mlp, above_attn)],
        quarters,
    )
    loss = loss.reshape(())
    return (
        arrive(activations),
        loss,
        arrive(input_grad),
        g_taps.transpose(1, 0, 2),
        g_bias.transpose(1, 0, 2),
        g_join,
        g_join_bias,
        g_gain_attn,
        g_attn_in,
        g_attn_out,
        g_position,
        g_gain_mlp,
        g_mlp_in,
        g_mlp_out,
    )


def chip_plan(mesh):
    grid = Mesh(
        mesh.devices.reshape(mesh.shape["seq"], mesh.shape["batch"] // 2, 2),
        ALL,
    )
    batch = ("z", "core")
    in_specs = (
        P(None, batch, "seq", None),
        P(None, batch, "seq", None),
        P(None, batch),
        P(None, None, ALL),
        P(None, None, ALL),
        P(None, ALL, None),
        P(None, ALL),
        P(None, ALL),
        P(None, None, ALL, None),
        P(None, ALL, None),
        P(None, ALL),
        P(None, ALL),
        P(None, None, ALL, None),
        P(None, ALL, None),
    )
    out_specs = (in_specs[0], P(), in_specs[0]) + in_specs[3:]
    return jax.shard_map(chip_body, mesh=grid, in_specs=in_specs, out_specs=out_specs, check_vma=False)


def shared_plan(mesh):
    in_specs = (
        P(None, "batch", "seq", None),
        P(None, "batch", "seq", None),
        P(None, "batch"),
        P(None, None, ("seq", "batch")),
        P(None, None, ("seq", "batch")),
        P(None, ("seq", "batch"), None),
        P(None, ("seq", "batch")),
        P(None, ("seq", "batch")),
        P(None, None, ("seq", "batch"), None),
        P(None, ("seq", "batch"), None),
        P(None, ("seq", "batch")),
        P(None, ("seq", "batch")),
        P(None, None, ("seq", "batch"), None),
        P(None, ("seq", "batch"), None),
    )
    out_specs = (
        P(None, "batch", "seq", None),
        P(),
        P(None, "batch", "seq", None),
        P(None, None, ("seq", "batch")),
        P(None, None, ("seq", "batch")),
        P(None, ("seq", "batch"), None),
        P(None, ("seq", "batch")),
        P(None, ("seq", "batch")),
        P(None, None, ("seq", "batch"), None),
        P(None, ("seq", "batch"), None),
        P(None, ("seq", "batch")),
        P(None, ("seq", "batch")),
        P(None, None, ("seq", "batch"), None),
        P(None, ("seq", "batch"), None),
    )
    return jax.shard_map(body, mesh=mesh, in_specs=in_specs, out_specs=out_specs, check_vma=False)


def solution(mesh):
    shared = shared_plan(mesh)

    def run(*arrays):
        sequences = arrays[0].shape[0] * arrays[0].shape[1]
        one_per_chip = 2 * sequences == mesh.devices.size and 2 * arrays[0].shape[0] == mesh.shape["seq"]
        two_layers = arrays[3].shape[0] == 2
        lanes_fit = arrays[5].shape[1] == SHARE * mesh.devices.size and arrays[0].shape[2] == 4 * BLOCK
        plan = chip_plan(mesh) if one_per_chip and lanes_fit and two_layers else shared
        return plan(*arrays)

    return run
```

```python
import jax
import jax.numpy as jnp
from jax import lax
from jax.experimental import pallas as pl
from jax.experimental.pallas import tpu as pltpu
from jax.sharding import Mesh
from jax.sharding import PartitionSpec as P

HEADS = 8
HEAD_DIM = 64
BUCKETS = 32


eps = 1e-06
bounds = (12, 16, 23, 32, 46, 64, 91)
windows = ((2, 0), (3, 2), (4, 5))


def passed_along(block, axis, distance):
    devices = range(lax.axis_size(axis))
    route = [(i - distance, i) for i in devices if i - distance in devices]
    return lax.ppermute(block, axis, route)


def bucket_ids(offsets):
    magnitude = jnp.abs(offsets)
    far_ids = 8 + sum(((magnitude >= bound_value).astype(jnp.int32) for bound_value in bounds))
    near_ids = jnp.where(magnitude < 8, magnitude, far_ids)
    return jnp.where(offsets > 0, 16, 0) + near_ids


def rms_norm(values, gain):
    return values * lax.rsqrt(jnp.mean(values * values, -1, keepdims=True) + eps) * gain


def conv_sum(extended, tap_rows, biases, row_count):
    total = jnp.zeros((row_count, extended.shape[1]), jnp.float32) + jnp.sum(biases, 0)
    for window, offset in windows:
        for tap_index in range(window):
            first_row = 4 - window + tap_index
            total = (
                total + tap_rows[offset + tap_index] * extended[first_row : first_row + row_count]
            )
    return total


def project(left, right):
    return jnp.dot(left, right, preferred_element_type=jnp.float32)


def project_left(left, right):
    return lax.dot_general(
        left, right, (((0,), (0,)), ((), ())), preferred_element_type=jnp.float32
    )


def project_right(left, right):
    return lax.dot_general(
        left, right, (((1,), (1,)), ((), ())), preferred_element_type=jnp.float32
    )


def score_block(query, keys_all, pos_table, one_hot_ids, key_valid):
    query_heads = query.reshape(query.shape[0], HEADS, HEAD_DIM)
    key_heads = keys_all.reshape(keys_all.shape[0], HEADS, HEAD_DIM)
    rel_bias = jnp.einsum(
        "slb,bh->hsl",
        one_hot_ids,
        pos_table.reshape(BUCKETS, HEADS),
        preferred_element_type=jnp.float32,
    )
    scores = (
        jnp.einsum("shd,lhd->hsl", query_heads, key_heads, preferred_element_type=jnp.float32)
        + rel_bias
    )
    return jnp.where(key_valid[None, None, :], scores, -1e30)


def layer_forward(state, weights, one_hot_ids, key_valid):
    (
        tap_rows,
        biases,
        join_matrix,
        join_shift,
        gain_first,
        attn_in,
        attn_out,
        pos_table,
        gain_second,
        mlp_in,
        mlp_out,
    ) = weights
    row_count = state.shape[0]
    rounded_in = state.astype(jnp.bfloat16)
    prior_rows = passed_along(rounded_in[row_count - 3 :], "seq", 1)
    extended = jnp.concatenate([prior_rows, rounded_in], 0).astype(jnp.float32)
    mixed = conv_sum(
        extended, tap_rows.astype(jnp.float32), biases.astype(jnp.float32), row_count
    ).astype(jnp.bfloat16)
    joined = state + project(mixed, join_matrix) + join_shift.astype(jnp.float32)
    normed = rms_norm(joined, gain_first.astype(jnp.float32)).astype(jnp.bfloat16)
    projected = jnp.einsum(
        "sd,cdi->csi", normed, attn_in, preferred_element_type=jnp.float32
    ).astype(jnp.bfloat16)
    keys_all, values_all = (
        lax.all_gather(projected[1], "seq", axis=0, tiled=True),
        lax.all_gather(projected[2], "seq", axis=0, tiled=True),
    )
    scores = score_block(projected[0], keys_all, pos_table, one_hot_ids, key_valid)
    row_max = jnp.max(scores, -1, keepdims=True)
    log_total = row_max + jnp.log(jnp.sum(jnp.exp(scores - row_max), -1, keepdims=True))
    probs = jnp.exp(scores - log_total)
    value_heads = values_all.reshape(values_all.shape[0], HEADS, HEAD_DIM)
    attended = jnp.einsum(
        "hsl,lhd->shd", probs.astype(jnp.bfloat16), value_heads, preferred_element_type=jnp.float32
    )
    attended = attended.reshape(row_count, -1).astype(jnp.bfloat16)
    mid_state = joined + project(attended, attn_out)
    normed_mid = rms_norm(mid_state, gain_second.astype(jnp.float32)).astype(jnp.bfloat16)
    gate_up = jnp.einsum("sd,cdf->csf", normed_mid, mlp_in, preferred_element_type=jnp.float32)
    hidden = (jax.nn.gelu(gate_up[0], approximate=True) * gate_up[1]).astype(jnp.bfloat16)
    out_state = mid_state + project(hidden, mlp_out)
    saved = (
        extended,
        mixed,
        joined,
        normed,
        projected,
        keys_all,
        values_all,
        log_total,
        attended,
        mid_state,
        normed_mid,
        gate_up,
        hidden,
    )
    return (out_state, saved)


def gated_unit(gate_in, up_in):
    return jax.nn.gelu(gate_in, approximate=True) * up_in


def layer_backward(grad_out, saved, weights, one_hot_ids, key_valid):
    (
        tap_rows,
        biases,
        join_matrix,
        join_shift,
        gain_first,
        attn_in,
        attn_out,
        pos_table,
        gain_second,
        mlp_in,
        mlp_out,
    ) = weights
    (
        extended,
        mixed,
        joined,
        normed,
        projected,
        keys_all,
        values_all,
        log_total,
        attended,
        mid_state,
        normed_mid,
        gate_up,
        hidden,
    ) = saved
    row_count = grad_out.shape[0]
    model_width = grad_out.shape[1]
    grad_branch = grad_out.astype(jnp.bfloat16)
    grad_mlp_out = project_left(hidden, grad_branch)
    grad_hidden = project_right(grad_branch, mlp_out)
    unused_value, gelu_back = jax.vjp(gated_unit, gate_up[0], gate_up[1])
    grad_gate, grad_up = gelu_back(grad_hidden)
    grad_gate_up = jnp.stack([grad_gate, grad_up]).astype(jnp.bfloat16)
    grad_mlp_in = jnp.einsum(
        "sd,csf->cdf", normed_mid, grad_gate_up, preferred_element_type=jnp.float32
    )
    grad_normed_mid = jnp.einsum(
        "csf,cdf->sd", grad_gate_up, mlp_in, preferred_element_type=jnp.float32
    )
    unused_mid, mid_back = jax.vjp(rms_norm, mid_state, gain_second.astype(jnp.float32))
    grad_mid_part, grad_gain_second = mid_back(grad_normed_mid)
    grad_mid = grad_out + grad_mid_part
    grad_attn = grad_mid.astype(jnp.bfloat16)
    grad_attn_out = project_left(attended, grad_attn)
    grad_attended = (
        project_right(grad_attn, attn_out).astype(jnp.bfloat16).reshape(row_count, HEADS, HEAD_DIM)
    )
    query = projected[0]
    scores = score_block(query, keys_all, pos_table, one_hot_ids, key_valid)
    probs = jnp.exp(scores - log_total)
    value_heads = values_all.reshape(values_all.shape[0], HEADS, HEAD_DIM)
    key_heads = keys_all.reshape(keys_all.shape[0], HEADS, HEAD_DIM)
    query_heads = query.reshape(row_count, HEADS, HEAD_DIM)
    grad_probs = jnp.einsum(
        "shd,lhd->hsl", grad_attended, value_heads, preferred_element_type=jnp.float32
    )
    row_delta = jnp.sum(probs * grad_probs, -1, keepdims=True)
    grad_scores = (probs * (grad_probs - row_delta)).astype(jnp.bfloat16)
    grad_table = jnp.einsum(
        "slb,hsl->bh", one_hot_ids, grad_scores, preferred_element_type=jnp.float32
    ).reshape(-1)
    grad_query = jnp.einsum(
        "hsl,lhd->shd", grad_scores, key_heads, preferred_element_type=jnp.float32
    ).reshape(row_count, -1)
    grad_values_all = jnp.einsum(
        "hsl,shd->lhd",
        probs.astype(jnp.bfloat16),
        grad_attended,
        preferred_element_type=jnp.float32,
    )
    grad_keys_all = jnp.einsum(
        "hsl,shd->lhd", grad_scores, query_heads, preferred_element_type=jnp.float32
    )
    key_total = grad_keys_all.shape[0]
    grad_key, grad_value = (
        lax.psum_scatter(
            grad_keys_all.reshape(key_total, -1).astype(jnp.bfloat16),
            "seq",
            scatter_dimension=0,
            tiled=True,
        ).astype(jnp.float32),
        lax.psum_scatter(
            grad_values_all.reshape(key_total, -1).astype(jnp.bfloat16),
            "seq",
            scatter_dimension=0,
            tiled=True,
        ).astype(jnp.float32),
    )
    grad_projected = jnp.stack([grad_query, grad_key, grad_value]).astype(jnp.bfloat16)
    grad_attn_in = jnp.einsum(
        "sd,csi->cdi", normed, grad_projected, preferred_element_type=jnp.float32
    )
    grad_normed = jnp.einsum(
        "csi,cdi->sd", grad_projected, attn_in, preferred_element_type=jnp.float32
    )
    unused_joined, joined_back = jax.vjp(rms_norm, joined, gain_first.astype(jnp.float32))
    grad_joined_part, grad_gain_first = joined_back(grad_normed)
    grad_joined = grad_mid + grad_joined_part
    grad_join = grad_joined.astype(jnp.bfloat16)
    grad_join_matrix = project_left(mixed, grad_join)
    grad_join_shift = jnp.sum(grad_join.astype(jnp.float32), 0)
    grad_mixed = project_right(grad_join, join_matrix).astype(jnp.bfloat16).astype(jnp.float32)
    grad_biases = jnp.broadcast_to(jnp.sum(grad_mixed, 0), (3, model_width))
    tap_float = tap_rows.astype(jnp.float32)
    grad_taps = [None] * 9
    grad_extended = jnp.zeros((row_count + 3, model_width), jnp.float32)
    for window, offset in windows:
        for tap_index in range(window):
            first_row = 4 - window + tap_index
            grad_taps[offset + tap_index] = jnp.sum(
                grad_mixed * extended[first_row : first_row + row_count], 0
            )
            grad_extended = grad_extended + jnp.pad(
                tap_float[offset + tap_index] * grad_mixed, ((first_row, 3 - first_row), (0, 0))
            )
    back_rows = passed_along(grad_extended[:3], "seq", -1)
    grad_in = grad_joined + grad_extended[3:] + jnp.pad(back_rows, ((row_count - 3, 0), (0, 0)))
    layer_grads = (
        jnp.stack(grad_taps),
        grad_biases,
        grad_join_matrix,
        grad_join_shift,
        grad_gain_first,
        grad_attn_in,
        grad_attn_out,
        grad_table,
        grad_gain_second,
        grad_mlp_in,
        grad_mlp_out,
    )
    return (grad_in, layer_grads)


def body(
    byte_states,
    teacher,
    lengths,
    conv_taps,
    conv_bias,
    join_weight,
    join_bias,
    gain_attn,
    attn_in_weight,
    attn_out_weight,
    position_bias,
    gain_mlp,
    mlp_in_weight,
    mlp_out_weight,
):
    layer_count = conv_taps.shape[0]
    micro_count = byte_states.shape[0]
    row_count = byte_states.shape[2]
    model_width = byte_states.shape[3]
    seq_total = row_count * lax.axis_size("seq")
    positions = lax.axis_index("seq") * row_count + jnp.arange(row_count)
    key_positions = jnp.arange(seq_total)
    bucket_grid = bucket_ids(key_positions[None, :] - positions[:, None])
    one_hot_ids = (bucket_grid[:, :, None] == jnp.arange(BUCKETS)[None, None, :]).astype(
        jnp.bfloat16
    )
    total_valid = lax.psum(jnp.sum(lengths.astype(jnp.float32)), "batch")
    sums = [None] * layer_count
    out_rows = []
    grad_rows = []
    local_squares = jnp.zeros((), jnp.float32)
    for batch_index in range(micro_count):
        state = byte_states[batch_index, 0].astype(jnp.float32)
        length = lengths[batch_index, 0]
        key_valid = key_positions < length
        row_valid = positions < length
        kept = []
        for layer_index in range(layer_count):
            weights = (
                lax.all_gather(conv_taps[layer_index], ("seq", "batch"), axis=1, tiled=True),
                lax.all_gather(conv_bias[layer_index], ("seq", "batch"), axis=1, tiled=True),
                lax.all_gather(join_weight[layer_index], ("seq", "batch"), axis=0, tiled=True),
                lax.all_gather(join_bias[layer_index], ("seq", "batch"), axis=0, tiled=True),
                lax.all_gather(gain_attn[layer_index], ("seq", "batch"), axis=0, tiled=True),
                lax.all_gather(attn_in_weight[layer_index], ("seq", "batch"), axis=1, tiled=True),
                lax.all_gather(attn_out_weight[layer_index], ("seq", "batch"), axis=0, tiled=True),
                lax.all_gather(position_bias[layer_index], ("seq", "batch"), axis=0, tiled=True),
                lax.all_gather(gain_mlp[layer_index], ("seq", "batch"), axis=0, tiled=True),
                lax.all_gather(mlp_in_weight[layer_index], ("seq", "batch"), axis=1, tiled=True),
                lax.all_gather(mlp_out_weight[layer_index], ("seq", "batch"), axis=0, tiled=True),
            )
            state, saved = layer_forward(state, weights, one_hot_ids, key_valid)
            kept.append(saved)
        out_rows.append(state)
        diff = jnp.where(
            row_valid[:, None], state - teacher[batch_index, 0].astype(jnp.float32), 0.0
        )
        local_squares = local_squares + jnp.sum(diff * diff)
        grad_state = 2.0 * diff / (total_valid * model_width)
        for layer_index in reversed(range(layer_count)):
            weights = (
                lax.all_gather(conv_taps[layer_index], ("seq", "batch"), axis=1, tiled=True),
                lax.all_gather(conv_bias[layer_index], ("seq", "batch"), axis=1, tiled=True),
                lax.all_gather(join_weight[layer_index], ("seq", "batch"), axis=0, tiled=True),
                lax.all_gather(join_bias[layer_index], ("seq", "batch"), axis=0, tiled=True),
                lax.all_gather(gain_attn[layer_index], ("seq", "batch"), axis=0, tiled=True),
                lax.all_gather(attn_in_weight[layer_index], ("seq", "batch"), axis=1, tiled=True),
                lax.all_gather(attn_out_weight[layer_index], ("seq", "batch"), axis=0, tiled=True),
                lax.all_gather(position_bias[layer_index], ("seq", "batch"), axis=0, tiled=True),
                lax.all_gather(gain_mlp[layer_index], ("seq", "batch"), axis=0, tiled=True),
                lax.all_gather(mlp_in_weight[layer_index], ("seq", "batch"), axis=1, tiled=True),
                lax.all_gather(mlp_out_weight[layer_index], ("seq", "batch"), axis=0, tiled=True),
            )
            grad_state, layer_grads = layer_backward(
                grad_state, kept[layer_index], weights, one_hot_ids, key_valid
            )
            if sums[layer_index] is None:
                sums[layer_index] = layer_grads
            else:
                sums[layer_index] = jax.tree.map(jnp.add, sums[layer_index], layer_grads)
        grad_rows.append(grad_state)
    loss = lax.psum(local_squares, ("seq", "batch")) / (total_valid * model_width)
    stacked_grads = tuple(
        (
            jnp.stack([sums[layer_index][member] for layer_index in range(layer_count)])
            for member in range(11)
        )
    )
    (
        grad_taps,
        grad_biases,
        grad_join_matrix,
        grad_join_shift,
        grad_gain_first,
        grad_attn_in,
        grad_attn_out,
        grad_table,
        grad_gain_second,
        grad_mlp_in,
        grad_mlp_out,
    ) = stacked_grads
    owned = (
        lax.psum_scatter(grad_taps, ("seq", "batch"), scatter_dimension=2, tiled=True),
        lax.psum_scatter(grad_biases, ("seq", "batch"), scatter_dimension=2, tiled=True),
        lax.psum_scatter(grad_join_matrix, ("seq", "batch"), scatter_dimension=1, tiled=True),
        lax.psum_scatter(grad_join_shift, ("seq", "batch"), scatter_dimension=1, tiled=True),
        lax.psum_scatter(grad_gain_first, ("seq", "batch"), scatter_dimension=1, tiled=True),
        lax.psum_scatter(grad_attn_in, ("seq", "batch"), scatter_dimension=2, tiled=True),
        lax.psum_scatter(grad_attn_out, ("seq", "batch"), scatter_dimension=1, tiled=True),
        lax.psum_scatter(grad_table, ("seq", "batch"), scatter_dimension=1, tiled=True),
        lax.psum_scatter(grad_gain_second, ("seq", "batch"), scatter_dimension=1, tiled=True),
        lax.psum_scatter(grad_mlp_in, ("seq", "batch"), scatter_dimension=2, tiled=True),
        lax.psum_scatter(grad_mlp_out, ("seq", "batch"), scatter_dimension=1, tiled=True),
    )
    activations = jnp.stack(out_rows)[:, None]
    input_grad = jnp.stack(grad_rows)[:, None]
    return (
        activations,
        loss,
        input_grad,
        owned[0],
        owned[1],
        owned[2],
        owned[3],
        owned[4],
        owned[5],
        owned[6],
        owned[7],
        owned[8],
        owned[9],
        owned[10],
    )


ALL = ("seq", "z", "core")
LOW = jnp.bfloat16
WIDE = jnp.float32
BLOCK = 256
SHARE = 16
MASKED = -1e30


def nt(left, right):
    return lax.dot_general(left, right, (((1,), (1,)), ((), ())), preferred_element_type=WIDE)


def nn(left, right):
    return lax.dot_general(left, right, (((1,), (0,)), ((), ())), preferred_element_type=WIDE)


def tn(left, right):
    return lax.dot_general(left, right, (((0,), (0,)), ((), ())), preferred_element_type=WIDE)


def band_kernel(line_ref, band_ref):
    eight = jnp.broadcast_to(line_ref[0], (8, 4 * BLOCK))
    eight = pltpu.roll(eight, 0, 1, stride=1, stride_axis=0)
    for g in range(BLOCK // 8):
        rolled = pltpu.roll(eight, 8 * g, 1) if g else eight
        rows = slice(8 * g, 8 * g + 8)
        band_ref[0, 0, rows] = rolled[:, :BLOCK]
        band_ref[0, 1, rows] = rolled[:, BLOCK : 2 * BLOCK]
        band_ref[0, 2, rows] = rolled[:, 3 * BLOCK :]


def build_band(line):
    return pl.pallas_call(
        band_kernel,
        grid=(HEADS,),
        in_specs=[pl.BlockSpec((1, 1, 4 * BLOCK), lambda h: (h, 0, 0))],
        out_specs=pl.BlockSpec((1, 3, BLOCK, BLOCK), lambda h: (h, 0, 0, 0)),
        out_shape=jax.ShapeDtypeStruct((HEADS, 3, BLOCK, BLOCK), WIDE),
        name="bias_band",
    )(line.reshape(HEADS, 1, 4 * BLOCK))


def key_blocks(core, near):
    near_rows = pl.multiple_of(BLOCK * (1 - core), BLOCK)
    far_rows = pl.multiple_of(BLOCK * core, BLOCK)
    below, above = 1 + core, 2 - core
    if near:
        return near_rows, ((0, near_rows, 0), (0, far_rows, below), (1, far_rows, above), (1, near_rows, None))
    return far_rows, ((0, far_rows, 0), (0, near_rows, above), (1, far_rows, None), (1, near_rows, None))


def keys_with_mask(block, lane, head, first_position, length, constant):
    rows = first_position + lax.broadcasted_iota(jnp.int32, (BLOCK, 1), 0)
    mask = jnp.where(rows < length, 0.0, MASKED)
    spare = (1 - head) * HEAD_DIM
    extra = jnp.where(lane == spare, mask, jnp.where(lane == spare + 1, constant, 0.0))
    return jnp.where(lane // HEAD_DIM == head, block.astype(WIDE), extra).astype(LOW)


def query_with_ones(block, lane, head):
    spare = (1 - head) * HEAD_DIM
    extra = jnp.where((lane == spare) | (lane == spare + 1), 1.0, 0.0)
    return jnp.where(lane // HEAD_DIM == head, block.astype(WIDE), extra).astype(LOW)


def only_head(block, lane, head):
    return jnp.where(lane // HEAD_DIM == head, block.astype(WIDE), 0.0).astype(LOW)


def attend_kernel(
    info_ref, far_ref, q_ref, k_ref, v_ref, ko_ref, vo_ref, band_ref, out_ref, lse_ref, score_ref
):
    core, length = info_ref[0], info_ref[1]
    pair = pl.program_id(0)
    lane = lax.broadcasted_iota(jnp.int32, (1, 2 * HEAD_DIM), 1)
    for n in range(2):
        q_rows, blocks = key_blocks(core, n == 0)
        query = q_ref[pl.ds(q_rows, BLOCK), :]
        halves = []
        for head in range(2):
            q_low = query_with_ones(query, lane, head)
            top = None
            for b, (side, start, slot) in enumerate(blocks):
                first = 2 * BLOCK * (core if side == 0 else 1 - core) + start
                keys = (k_ref, ko_ref)[side][pl.ds(start, BLOCK), :]
                constant = far_ref[2 * pair + head] if slot is None else 0.0
                scores = nt(keys_with_mask(keys, lane, head, first, length, constant), q_low)
                if slot is not None:
                    scores = scores + band_ref[head, slot]
                score_ref[b] = scores
                block_top = jnp.max(scores, 0, keepdims=True)
                top = block_top if top is None else jnp.maximum(top, block_top)
            total = jnp.zeros((1, BLOCK), WIDE)
            mixed = jnp.zeros((2 * HEAD_DIM, BLOCK), WIDE)
            for b, (side, start, slot) in enumerate(blocks):
                weights = jnp.exp(score_ref[b] - top)
                total = total + jnp.sum(weights, 0, keepdims=True)
                values = (v_ref, vo_ref)[side][pl.ds(start, BLOCK), :]
                mixed = mixed + tn(values, weights.astype(LOW))
            lse_ref[0, n, head : head + 1, :] = top + jnp.log(total)
            halves.append((mixed / total)[head * HEAD_DIM : (head + 1) * HEAD_DIM])
        out_ref[pl.ds(q_rows, BLOCK), :] = jnp.transpose(jnp.concatenate(halves, 0)).astype(LOW)


def attend(info, far, projected, others, band):
    query, own_kv = projected
    rows = query.shape[0]
    pairs = HEADS // 2
    width = 2 * HEAD_DIM
    col = lambda shift: pl.BlockSpec((rows, width), lambda p: (0, p + shift))
    return pl.pallas_call(
        attend_kernel,
        grid=(pairs,),
        in_specs=[
            pl.BlockSpec(memory_space=pltpu.SMEM),
            pl.BlockSpec(memory_space=pltpu.SMEM),
            col(0),
            col(0),
            col(pairs),
            col(0),
            col(pairs),
            pl.BlockSpec((2, 3, BLOCK, BLOCK), lambda p: (p, 0, 0, 0)),
        ],
        out_specs=[col(0), pl.BlockSpec((1, 2, 2, BLOCK), lambda p: (p, 0, 0, 0))],
        out_shape=[
            jax.ShapeDtypeStruct((rows, HEADS * HEAD_DIM), LOW),
            jax.ShapeDtypeStruct((pairs, 2, 2, BLOCK), WIDE),
        ],
        scratch_shapes=[pltpu.VMEM((4, BLOCK, BLOCK), WIDE)],
        name="attend",
    )(info, far, query, own_kv, own_kv, others, others, band)


def attend_back_kernel(
    info_ref,
    far_ref,
    q_ref,
    k_ref,
    v_ref,
    ko_ref,
    vo_ref,
    band_ref,
    out_ref,
    gout_ref,
    lse_ref,
    *refs,
):
    gq_ref, gown_ref, goth_ref, gband_ref, gfar_ref, gk_acc, gv_acc, band_acc, far_acc = refs[-9:]
    core, length, first_pair = info_ref[0], info_ref[1], info_ref[2]
    pair = first_pair + pl.program_id(0)
    width = 2 * HEAD_DIM
    lane = lax.broadcasted_iota(jnp.int32, (1, width), 1)
    gk_acc[...] = jnp.zeros_like(gk_acc)
    gv_acc[...] = jnp.zeros_like(gv_acc)
    band_acc[...] = jnp.zeros_like(band_acc)
    far_acc[...] = jnp.zeros_like(far_acc)
    select = jnp.where(
        lax.broadcasted_iota(jnp.int32, (8, width), 0)
        == lax.broadcasted_iota(jnp.int32, (8, width), 1) // HEAD_DIM,
        1.0,
        0.0,
    )
    for n in range(2):
        q_rows, blocks = key_blocks(core, n == 0)
        query = q_ref[pl.ds(q_rows, BLOCK), :]
        gout = gout_ref[pl.ds(q_rows, BLOCK), :]
        dots = gout.astype(WIDE) * out_ref[pl.ds(q_rows, BLOCK), :].astype(WIDE)
        deltas = lax.dot_general(
            select,
            dots,
            (((1,), (1,)), ((), ())),
            precision=lax.Precision.HIGHEST,
            preferred_element_type=WIDE,
        )
        halves = []
        for head in range(2):
            q_ones = query_with_ones(query, lane, head)
            q_low = only_head(query, lane, head)
            g_low = only_head(gout, lane, head)
            lse = lse_ref[0, n, head : head + 1, :]
            delta = deltas[head : head + 1]
            gq = jnp.zeros((width, BLOCK), WIDE)
            for side, start, slot in blocks:
                first = 2 * BLOCK * (core if side == 0 else 1 - core) + start
                keys = (k_ref, ko_ref)[side][pl.ds(start, BLOCK), :]
                values = (v_ref, vo_ref)[side][pl.ds(start, BLOCK), :]
                constant = far_ref[2 * pair + head] if slot is None else 0.0
                scores = nt(keys_with_mask(keys, lane, head, first, length, constant), q_ones)
                if slot is not None:
                    scores = scores + band_ref[head, slot]
                probs = jnp.exp(scores - lse)
                gprobs = nt(values, g_low)
                gscores = probs * (gprobs - delta)
                if slot is None:
                    part = jnp.sum(gscores.reshape(BLOCK // 8, 8, BLOCK), 0)
                    far_acc[head] = far_acc[head] + part
                else:
                    band_acc[head, slot] = band_acc[head, slot] + gscores
                gs_low = gscores.astype(LOW)
                at = pl.ds(2 * BLOCK * side + start, BLOCK)
                gv_acc[at, :] = gv_acc[at, :] + nn(probs.astype(LOW), g_low)
                gk_acc[at, :] = gk_acc[at, :] + nn(gs_low, q_low)
                gq = gq + tn(keys, gs_low)
            halves.append(gq[head * HEAD_DIM : (head + 1) * HEAD_DIM])
        gq_ref[pl.ds(q_rows, BLOCK), :] = jnp.transpose(jnp.concatenate(halves, 0)).astype(LOW)
    own = 2 * BLOCK
    gown_ref[0] = gk_acc[:own, :]
    gown_ref[1] = gv_acc[:own, :]
    goth_ref[0] = gk_acc[own:, :].astype(LOW)
    goth_ref[1] = gv_acc[own:, :].astype(LOW)
    span = 4 * BLOCK
    gap = jnp.zeros((8, BLOCK), WIDE)
    row = lax.broadcasted_iota(jnp.int32, (8, span), 0)
    for head in range(2):
        lines = jnp.zeros((8, span), WIDE)
        for g in range(BLOCK // 8):
            rows = slice(8 * g, 8 * g + 8)
            piece = jnp.concatenate(
                [band_acc[head, 0, rows], band_acc[head, 1, rows], gap, band_acc[head, 2, rows]], 1
            )
            lines = lines + (pltpu.roll(piece, span - 8 * g, 1) if g else piece)
        for bit in (1, 2, 4):
            lines = jnp.where((row & bit) != 0, pltpu.roll(lines, span - bit, 1), lines)
        gband_ref[0, head : head + 1, :] = jnp.sum(lines, 0, keepdims=True)
        gfar_ref[0, head : head + 1, :] = jnp.sum(far_acc[head], 0, keepdims=True)


def attend_back(info, far, projected, others, band, out, gout, lse, first, count, before=()):
    query, own_kv = projected
    rows = query.shape[0]
    pairs = HEADS // 2
    width = 2 * HEAD_DIM
    inner = HEADS * HEAD_DIM
    col = lambda shift: pl.BlockSpec((rows, width), lambda p: (0, first + p + shift))
    two = pl.BlockSpec((2, rows, width), lambda p: (0, 0, first + p))
    some = lambda *block: pl.BlockSpec(block, lambda p: (first + p,) + (0,) * (len(block) - 1))
    info = jnp.concatenate([info, jnp.full((1,), first, jnp.int32)])
    return pl.pallas_call(
        attend_back_kernel,
        grid=(count,),
        in_specs=[
            pl.BlockSpec(memory_space=pltpu.SMEM),
            pl.BlockSpec(memory_space=pltpu.SMEM),
            col(0),
            col(0),
            col(pairs),
            col(0),
            col(pairs),
            some(2, 3, BLOCK, BLOCK),
            col(0),
            col(0),
            some(1, 2, 2, BLOCK),
        ]
        + [pl.BlockSpec(memory_space=pl.ANY)] * len(before),
        out_specs=[col(0), two, two, some(1, 2, 4 * BLOCK), some(1, 2, BLOCK)],
        out_shape=[
            jax.ShapeDtypeStruct((rows, inner), LOW),
            jax.ShapeDtypeStruct((2, rows, inner), WIDE),
            jax.ShapeDtypeStruct((2, rows, inner), LOW),
            jax.ShapeDtypeStruct((pairs, 2, 4 * BLOCK), WIDE),
            jax.ShapeDtypeStruct((pairs, 2, BLOCK), WIDE),
        ],
        input_output_aliases={11 + at: at for at in range(len(before))},
        scratch_shapes=[
            pltpu.VMEM((4 * BLOCK, width), WIDE),
            pltpu.VMEM((4 * BLOCK, width), WIDE),
            pltpu.VMEM((2, 3, BLOCK, BLOCK), WIDE),
            pltpu.VMEM((2, 8, BLOCK), WIDE),
        ],
        name="attend_back",
    )(info, far, query, own_kv, own_kv, others, others, band, out, gout, lse, *before)


def store_terms(core, terms, kept_ref, sent_ref, at):
    for own in range(2):

        @pl.when(core == own)
        def _(own=own):
            kept_ref[at] = terms[:, own].astype(LOW)
            sent_ref[at] = terms[:, 1 - own].astype(LOW)


def unit_rows(values):
    inverse = lax.rsqrt(jnp.mean(values * values, -1, keepdims=True) + eps)
    return values * inverse, inverse


def normed(values, gain):
    return (unit_rows(values)[0] * gain).astype(LOW)


def normed_back(grad, values, gain):
    unit, inverse = unit_rows(values)
    scaled = grad * gain
    grad_in = inverse * (scaled - unit * jnp.mean(scaled * unit, -1, keepdims=True))
    return grad_in, jnp.sum(grad * unit, 0, keepdims=True)


def outward_chunk(block, share, width):
    owners = block.shape[0] // share
    parts = [
        block[:, at * width : (at + 1) * width].reshape(owners, 1, share, width)
        for at in range(block.shape[1] // width)
    ]
    return jnp.concatenate(parts, 1).reshape(-1, width)


ROOT = 0.7978845608028654
CUBIC = 0.044715


def mlp_kernel(att_ref, joined_ref, gain_ref, ao_ref, gate_ref, up_ref, out_ref, mid_ref, norm_ref, state_ref):
    width = att_ref.shape[1]

    @pl.when(pl.program_id(0) == 0)
    def _():
        mid = joined_ref[...] + nn(att_ref[...], ao_ref[...])
        mid_ref[...] = mid
        norm_ref[...] = normed(mid, gain_ref[...])
        state_ref[...] = mid

    norm = norm_ref[...]
    gate = nn(norm, gate_ref[...])
    turn = jnp.tanh(ROOT * (gate + CUBIC * gate * gate * gate))
    hidden = 0.5 * gate * (1.0 + turn) * nn(norm, up_ref[...])
    outward = outward_chunk(out_ref[...], SHARE, width)
    state_ref[...] += nn(hidden.astype(LOW), outward)


def rest_specs(width, quarters, layers, l):
    start = layers * quarters + l * (2 * quarters + 1)
    column = lambda first, moves: pl.BlockSpec(
        (width, width), lambda j: (0, start + first + j) if moves else (0, start + first)
    )
    return [
        column(0, False),
        column(1, True),
        column(1 + quarters, True),
        pl.BlockSpec((width // quarters, quarters * width), lambda j: (j, l)),
    ]


def mlp_forward(attended, joined, gain, rest, quarters, layers, l):
    rows, width = joined.shape
    whole = pl.BlockSpec((rows, width), lambda j: (0, 0))
    return pl.pallas_call(
        mlp_kernel,
        grid=(quarters,),
        in_specs=[whole, whole, pl.BlockSpec((1, width), lambda j: (0, 0))]
        + rest_specs(width, quarters, layers, l),
        out_specs=[whole] * 3,
        out_shape=[
            jax.ShapeDtypeStruct((rows, width), WIDE),
            jax.ShapeDtypeStruct((rows, width), LOW),
            jax.ShapeDtypeStruct((rows, width), WIDE),
        ],
        name="mlp",
    )(attended, joined, gain.reshape(1, width), rest, rest, rest, rest)


def mlp_back_kernel(
    info_ref,
    grad_ref,
    norm_ref,
    mid_ref,
    gain_ref,
    ao_ref,
    gate_ref,
    up_ref,
    out_ref,
    gmid_ref,
    gmid_low_ref,
    gatt_ref,
    ggain_ref,
    kept_ref,
    sent_ref,
    turned_ref,
    low_ref,
    gnorm_ref,
):
    core = info_ref[0]
    step = pl.program_id(0)
    owners, blocks, share, width = kept_ref.shape
    quarters = blocks // 3

    @pl.when(step == 0)
    def _():
        turned_ref[...] = jnp.transpose(norm_ref[...])
        low_ref[...] = grad_ref[...].astype(LOW)
        gnorm_ref[...] = jnp.zeros_like(gnorm_ref)

    norm, low = norm_ref[...], low_ref[...]
    gate, up = nn(norm, gate_ref[...]), nn(norm, up_ref[...])
    square = gate * gate
    turn = jnp.tanh(ROOT * gate * (1.0 + CUBIC * square))
    half = 0.5 * (1.0 + turn)
    slope = half + 0.5 * ROOT * gate * (1.0 - turn * turn) * (1.0 + 3.0 * CUBIC * square)
    bent = half * gate
    g_hidden = nt(low, outward_chunk(out_ref[...], share, width))
    g_gate = (g_hidden * up * slope).astype(LOW)
    g_up = (g_hidden * bent).astype(LOW)
    hidden = (bent * up).astype(LOW)
    every = slice(None)
    for at, part in ((step, g_gate), (step + quarters, g_up)):
        terms = nn(turned_ref[...], part).reshape(owners, 2, share, width)
        store_terms(core, terms, kept_ref, sent_ref, (every, at))
    few = owners // quarters
    terms = tn(hidden, low).reshape(few, 2, quarters, share, width)
    at = (pl.ds(step * few, few), slice(2 * quarters, blocks))
    store_terms(core, terms, kept_ref, sent_ref, at)
    gnorm_ref[...] += nt(g_gate, gate_ref[...]) + nt(g_up, up_ref[...])

    @pl.when(step == quarters - 1)
    def _():
        part, ggain_ref[...] = normed_back(gnorm_ref[...], mid_ref[...], gain_ref[...])
        g_mid = grad_ref[...] + part
        gmid_ref[...] = g_mid
        g_low = g_mid.astype(LOW)
        gmid_low_ref[...] = g_low
        gatt_ref[...] = nt(g_low, ao_ref[...]).astype(LOW)


def mlp_back(info, grad, norm, mid, gain, rest, quarters, layers, l, owners, share):
    rows, width = grad.shape
    shape = jax.ShapeDtypeStruct((owners, 3 * quarters, share, width), LOW)
    whole = pl.BlockSpec((rows, width), lambda j: (0, 0))
    line = pl.BlockSpec((1, width), lambda j: (0, 0))
    out = pl.BlockSpec(shape.shape, lambda j: (0, 0, 0, 0))
    return pl.pallas_call(
        mlp_back_kernel,
        grid=(quarters,),
        in_specs=[pl.BlockSpec(memory_space=pltpu.SMEM), whole, whole, whole, line]
        + rest_specs(width, quarters, layers, l),
        out_specs=[whole, whole, whole, line, out, out],
        out_shape=[
            jax.ShapeDtypeStruct((rows, width), WIDE),
            jax.ShapeDtypeStruct((rows, width), LOW),
            jax.ShapeDtypeStruct((rows, width), LOW),
            jax.ShapeDtypeStruct((1, width), WIDE),
            shape,
            shape,
        ],
        scratch_shapes=[
            pltpu.VMEM((width, rows), LOW),
            pltpu.VMEM((rows, width), LOW),
            pltpu.VMEM((rows, width), WIDE),
        ],
        name="mlp_back",
    )(info, grad, norm, mid, gain.reshape(1, width), rest, rest, rest, rest)


def attn_terms_kernel(
    info_ref,
    mixed_ref,
    gjoin_ref,
    norm_ref,
    gquery_ref,
    gkv_ref,
    att_ref,
    gmid_ref,
    small_ref,
    kept_ref,
    sent_ref,
):
    core = info_ref[0]
    owners, blocks, share, width = kept_ref.shape

    def put(at, turned, right):
        terms = nn(turned, right).reshape(owners, 2, share, width)
        store_terms(core, terms, kept_ref, sent_ref, (slice(None), at))

    put(0, jnp.transpose(mixed_ref[...]), gjoin_ref[...])
    turned = jnp.transpose(norm_ref[...])
    put(1, turned, gquery_ref[...])
    put(2, turned, gkv_ref[0])
    put(3, turned, gkv_ref[1])
    put(4, jnp.transpose(att_ref[...]), gmid_ref[...])
    small = jnp.broadcast_to(small_ref[...].astype(LOW)[None], (owners, share, width))
    kept_ref[:, 5] = small
    sent_ref[:, 5] = small


def attn_terms(info, mixed, gjoin, norm, gquery, gkv, att, gmid, small, owners, share):
    width = mixed.shape[1]
    shape = jax.ShapeDtypeStruct((owners, 6, share, width), LOW)
    vmem = pl.BlockSpec(memory_space=pltpu.VMEM)
    return pl.pallas_call(
        attn_terms_kernel,
        in_specs=[pl.BlockSpec(memory_space=pltpu.SMEM)] + [vmem] * 8,
        out_specs=[vmem, vmem],
        out_shape=[shape, shape],
        name="attn_terms",
    )(info, mixed, gjoin, norm, gquery, gkv, att, gmid, small)


def pack_kernel(
    info_ref,
    lengths_ref,
    taps_ref,
    bias_ref,
    join_ref,
    join_bias_ref,
    gain_attn_ref,
    attn_in_ref,
    attn_out_ref,
    position_ref,
    gain_mlp_ref,
    mlp_in_ref,
    mlp_out_ref,
    *refs,
):
    small_ref = refs[-1]
    device = info_ref[0]
    layers, share, width = join_ref.shape
    lane = lax.broadcasted_iota(jnp.int32, (share, width), 1)
    item = lax.broadcasted_iota(jnp.int32, (share, width), 0)
    spread = jnp.where(lane == device * share + item, 1.0, 0.0).astype(LOW)
    place = lane[:1] - device * share - HEADS
    extra = jnp.zeros((1, width), WIDE)
    for m in range(lengths_ref.shape[0]):
        whole, rest = lengths_ref[m] // 32, lengths_ref[m] % 32
        extra = extra + jnp.where(place == 2 * m, whole, jnp.where(place == 2 * m + 1, rest, 0)).astype(WIDE)
    for l in range(layers):
        small_ref[0:9] = nn(taps_ref[:, l], spread)
        small_ref[9:12] = nn(bias_ref[:, l], spread)
        small_ref[12:13] = nn(join_bias_ref[l : l + 1], spread)
        small_ref[13:14] = nn(gain_attn_ref[l : l + 1], spread)
        small_ref[14:15] = nn(gain_mlp_ref[l : l + 1], spread)
        small_ref[15:16] = nn(position_ref[l : l + 1], spread[:HEADS]) + extra
        first = [join_ref[l]] + [attn_in_ref[l, c] for c in range(3)] + [small_ref[...].astype(LOW)]
        outward = [mlp_out_ref[l, a * share : (a + 1) * share] for a in range(mlp_out_ref.shape[1] // share)]
        inward = [attn_out_ref[l], mlp_in_ref[l, 0], mlp_in_ref[l, 1]]
        out_width = mlp_out_ref.shape[1] // share * width
        in_width = width + 2 * mlp_in_ref.shape[3]
        places = (
            (refs[l], 0, first),
            (refs[layers], l * out_width, outward),
            (refs[layers], layers * out_width + l * in_width, inward),
        )
        for out_ref, cursor, pieces in places:
            for piece in pieces:
                out_ref[:, cursor : cursor + piece.shape[1]] = piece
                cursor += piece.shape[1]


def pack(info, lengths, arrays, share):
    layers, width = arrays[2].shape[0], arrays[2].shape[2]
    quarters = arrays[-2].shape[3] // width
    first, rest = 5 * width, (1 + 3 * quarters) * width
    smem = pl.BlockSpec(memory_space=pltpu.SMEM)
    vmem = pl.BlockSpec(memory_space=pltpu.VMEM)
    return pl.pallas_call(
        pack_kernel,
        in_specs=[smem, smem] + [vmem] * len(arrays),
        out_specs=[vmem] * (layers + 1),
        out_shape=[
            jax.ShapeDtypeStruct((share, span), LOW) for span in [first] * layers + [layers * rest]
        ],
        scratch_shapes=[pltpu.VMEM((share, width), WIDE)],
        name="pack",
    )(info, lengths, *arrays)


def collected_kernel(device_ref, inverse_ref, *refs):
    device = device_ref[0]
    inputs, outputs = refs[:16], refs[16:]
    join_ref, attn_in_ref, attn_out_ref, mlp_in_ref, mlp_out_ref, loss_ref = outputs[:6]
    taps_ref, bias_ref, join_bias_ref, gain_attn_ref, gain_mlp_ref, position_ref = outputs[6:]
    share, width = join_ref.shape[1:]
    quarters = mlp_in_ref.shape[3] // width
    lane = lax.broadcasted_iota(jnp.int32, (share, width), 1)
    item = lax.broadcasted_iota(jnp.int32, (share, width), 0)
    own = jnp.where(lane == device * share + item, 1.0, 0.0)

    def total(pieces, at):
        return sum(piece[at].astype(WIDE) for piece in pieces)

    for l in range(2):
        mlp, attn = inputs[8 * l : 8 * l + 4], inputs[8 * l + 4 : 8 * l + 8]
        join_ref[l] = total(attn, 0)
        for c in range(3):
            attn_in_ref[l, c] = total(attn, 1 + c)
        attn_out_ref[l] = total(attn, 4)
        for c in range(2):
            for a in range(quarters):
                mlp_in_ref[l, c, :, a * width : (a + 1) * width] = total(mlp, c * quarters + a)
        for a in range(quarters):
            mlp_out_ref[l, a * share : (a + 1) * share] = total(mlp, 2 * quarters + a)
        small = total(attn, 5)
        small_own = lax.dot_general(
            small,
            own,
            (((1,), (1,)), ((), ())),
            precision=lax.Precision.HIGHEST,
            preferred_element_type=WIDE,
        )
        line = slice(l, l + 1)
        for at, tap in enumerate((2, 3, 1, 2, 3, 0, 1, 2, 3)):
            taps_ref[at, line] = small_own[tap : tap + 1]
        for at in range(3):
            bias_ref[at, line] = small_own[4:5]
        for at, out_ref in enumerate((join_bias_ref, gain_attn_ref, gain_mlp_ref)):
            out_ref[line] = small_own[5 + at : 6 + at]
        position_ref[line] = small_own[8:9, :HEADS]
        if l == 1:
            loss_ref[...] = jnp.sum(small[9:10], 1, keepdims=True) * inverse_ref[0]


def collected(device, inverse, layers, quarters):
    pieces = [piece for mlp, attn in layers for piece in list(mlp) + list(attn)]
    share, width = pieces[0].shape[1:]
    count = len(layers)
    shapes = [
        (count, share, width),
        (count, 3, share, width),
        (count, share, width),
        (count, 2, share, quarters * width),
        (count, quarters * share, width),
        (1, 1),
        (9, count, share),
        (3, count, share),
        (count, share),
        (count, share),
        (count, share),
        (count, HEADS),
    ]
    vmem = pl.BlockSpec(memory_space=pltpu.VMEM)
    return pl.pallas_call(
        collected_kernel,
        in_specs=[pl.BlockSpec(memory_space=pltpu.SMEM)] * 2 + [vmem] * len(pieces),
        out_specs=[vmem] * len(shapes),
        out_shape=[jax.ShapeDtypeStruct(shape, WIDE) for shape in shapes],
        name="collected",
    )(device, inverse, *pieces)


def tie(*values):
    return lax.optimization_barrier(values)


def chip_body(
    byte_states,
    teacher,
    lengths,
    conv_taps,
    conv_bias,
    join_weight,
    join_bias,
    gain_attn,
    attn_in_weight,
    attn_out_weight,
    position_bias,
    gain_mlp,
    mlp_in_weight,
    mlp_out_weight,
):
    layer_count = conv_taps.shape[0]
    model_width = byte_states.shape[3]
    slot_rows = byte_states.shape[2]
    rows = 2 * slot_rows
    hidden_width = mlp_in_weight.shape[3]
    quarters = hidden_width // model_width
    seqs, zs, cores = (lax.axis_size(name) for name in ALL)
    devices = seqs * zs * cores
    share = SHARE
    s_at, z_at, c_at = (lax.axis_index(name) for name in ALL)
    device_at = (s_at * zs + z_at) * cores + c_at

    def number(s, z, c):
        return (s * zs + z) * cores + c

    places = [(s, z, c) for s in range(seqs) for z in range(zs) for c in range(cores)]
    swap = [(number(s, z, c), number(s, z, 1 - c)) for s, z, c in places]
    routes = [
        [(number(s, z, c), number(2 * (s % 2 if turn == 0 else 1 - s % 2) + c, z, s // 2)) for s, z, c in places]
        for turn in range(2)
    ]
    back_routes = [[(b, a) for a, b in route] for route in routes]

    def to_chips(block):
        odd, high = s_at % 2, s_at // 2
        first, second = (
            lax.ppermute(jnp.where(odd == turn, block[0], block[1]), ALL, routes[turn]) for turn in range(2)
        )
        return jnp.concatenate(
            [jnp.where(high == 0, first, second), jnp.where(high == 0, second, first)], 0
        )

    def leave(block):
        high = s_at // 2
        halves = (block[:slot_rows], block[slot_rows:])
        return [
            lax.ppermute(jnp.where(high == turn, halves[0], halves[1]), ALL, back_routes[turn])
            for turn in range(2)
        ]

    def arrive(pieces):
        first, second = pieces
        odd = s_at % 2
        whole = jnp.stack([jnp.where(odd == 0, first, second), jnp.where(odd == 0, second, first)])
        return whole.astype(WIDE)[:, None]

    def trade(block):
        return lax.ppermute(block, ALL, swap)

    to_high = [(number(s, z, 0), number(s, z, 1)) for s, z, c in places if c == 0]
    to_low = [(b, a) for a, b in to_high]

    lanes = jnp.arange(model_width)
    lane_owner, lane_item = lanes // share, lanes % share
    every_layer = range(layer_count)
    packed = pack(
        device_at.astype(jnp.int32).reshape(1),
        lengths.reshape(-1),
        (
            conv_taps.transpose(1, 0, 2),
            conv_bias.transpose(1, 0, 2),
            join_weight,
            join_bias,
            gain_attn,
            attn_in_weight,
            attn_out_weight,
            position_bias,
            gain_mlp,
            mlp_in_weight,
            mlp_out_weight,
        ),
        share,
    )

    def moved(block, name, change):
        def target(s, z, c):
            return number(s ^ change, z, c) if name == "seq" else number(s, z ^ change, c)

        return lax.ppermute(block, ALL, [(number(s, z, c), target(s, z, c)) for s, z, c in places])

    def spread_out(block, name, at, size):
        whole = jnp.zeros((size,) + block.shape, block.dtype)
        pieces = [block] + [moved(block, name, change) for change in range(1, size)]
        for change, piece in enumerate(pieces):
            whole = lax.dynamic_update_index_in_dim(whole, piece, at ^ change, 0)
        return whole

    def pair_up(block):
        other = trade(block)
        return jnp.stack(
            [jnp.where(c_at == 0, block, other), jnp.where(c_at == 0, other, block)], 2
        ).reshape(model_width, -1)

    def split_halves(kept, arrived):
        shape = (seqs, zs) + kept.shape[1:]
        return kept.reshape(shape), arrived.reshape(shape)

    def plane_terms(kept, arrived):
        kept, arrived = split_halves(kept, arrived)
        pick = lambda whole, s: lax.dynamic_index_in_dim(whole, s, 0, False).astype(WIDE)
        return [
            (pick(kept, s_at ^ change) + pick(arrived, s_at ^ change)).astype(LOW)
            for change in range(seqs)
        ]

    def line_terms(pieces):
        total = finish(pieces).astype(LOW)
        return [lax.dynamic_index_in_dim(total, z_at ^ change, 0, False) for change in range(zs)]

    def send(name, terms):
        return [moved(part, name, change) if change else part for change, part in enumerate(terms)]

    def finish(pieces):
        return sum(piece.astype(WIDE) for piece in pieces)

    early, behind = spread_out(packed[0], "z", z_at, zs), packed[1]
    early = spread_out(early, "seq", s_at, seqs)
    early, behind = tie(early, behind)
    early = [pair_up(early), spread_out(spread_out(behind, "z", z_at, zs), "seq", s_at, seqs)]
    later = lax.all_gather(packed[2], ALL, axis=0, tiled=True)

    def unpack_first(first):
        small = jnp.sum(first[:, 4 * model_width :].reshape(devices, share, model_width).astype(WIDE), 0)
        return dict(
            join=first[:, :model_width],
            attn_in=first[:, model_width : 4 * model_width],
            taps=jnp.stack(
                [
                    small[5],
                    small[2] + small[6],
                    small[0] + small[3] + small[7],
                    small[1] + small[4] + small[8],
                ]
            ),
            bias=small[9] + small[10] + small[11],
            join_bias=small[12],
            gain_attn=small[13],
            gain_mlp=small[14],
            last=small[15],
        )

    weights = [unpack_first(early[0])]
    state = to_chips(byte_states[:, 0]).astype(WIDE)

    counts = weights[0]["last"]
    scale = jnp.where((lane_item >= HEADS) & (lane_item < HEADS + 4), jnp.where(lane_item % 2 == 0, 32.0, 1.0), 0.0)
    total_valid = jnp.sum(jnp.where(lane_owner < zs * cores, counts * scale, 0.0))
    mine = (lane_owner == z_at * cores + s_at % 2) & ((lane_item - HEADS) // 2 == s_at // 2)
    length = jnp.sum(jnp.where(mine, counts * scale, 0.0)).astype(jnp.int32)
    info = jnp.stack([c_at.astype(jnp.int32), length])
    row_valid = (rows * c_at + jnp.arange(rows) < length)[:, None]

    offsets = -((jnp.arange(4 * BLOCK) + 2 * BLOCK) % (4 * BLOCK) - 2 * BLOCK)
    in_bucket = (lane_owner[:, None] == bucket_ids(offsets)[None, :]).astype(LOW)
    of_head = (lane_item[None, :] == jnp.arange(HEADS)[:, None]).astype(WIDE)
    far_bucket = (lane_owner == jnp.where(c_at == 0, 31, 15)).astype(WIDE)

    def bias_of(last):
        line = jnp.dot((of_head * last).astype(LOW), in_bucket, preferred_element_type=WIDE)
        return jnp.sum(of_head * (last * far_bucket), 1), build_band(line)

    biases = [bias_of(weights[0]["last"])]
    kept = []
    for l in range(layer_count):
        w = weights[l]
        low_state = state.astype(LOW)
        prior = lax.ppermute(low_state[rows - 8 :], ALL, to_high)[5:]
        extended = jnp.concatenate([prior, low_state], 0).astype(WIDE)
        mixed = w["bias"] + sum(w["taps"][k] * extended[k : k + rows] for k in range(4))
        mixed = mixed.astype(LOW)
        joined = state + nn(mixed, w["join"]) + w["join_bias"]
        norm_a = normed(joined, w["gain_attn"])
        inner = HEADS * HEAD_DIM
        own = nn(norm_a, w["attn_in"][:, inner:]).astype(LOW)
        others = trade(own)
        projected = (nn(norm_a, w["attn_in"][:, :inner]).astype(LOW), own)
        far, band = biases[l]
        attended, lse = attend(info, far, projected, others, band)
        if l + 1 < layer_count:
            attended, lse, early[l + 1] = tie(attended, lse, early[l + 1])
            weights.append(unpack_first(pair_up(early[l + 1])))
            biases.append(bias_of(weights[l + 1]["last"]))
            attended, lse, later, biases[l + 1], weights[l + 1], teacher = tie(
                attended, lse, later, biases[l + 1], weights[l + 1], teacher
            )
        mid, norm_m, state = mlp_forward(attended, joined, w["gain_mlp"], later, quarters, layer_count, l)
        if l == 0:
            state, target = tie(state, to_chips(teacher[:, 0]))
        kept.append(
            (extended, mixed, joined, norm_a, projected, others, far, band, attended, lse, mid, norm_m)
        )

    activations = leave(state)
    diff = jnp.where(row_valid, state - target.astype(WIDE), 0.0)
    squares = jnp.sum(diff * diff, 0)
    grad = 2.0 * diff / (total_valid * model_width)
    owners = seqs * zs
    mlp_way = attn_way = None
    for l in reversed(every_layer):
        w = weights[l]
        (extended, mixed, joined, norm_a, projected, others, far, band, attended, lse, mid, norm_m) = kept[l]
        g_mid, g_mid_low, g_att, g_gain_mlp, mlp_kept, mlp_sent = mlp_back(
            info, grad, norm_m, mid, w["gain_mlp"], later, quarters, layer_count, l, owners, share
        )
        if mlp_way is None:
            g_att, mlp_kept, mlp_sent, activations = tie(g_att, mlp_kept, mlp_sent, activations)
        else:
            g_att, mlp_kept, mlp_sent, mlp_way, attn_way = tie(
                g_att, mlp_kept, mlp_sent, mlp_way, attn_way
            )
            line = line_terms(attn_way)
            g_att, line = tie(g_att, line)
            attn_way = send("z", line)
        mlp_half = (mlp_kept, trade(mlp_sent))
        attention = (info, far, projected, others, band, attended, g_att, lse)
        back = attend_back(*attention, 0, 1)
        back, mlp_half = tie(back, mlp_half)
        plane = plane_terms(*mlp_half)
        back, plane = tie(back, plane)
        mlp_half = send("seq", plane)
        back = attend_back(*attention, 1, HEADS // 2 - 1, back)
        mlp_near = mlp_half[: seqs - 1]
        back, mlp_near = tie(back, mlp_near)
        mlp_half = mlp_near + mlp_half[seqs - 1 :]
        g_query, g_own, g_other, g_band, g_far = back
        g_kv = (g_own + trade(g_other).astype(WIDE)).astype(LOW)
        g_norm = sum(
            nt(part, w["attn_in"][:, c * model_width : (c + 1) * model_width])
            for c, part in enumerate((g_query, g_kv[0], g_kv[1]))
        )
        g_joined, g_gain_attn = normed_back(g_norm, joined, w["gain_attn"])
        g_joined = g_mid + g_joined
        g_join_low = g_joined.astype(LOW)
        g_join_bias = jnp.sum(g_join_low.astype(WIDE), 0)
        g_mixed = nt(g_join_low, w["join"]).astype(LOW).astype(WIDE)
        g_taps = [jnp.sum(g_mixed * extended[k : k + rows], 0) for k in range(4)]
        g_bias = jnp.sum(g_mixed, 0)
        head_rows = [
            sum(w["taps"][k] * g_mixed[r - k : r - k + 1] for k in range(r + 1)) for r in range(3)
        ]
        beyond = lax.ppermute(
            jnp.concatenate(head_rows + [jnp.zeros((5, model_width), WIDE)], 0), ALL, to_low
        )
        padded = jnp.concatenate([g_mixed, jnp.zeros((3, model_width), WIDE)], 0)
        g_state = sum(w["taps"][k] * padded[3 - k : 3 - k + rows] for k in range(4))
        tail = jnp.concatenate([jnp.zeros((rows - 8, model_width), WIDE), jnp.zeros((5, model_width), WIDE), beyond[:3]], 0)
        grad = g_joined + g_state + tail

        by_lane = jnp.dot(
            g_band.reshape(HEADS, -1),
            in_bucket.T.astype(WIDE),
            precision=lax.Precision.HIGHEST,
            preferred_element_type=WIDE,
        )
        g_far = jnp.sum(g_far.reshape(HEADS, -1), 1)[:, None]
        g_last = jnp.sum(of_head * (by_lane + g_far * far_bucket), 0)
        small = jnp.stack(
            g_taps
            + [g_bias, g_join_bias, g_gain_attn[0], g_gain_mlp[0], g_last, squares]
            + [jnp.zeros((model_width,), WIDE)] * (share - 10)
        )
        attn_kept, attn_sent = attn_terms(
            info, mixed, g_join_low, norm_a, g_query, g_kv, attended, g_mid_low, small, owners, share
        )
        if l > 0:
            grad, attn_kept, attn_sent, mlp_half = tie(grad, attn_kept, attn_sent, mlp_half)
            line = line_terms(mlp_half)
            attn_arrived, line = tie(trade(attn_sent), line)
            plane = plane_terms(attn_kept, attn_arrived)
            grad, line, plane = tie(grad, line, plane)
            attn_way, mlp_way = send("seq", plane), send("z", line)

    above_mlp, above_attn = mlp_way, attn_way
    grad, attn_kept, attn_sent, above_mlp, above_attn, mlp_half = tie(
        grad, attn_kept, attn_sent, above_mlp, above_attn, mlp_half
    )
    plane = plane_terms(attn_kept, trade(attn_sent))
    mlp_half = send("z", line_terms(mlp_half))
    attn_way = send("seq", plane)
    attn_way, mlp_way = tie(attn_way, mlp_half)
    grad, line = tie(grad.astype(LOW), line_terms(attn_way))
    attn_way = send("z", line)
    input_grad = leave(grad)
    (
        g_join,
        g_attn_in,
        g_attn_out,
        g_mlp_in,
        g_mlp_out,
        loss,
        g_taps,
        g_bias,
        g_join_bias,
        g_gain_attn,
        g_gain_mlp,
        g_position,
    ) = collected(
        device_at.astype(jnp.int32).reshape(1),
        (1.0 / (total_valid * model_width)).reshape(1),
        [(mlp_way, attn_way), (above_mlp, above_attn)],
        quarters,
    )
    loss = loss.reshape(())
    return (
        arrive(activations),
        loss,
        arrive(input_grad),
        g_taps.transpose(1, 0, 2),
        g_bias.transpose(1, 0, 2),
        g_join,
        g_join_bias,
        g_gain_attn,
        g_attn_in,
        g_attn_out,
        g_position,
        g_gain_mlp,
        g_mlp_in,
        g_mlp_out,
    )


def chip_plan(mesh):
    grid = Mesh(
        mesh.devices.reshape(mesh.shape["seq"], mesh.shape["batch"] // 2, 2),
        ALL,
    )
    batch = ("z", "core")
    in_specs = (
        P(None, batch, "seq", None),
        P(None, batch, "seq", None),
        P(None, batch),
        P(None, None, ALL),
        P(None, None, ALL),
        P(None, ALL, None),
        P(None, ALL),
        P(None, ALL),
        P(None, None, ALL, None),
        P(None, ALL, None),
        P(None, ALL),
        P(None, ALL),
        P(None, None, ALL, None),
        P(None, ALL, None),
    )
    out_specs = (in_specs[0], P(), in_specs[0]) + in_specs[3:]
    return jax.shard_map(chip_body, mesh=grid, in_specs=in_specs, out_specs=out_specs, check_vma=False)


def shared_plan(mesh):
    in_specs = (
        P(None, "batch", "seq", None),
        P(None, "batch", "seq", None),
        P(None, "batch"),
        P(None, None, ("seq", "batch")),
        P(None, None, ("seq", "batch")),
        P(None, ("seq", "batch"), None),
        P(None, ("seq", "batch")),
        P(None, ("seq", "batch")),
        P(None, None, ("seq", "batch"), None),
        P(None, ("seq", "batch"), None),
        P(None, ("seq", "batch")),
        P(None, ("seq", "batch")),
        P(None, None, ("seq", "batch"), None),
        P(None, ("seq", "batch"), None),
    )
    out_specs = (
        P(None, "batch", "seq", None),
        P(),
        P(None, "batch", "seq", None),
        P(None, None, ("seq", "batch")),
        P(None, None, ("seq", "batch")),
        P(None, ("seq", "batch"), None),
        P(None, ("seq", "batch")),
        P(None, ("seq", "batch")),
        P(None, None, ("seq", "batch"), None),
        P(None, ("seq", "batch"), None),
        P(None, ("seq", "batch")),
        P(None, ("seq", "batch")),
        P(None, None, ("seq", "batch"), None),
        P(None, ("seq", "batch"), None),
    )
    return jax.shard_map(body, mesh=mesh, in_specs=in_specs, out_specs=out_specs, check_vma=False)


def solution(mesh):
    shared = shared_plan(mesh)

    def run(*arrays):
        sequences = arrays[0].shape[0] * arrays[0].shape[1]
        one_per_chip = 2 * sequences == mesh.devices.size and 2 * arrays[0].shape[0] == mesh.shape["seq"]
        two_layers = arrays[3].shape[0] == 2
        lanes_fit = arrays[5].shape[1] == SHARE * mesh.devices.size and arrays[0].shape[2] == 4 * BLOCK
        plan = chip_plan(mesh) if one_per_chip and lanes_fit and two_layers else shared
        return plan(*arrays)

    return run
```

```python
import jax
import jax.numpy as jnp
from jax import lax
from jax.experimental import pallas as pl
from jax.experimental.pallas import tpu as pltpu
from jax.sharding import Mesh
from jax.sharding import PartitionSpec as P

HEADS = 8
HEAD_DIM = 64
BUCKETS = 32


eps = 1e-06
bounds = (12, 16, 23, 32, 46, 64, 91)
windows = ((2, 0), (3, 2), (4, 5))


def passed_along(block, axis, distance):
    devices = range(lax.axis_size(axis))
    route = [(i - distance, i) for i in devices if i - distance in devices]
    return lax.ppermute(block, axis, route)


def bucket_ids(offsets):
    magnitude = jnp.abs(offsets)
    far_ids = 8 + sum(((magnitude >= bound_value).astype(jnp.int32) for bound_value in bounds))
    near_ids = jnp.where(magnitude < 8, magnitude, far_ids)
    return jnp.where(offsets > 0, 16, 0) + near_ids


def rms_norm(values, gain):
    return values * lax.rsqrt(jnp.mean(values * values, -1, keepdims=True) + eps) * gain


def conv_sum(extended, tap_rows, biases, row_count):
    total = jnp.zeros((row_count, extended.shape[1]), jnp.float32) + jnp.sum(biases, 0)
    for window, offset in windows:
        for tap_index in range(window):
            first_row = 4 - window + tap_index
            total = (
                total + tap_rows[offset + tap_index] * extended[first_row : first_row + row_count]
            )
    return total


def project(left, right):
    return jnp.dot(left, right, preferred_element_type=jnp.float32)


def project_left(left, right):
    return lax.dot_general(
        left, right, (((0,), (0,)), ((), ())), preferred_element_type=jnp.float32
    )


def project_right(left, right):
    return lax.dot_general(
        left, right, (((1,), (1,)), ((), ())), preferred_element_type=jnp.float32
    )


def score_block(query, keys_all, pos_table, one_hot_ids, key_valid):
    query_heads = query.reshape(query.shape[0], HEADS, HEAD_DIM)
    key_heads = keys_all.reshape(keys_all.shape[0], HEADS, HEAD_DIM)
    rel_bias = jnp.einsum(
        "slb,bh->hsl",
        one_hot_ids,
        pos_table.reshape(BUCKETS, HEADS),
        preferred_element_type=jnp.float32,
    )
    scores = (
        jnp.einsum("shd,lhd->hsl", query_heads, key_heads, preferred_element_type=jnp.float32)
        + rel_bias
    )
    return jnp.where(key_valid[None, None, :], scores, -1e30)


def layer_forward(state, weights, one_hot_ids, key_valid):
    (
        tap_rows,
        biases,
        join_matrix,
        join_shift,
        gain_first,
        attn_in,
        attn_out,
        pos_table,
        gain_second,
        mlp_in,
        mlp_out,
    ) = weights
    row_count = state.shape[0]
    rounded_in = state.astype(jnp.bfloat16)
    prior_rows = passed_along(rounded_in[row_count - 3 :], "seq", 1)
    extended = jnp.concatenate([prior_rows, rounded_in], 0).astype(jnp.float32)
    mixed = conv_sum(
        extended, tap_rows.astype(jnp.float32), biases.astype(jnp.float32), row_count
    ).astype(jnp.bfloat16)
    joined = state + project(mixed, join_matrix) + join_shift.astype(jnp.float32)
    normed = rms_norm(joined, gain_first.astype(jnp.float32)).astype(jnp.bfloat16)
    projected = jnp.einsum(
        "sd,cdi->csi", normed, attn_in, preferred_element_type=jnp.float32
    ).astype(jnp.bfloat16)
    keys_all, values_all = (
        lax.all_gather(projected[1], "seq", axis=0, tiled=True),
        lax.all_gather(projected[2], "seq", axis=0, tiled=True),
    )
    scores = score_block(projected[0], keys_all, pos_table, one_hot_ids, key_valid)
    row_max = jnp.max(scores, -1, keepdims=True)
    log_total = row_max + jnp.log(jnp.sum(jnp.exp(scores - row_max), -1, keepdims=True))
    probs = jnp.exp(scores - log_total)
    value_heads = values_all.reshape(values_all.shape[0], HEADS, HEAD_DIM)
    attended = jnp.einsum(
        "hsl,lhd->shd", probs.astype(jnp.bfloat16), value_heads, preferred_element_type=jnp.float32
    )
    attended = attended.reshape(row_count, -1).astype(jnp.bfloat16)
    mid_state = joined + project(attended, attn_out)
    normed_mid = rms_norm(mid_state, gain_second.astype(jnp.float32)).astype(jnp.bfloat16)
    gate_up = jnp.einsum("sd,cdf->csf", normed_mid, mlp_in, preferred_element_type=jnp.float32)
    hidden = (jax.nn.gelu(gate_up[0], approximate=True) * gate_up[1]).astype(jnp.bfloat16)
    out_state = mid_state + project(hidden, mlp_out)
    saved = (
        extended,
        mixed,
        joined,
        normed,
        projected,
        keys_all,
        values_all,
        log_total,
        attended,
        mid_state,
        normed_mid,
        gate_up,
        hidden,
    )
    return (out_state, saved)


def gated_unit(gate_in, up_in):
    return jax.nn.gelu(gate_in, approximate=True) * up_in


def layer_backward(grad_out, saved, weights, one_hot_ids, key_valid):
    (
        tap_rows,
        biases,
        join_matrix,
        join_shift,
        gain_first,
        attn_in,
        attn_out,
        pos_table,
        gain_second,
        mlp_in,
        mlp_out,
    ) = weights
    (
        extended,
        mixed,
        joined,
        normed,
        projected,
        keys_all,
        values_all,
        log_total,
        attended,
        mid_state,
        normed_mid,
        gate_up,
        hidden,
    ) = saved
    row_count = grad_out.shape[0]
    model_width = grad_out.shape[1]
    grad_branch = grad_out.astype(jnp.bfloat16)
    grad_mlp_out = project_left(hidden, grad_branch)
    grad_hidden = project_right(grad_branch, mlp_out)
    unused_value, gelu_back = jax.vjp(gated_unit, gate_up[0], gate_up[1])
    grad_gate, grad_up = gelu_back(grad_hidden)
    grad_gate_up = jnp.stack([grad_gate, grad_up]).astype(jnp.bfloat16)
    grad_mlp_in = jnp.einsum(
        "sd,csf->cdf", normed_mid, grad_gate_up, preferred_element_type=jnp.float32
    )
    grad_normed_mid = jnp.einsum(
        "csf,cdf->sd", grad_gate_up, mlp_in, preferred_element_type=jnp.float32
    )
    unused_mid, mid_back = jax.vjp(rms_norm, mid_state, gain_second.astype(jnp.float32))
    grad_mid_part, grad_gain_second = mid_back(grad_normed_mid)
    grad_mid = grad_out + grad_mid_part
    grad_attn = grad_mid.astype(jnp.bfloat16)
    grad_attn_out = project_left(attended, grad_attn)
    grad_attended = (
        project_right(grad_attn, attn_out).astype(jnp.bfloat16).reshape(row_count, HEADS, HEAD_DIM)
    )
    query = projected[0]
    scores = score_block(query, keys_all, pos_table, one_hot_ids, key_valid)
    probs = jnp.exp(scores - log_total)
    value_heads = values_all.reshape(values_all.shape[0], HEADS, HEAD_DIM)
    key_heads = keys_all.reshape(keys_all.shape[0], HEADS, HEAD_DIM)
    query_heads = query.reshape(row_count, HEADS, HEAD_DIM)
    grad_probs = jnp.einsum(
        "shd,lhd->hsl", grad_attended, value_heads, preferred_element_type=jnp.float32
    )
    row_delta = jnp.sum(probs * grad_probs, -1, keepdims=True)
    grad_scores = (probs * (grad_probs - row_delta)).astype(jnp.bfloat16)
    grad_table = jnp.einsum(
        "slb,hsl->bh", one_hot_ids, grad_scores, preferred_element_type=jnp.float32
    ).reshape(-1)
    grad_query = jnp.einsum(
        "hsl,lhd->shd", grad_scores, key_heads, preferred_element_type=jnp.float32
    ).reshape(row_count, -1)
    grad_values_all = jnp.einsum(
        "hsl,shd->lhd",
        probs.astype(jnp.bfloat16),
        grad_attended,
        preferred_element_type=jnp.float32,
    )
    grad_keys_all = jnp.einsum(
        "hsl,shd->lhd", grad_scores, query_heads, preferred_element_type=jnp.float32
    )
    key_total = grad_keys_all.shape[0]
    grad_key, grad_value = (
        lax.psum_scatter(
            grad_keys_all.reshape(key_total, -1).astype(jnp.bfloat16),
            "seq",
            scatter_dimension=0,
            tiled=True,
        ).astype(jnp.float32),
        lax.psum_scatter(
            grad_values_all.reshape(key_total, -1).astype(jnp.bfloat16),
            "seq",
            scatter_dimension=0,
            tiled=True,
        ).astype(jnp.float32),
    )
    grad_projected = jnp.stack([grad_query, grad_key, grad_value]).astype(jnp.bfloat16)
    grad_attn_in = jnp.einsum(
        "sd,csi->cdi", normed, grad_projected, preferred_element_type=jnp.float32
    )
    grad_normed = jnp.einsum(
        "csi,cdi->sd", grad_projected, attn_in, preferred_element_type=jnp.float32
    )
    unused_joined, joined_back = jax.vjp(rms_norm, joined, gain_first.astype(jnp.float32))
    grad_joined_part, grad_gain_first = joined_back(grad_normed)
    grad_joined = grad_mid + grad_joined_part
    grad_join = grad_joined.astype(jnp.bfloat16)
    grad_join_matrix = project_left(mixed, grad_join)
    grad_join_shift = jnp.sum(grad_join.astype(jnp.float32), 0)
    grad_mixed = project_right(grad_join, join_matrix).astype(jnp.bfloat16).astype(jnp.float32)
    grad_biases = jnp.broadcast_to(jnp.sum(grad_mixed, 0), (3, model_width))
    tap_float = tap_rows.astype(jnp.float32)
    grad_taps = [None] * 9
    grad_extended = jnp.zeros((row_count + 3, model_width), jnp.float32)
    for window, offset in windows:
        for tap_index in range(window):
            first_row = 4 - window + tap_index
            grad_taps[offset + tap_index] = jnp.sum(
                grad_mixed * extended[first_row : first_row + row_count], 0
            )
            grad_extended = grad_extended + jnp.pad(
                tap_float[offset + tap_index] * grad_mixed, ((first_row, 3 - first_row), (0, 0))
            )
    back_rows = passed_along(grad_extended[:3], "seq", -1)
    grad_in = grad_joined + grad_extended[3:] + jnp.pad(back_rows, ((row_count - 3, 0), (0, 0)))
    layer_grads = (
        jnp.stack(grad_taps),
        grad_biases,
        grad_join_matrix,
        grad_join_shift,
        grad_gain_first,
        grad_attn_in,
        grad_attn_out,
        grad_table,
        grad_gain_second,
        grad_mlp_in,
        grad_mlp_out,
    )
    return (grad_in, layer_grads)


def body(
    byte_states,
    teacher,
    lengths,
    conv_taps,
    conv_bias,
    join_weight,
    join_bias,
    gain_attn,
    attn_in_weight,
    attn_out_weight,
    position_bias,
    gain_mlp,
    mlp_in_weight,
    mlp_out_weight,
):
    layer_count = conv_taps.shape[0]
    micro_count = byte_states.shape[0]
    row_count = byte_states.shape[2]
    model_width = byte_states.shape[3]
    seq_total = row_count * lax.axis_size("seq")
    positions = lax.axis_index("seq") * row_count + jnp.arange(row_count)
    key_positions = jnp.arange(seq_total)
    bucket_grid = bucket_ids(key_positions[None, :] - positions[:, None])
    one_hot_ids = (bucket_grid[:, :, None] == jnp.arange(BUCKETS)[None, None, :]).astype(
        jnp.bfloat16
    )
    total_valid = lax.psum(jnp.sum(lengths.astype(jnp.float32)), "batch")
    sums = [None] * layer_count
    out_rows = []
    grad_rows = []
    local_squares = jnp.zeros((), jnp.float32)
    for batch_index in range(micro_count):
        state = byte_states[batch_index, 0].astype(jnp.float32)
        length = lengths[batch_index, 0]
        key_valid = key_positions < length
        row_valid = positions < length
        kept = []
        for layer_index in range(layer_count):
            weights = (
                lax.all_gather(conv_taps[layer_index], ("seq", "batch"), axis=1, tiled=True),
                lax.all_gather(conv_bias[layer_index], ("seq", "batch"), axis=1, tiled=True),
                lax.all_gather(join_weight[layer_index], ("seq", "batch"), axis=0, tiled=True),
                lax.all_gather(join_bias[layer_index], ("seq", "batch"), axis=0, tiled=True),
                lax.all_gather(gain_attn[layer_index], ("seq", "batch"), axis=0, tiled=True),
                lax.all_gather(attn_in_weight[layer_index], ("seq", "batch"), axis=1, tiled=True),
                lax.all_gather(attn_out_weight[layer_index], ("seq", "batch"), axis=0, tiled=True),
                lax.all_gather(position_bias[layer_index], ("seq", "batch"), axis=0, tiled=True),
                lax.all_gather(gain_mlp[layer_index], ("seq", "batch"), axis=0, tiled=True),
                lax.all_gather(mlp_in_weight[layer_index], ("seq", "batch"), axis=1, tiled=True),
                lax.all_gather(mlp_out_weight[layer_index], ("seq", "batch"), axis=0, tiled=True),
            )
            state, saved = layer_forward(state, weights, one_hot_ids, key_valid)
            kept.append(saved)
        out_rows.append(state)
        diff = jnp.where(
            row_valid[:, None], state - teacher[batch_index, 0].astype(jnp.float32), 0.0
        )
        local_squares = local_squares + jnp.sum(diff * diff)
        grad_state = 2.0 * diff / (total_valid * model_width)
        for layer_index in reversed(range(layer_count)):
            weights = (
                lax.all_gather(conv_taps[layer_index], ("seq", "batch"), axis=1, tiled=True),
                lax.all_gather(conv_bias[layer_index], ("seq", "batch"), axis=1, tiled=True),
                lax.all_gather(join_weight[layer_index], ("seq", "batch"), axis=0, tiled=True),
                lax.all_gather(join_bias[layer_index], ("seq", "batch"), axis=0, tiled=True),
                lax.all_gather(gain_attn[layer_index], ("seq", "batch"), axis=0, tiled=True),
                lax.all_gather(attn_in_weight[layer_index], ("seq", "batch"), axis=1, tiled=True),
                lax.all_gather(attn_out_weight[layer_index], ("seq", "batch"), axis=0, tiled=True),
                lax.all_gather(position_bias[layer_index], ("seq", "batch"), axis=0, tiled=True),
                lax.all_gather(gain_mlp[layer_index], ("seq", "batch"), axis=0, tiled=True),
                lax.all_gather(mlp_in_weight[layer_index], ("seq", "batch"), axis=1, tiled=True),
                lax.all_gather(mlp_out_weight[layer_index], ("seq", "batch"), axis=0, tiled=True),
            )
            grad_state, layer_grads = layer_backward(
                grad_state, kept[layer_index], weights, one_hot_ids, key_valid
            )
            if sums[layer_index] is None:
                sums[layer_index] = layer_grads
            else:
                sums[layer_index] = jax.tree.map(jnp.add, sums[layer_index], layer_grads)
        grad_rows.append(grad_state)
    loss = lax.psum(local_squares, ("seq", "batch")) / (total_valid * model_width)
    stacked_grads = tuple(
        (
            jnp.stack([sums[layer_index][member] for layer_index in range(layer_count)])
            for member in range(11)
        )
    )
    (
        grad_taps,
        grad_biases,
        grad_join_matrix,
        grad_join_shift,
        grad_gain_first,
        grad_attn_in,
        grad_attn_out,
        grad_table,
        grad_gain_second,
        grad_mlp_in,
        grad_mlp_out,
    ) = stacked_grads
    owned = (
        lax.psum_scatter(grad_taps, ("seq", "batch"), scatter_dimension=2, tiled=True),
        lax.psum_scatter(grad_biases, ("seq", "batch"), scatter_dimension=2, tiled=True),
        lax.psum_scatter(grad_join_matrix, ("seq", "batch"), scatter_dimension=1, tiled=True),
        lax.psum_scatter(grad_join_shift, ("seq", "batch"), scatter_dimension=1, tiled=True),
        lax.psum_scatter(grad_gain_first, ("seq", "batch"), scatter_dimension=1, tiled=True),
        lax.psum_scatter(grad_attn_in, ("seq", "batch"), scatter_dimension=2, tiled=True),
        lax.psum_scatter(grad_attn_out, ("seq", "batch"), scatter_dimension=1, tiled=True),
        lax.psum_scatter(grad_table, ("seq", "batch"), scatter_dimension=1, tiled=True),
        lax.psum_scatter(grad_gain_second, ("seq", "batch"), scatter_dimension=1, tiled=True),
        lax.psum_scatter(grad_mlp_in, ("seq", "batch"), scatter_dimension=2, tiled=True),
        lax.psum_scatter(grad_mlp_out, ("seq", "batch"), scatter_dimension=1, tiled=True),
    )
    activations = jnp.stack(out_rows)[:, None]
    input_grad = jnp.stack(grad_rows)[:, None]
    return (
        activations,
        loss,
        input_grad,
        owned[0],
        owned[1],
        owned[2],
        owned[3],
        owned[4],
        owned[5],
        owned[6],
        owned[7],
        owned[8],
        owned[9],
        owned[10],
    )


ALL = ("seq", "z", "core")
LOW = jnp.bfloat16
WIDE = jnp.float32
BLOCK = 256
SHARE = 16
MASKED = -1e30


def nt(left, right):
    return lax.dot_general(left, right, (((1,), (1,)), ((), ())), preferred_element_type=WIDE)


def nn(left, right):
    return lax.dot_general(left, right, (((1,), (0,)), ((), ())), preferred_element_type=WIDE)


def tn(left, right):
    return lax.dot_general(left, right, (((0,), (0,)), ((), ())), preferred_element_type=WIDE)


def band_kernel(line_ref, band_ref):
    eight = jnp.broadcast_to(line_ref[0], (8, 4 * BLOCK))
    eight = pltpu.roll(eight, 0, 1, stride=1, stride_axis=0)
    for g in range(BLOCK // 8):
        rolled = pltpu.roll(eight, 8 * g, 1) if g else eight
        rows = slice(8 * g, 8 * g + 8)
        band_ref[0, 0, rows] = rolled[:, :BLOCK]
        band_ref[0, 1, rows] = rolled[:, BLOCK : 2 * BLOCK]
        band_ref[0, 2, rows] = rolled[:, 3 * BLOCK :]


def build_band(line):
    return pl.pallas_call(
        band_kernel,
        grid=(HEADS,),
        in_specs=[pl.BlockSpec((1, 1, 4 * BLOCK), lambda h: (h, 0, 0))],
        out_specs=pl.BlockSpec((1, 3, BLOCK, BLOCK), lambda h: (h, 0, 0, 0)),
        out_shape=jax.ShapeDtypeStruct((HEADS, 3, BLOCK, BLOCK), WIDE),
        name="bias_band",
    )(line.reshape(HEADS, 1, 4 * BLOCK))


def key_blocks(core, near):
    near_rows = pl.multiple_of(BLOCK * (1 - core), BLOCK)
    far_rows = pl.multiple_of(BLOCK * core, BLOCK)
    below, above = 1 + core, 2 - core
    if near:
        return near_rows, ((0, near_rows, 0), (0, far_rows, below), (1, far_rows, above), (1, near_rows, None))
    return far_rows, ((0, far_rows, 0), (0, near_rows, above), (1, far_rows, None), (1, near_rows, None))


def keys_with_mask(block, lane, head, first_position, length, constant):
    rows = first_position + lax.broadcasted_iota(jnp.int32, (BLOCK, 1), 0)
    mask = jnp.where(rows < length, 0.0, MASKED)
    spare = (1 - head) * HEAD_DIM
    extra = jnp.where(lane == spare, mask, jnp.where(lane == spare + 1, constant, 0.0))
    return jnp.where(lane // HEAD_DIM == head, block.astype(WIDE), extra).astype(LOW)


def query_with_ones(block, lane, head):
    spare = (1 - head) * HEAD_DIM
    extra = jnp.where((lane == spare) | (lane == spare + 1), 1.0, 0.0)
    return jnp.where(lane // HEAD_DIM == head, block.astype(WIDE), extra).astype(LOW)


def only_head(block, lane, head):
    return jnp.where(lane // HEAD_DIM == head, block.astype(WIDE), 0.0).astype(LOW)


def attend_kernel(
    info_ref, far_ref, q_ref, k_ref, v_ref, ko_ref, vo_ref, band_ref, out_ref, lse_ref, score_ref
):
    core, length = info_ref[0], info_ref[1]
    pair = pl.program_id(0)
    lane = lax.broadcasted_iota(jnp.int32, (1, 2 * HEAD_DIM), 1)
    for n in range(2):
        q_rows, blocks = key_blocks(core, n == 0)
        query = q_ref[pl.ds(q_rows, BLOCK), :]
        halves = []
        for head in range(2):
            q_low = query_with_ones(query, lane, head)
            top = None
            for b, (side, start, slot) in enumerate(blocks):
                first = 2 * BLOCK * (core if side == 0 else 1 - core) + start
                keys = (k_ref, ko_ref)[side][pl.ds(start, BLOCK), :]
                constant = far_ref[2 * pair + head] if slot is None else 0.0
                scores = nt(keys_with_mask(keys, lane, head, first, length, constant), q_low)
                if slot is not None:
                    scores = scores + band_ref[head, slot]
                score_ref[b] = scores
                block_top = jnp.max(scores, 0, keepdims=True)
                top = block_top if top is None else jnp.maximum(top, block_top)
            total = jnp.zeros((1, BLOCK), WIDE)
            mixed = jnp.zeros((2 * HEAD_DIM, BLOCK), WIDE)
            for b, (side, start, slot) in enumerate(blocks):
                weights = jnp.exp(score_ref[b] - top)
                total = total + jnp.sum(weights, 0, keepdims=True)
                values = (v_ref, vo_ref)[side][pl.ds(start, BLOCK), :]
                mixed = mixed + tn(values, weights.astype(LOW))
            lse_ref[0, n, head : head + 1, :] = top + jnp.log(total)
            halves.append((mixed / total)[head * HEAD_DIM : (head + 1) * HEAD_DIM])
        out_ref[pl.ds(q_rows, BLOCK), :] = jnp.transpose(jnp.concatenate(halves, 0)).astype(LOW)


def attend(info, far, projected, others, band):
    query, own_kv = projected
    rows = query.shape[0]
    pairs = HEADS // 2
    width = 2 * HEAD_DIM
    col = lambda shift: pl.BlockSpec((rows, width), lambda p: (0, p + shift))
    return pl.pallas_call(
        attend_kernel,
        grid=(pairs,),
        in_specs=[
            pl.BlockSpec(memory_space=pltpu.SMEM),
            pl.BlockSpec(memory_space=pltpu.SMEM),
            col(0),
            col(0),
            col(pairs),
            col(0),
            col(pairs),
            pl.BlockSpec((2, 3, BLOCK, BLOCK), lambda p: (p, 0, 0, 0)),
        ],
        out_specs=[col(0), pl.BlockSpec((1, 2, 2, BLOCK), lambda p: (p, 0, 0, 0))],
        out_shape=[
            jax.ShapeDtypeStruct((rows, HEADS * HEAD_DIM), LOW),
            jax.ShapeDtypeStruct((pairs, 2, 2, BLOCK), WIDE),
        ],
        scratch_shapes=[pltpu.VMEM((4, BLOCK, BLOCK), WIDE)],
        name="attend",
    )(info, far, query, own_kv, own_kv, others, others, band)


def attend_back_kernel(
    info_ref,
    far_ref,
    q_ref,
    k_ref,
    v_ref,
    ko_ref,
    vo_ref,
    band_ref,
    out_ref,
    gout_ref,
    lse_ref,
    *refs,
):
    gq_ref, gown_ref, goth_ref, gband_ref, gfar_ref, gk_acc, gv_acc, band_acc, far_acc = refs[-9:]
    core, length, first_pair = info_ref[0], info_ref[1], info_ref[2]
    pair = first_pair + pl.program_id(0)
    width = 2 * HEAD_DIM
    lane = lax.broadcasted_iota(jnp.int32, (1, width), 1)
    gk_acc[...] = jnp.zeros_like(gk_acc)
    gv_acc[...] = jnp.zeros_like(gv_acc)
    band_acc[...] = jnp.zeros_like(band_acc)
    far_acc[...] = jnp.zeros_like(far_acc)
    select = jnp.where(
        lax.broadcasted_iota(jnp.int32, (8, width), 0)
        == lax.broadcasted_iota(jnp.int32, (8, width), 1) // HEAD_DIM,
        1.0,
        0.0,
    )
    for n in range(2):
        q_rows, blocks = key_blocks(core, n == 0)
        query = q_ref[pl.ds(q_rows, BLOCK), :]
        gout = gout_ref[pl.ds(q_rows, BLOCK), :]
        dots = gout.astype(WIDE) * out_ref[pl.ds(q_rows, BLOCK), :].astype(WIDE)
        deltas = lax.dot_general(
            select,
            dots,
            (((1,), (1,)), ((), ())),
            precision=lax.Precision.HIGHEST,
            preferred_element_type=WIDE,
        )
        halves = []
        for head in range(2):
            q_ones = query_with_ones(query, lane, head)
            q_low = only_head(query, lane, head)
            g_low = only_head(gout, lane, head)
            lse = lse_ref[0, n, head : head + 1, :]
            delta = deltas[head : head + 1]
            gq = jnp.zeros((width, BLOCK), WIDE)
            for side, start, slot in blocks:
                first = 2 * BLOCK * (core if side == 0 else 1 - core) + start
                keys = (k_ref, ko_ref)[side][pl.ds(start, BLOCK), :]
                values = (v_ref, vo_ref)[side][pl.ds(start, BLOCK), :]
                constant = far_ref[2 * pair + head] if slot is None else 0.0
                scores = nt(keys_with_mask(keys, lane, head, first, length, constant), q_ones)
                if slot is not None:
                    scores = scores + band_ref[head, slot]
                probs = jnp.exp(scores - lse)
                gprobs = nt(values, g_low)
                gscores = probs * (gprobs - delta)
                if slot is None:
                    part = jnp.sum(gscores.reshape(BLOCK // 8, 8, BLOCK), 0)
                    far_acc[head] = far_acc[head] + part
                else:
                    band_acc[head, slot] = band_acc[head, slot] + gscores
                gs_low = gscores.astype(LOW)
                at = pl.ds(2 * BLOCK * side + start, BLOCK)
                gv_acc[at, :] = gv_acc[at, :] + nn(probs.astype(LOW), g_low)
                gk_acc[at, :] = gk_acc[at, :] + nn(gs_low, q_low)
                gq = gq + tn(keys, gs_low)
            halves.append(gq[head * HEAD_DIM : (head + 1) * HEAD_DIM])
        gq_ref[pl.ds(q_rows, BLOCK), :] = jnp.transpose(jnp.concatenate(halves, 0)).astype(LOW)
    own = 2 * BLOCK
    gown_ref[0] = gk_acc[:own, :]
    gown_ref[1] = gv_acc[:own, :]
    goth_ref[0] = gk_acc[own:, :].astype(LOW)
    goth_ref[1] = gv_acc[own:, :].astype(LOW)
    span = 4 * BLOCK
    gap = jnp.zeros((8, BLOCK), WIDE)
    row = lax.broadcasted_iota(jnp.int32, (8, span), 0)
    for head in range(2):
        lines = jnp.zeros((8, span), WIDE)
        for g in range(BLOCK // 8):
            rows = slice(8 * g, 8 * g + 8)
            piece = jnp.concatenate(
                [band_acc[head, 0, rows], band_acc[head, 1, rows], gap, band_acc[head, 2, rows]], 1
            )
            lines = lines + (pltpu.roll(piece, span - 8 * g, 1) if g else piece)
        for bit in (1, 2, 4):
            lines = jnp.where((row & bit) != 0, pltpu.roll(lines, span - bit, 1), lines)
        gband_ref[0, head : head + 1, :] = jnp.sum(lines, 0, keepdims=True)
        gfar_ref[0, head : head + 1, :] = jnp.sum(far_acc[head], 0, keepdims=True)


def attend_back(info, far, projected, others, band, out, gout, lse, first, count, before=()):
    query, own_kv = projected
    rows = query.shape[0]
    pairs = HEADS // 2
    width = 2 * HEAD_DIM
    inner = HEADS * HEAD_DIM
    col = lambda shift: pl.BlockSpec((rows, width), lambda p: (0, first + p + shift))
    two = pl.BlockSpec((2, rows, width), lambda p: (0, 0, first + p))
    some = lambda *block: pl.BlockSpec(block, lambda p: (first + p,) + (0,) * (len(block) - 1))
    info = jnp.concatenate([info, jnp.full((1,), first, jnp.int32)])
    return pl.pallas_call(
        attend_back_kernel,
        grid=(count,),
        in_specs=[
            pl.BlockSpec(memory_space=pltpu.SMEM),
            pl.BlockSpec(memory_space=pltpu.SMEM),
            col(0),
            col(0),
            col(pairs),
            col(0),
            col(pairs),
            some(2, 3, BLOCK, BLOCK),
            col(0),
            col(0),
            some(1, 2, 2, BLOCK),
        ]
        + [pl.BlockSpec(memory_space=pl.ANY)] * len(before),
        out_specs=[col(0), two, two, some(1, 2, 4 * BLOCK), some(1, 2, BLOCK)],
        out_shape=[
            jax.ShapeDtypeStruct((rows, inner), LOW),
            jax.ShapeDtypeStruct((2, rows, inner), WIDE),
            jax.ShapeDtypeStruct((2, rows, inner), LOW),
            jax.ShapeDtypeStruct((pairs, 2, 4 * BLOCK), WIDE),
            jax.ShapeDtypeStruct((pairs, 2, BLOCK), WIDE),
        ],
        input_output_aliases={11 + at: at for at in range(len(before))},
        scratch_shapes=[
            pltpu.VMEM((4 * BLOCK, width), WIDE),
            pltpu.VMEM((4 * BLOCK, width), WIDE),
            pltpu.VMEM((2, 3, BLOCK, BLOCK), WIDE),
            pltpu.VMEM((2, 8, BLOCK), WIDE),
        ],
        name="attend_back",
    )(info, far, query, own_kv, own_kv, others, others, band, out, gout, lse, *before)


def store_terms(core, terms, kept_ref, sent_ref, at):
    for own in range(2):

        @pl.when(core == own)
        def _(own=own):
            kept_ref[at] = terms[:, own].astype(LOW)
            sent_ref[at] = terms[:, 1 - own].astype(LOW)


def unit_rows(values):
    inverse = lax.rsqrt(jnp.mean(values * values, -1, keepdims=True) + eps)
    return values * inverse, inverse


def normed(values, gain):
    return (unit_rows(values)[0] * gain).astype(LOW)


def normed_back(grad, values, gain):
    unit, inverse = unit_rows(values)
    scaled = grad * gain
    grad_in = inverse * (scaled - unit * jnp.mean(scaled * unit, -1, keepdims=True))
    return grad_in, jnp.sum(grad * unit, 0, keepdims=True)


def outward_chunk(block, share, width):
    owners = block.shape[0] // share
    parts = [
        block[:, at * width : (at + 1) * width].reshape(owners, 1, share, width)
        for at in range(block.shape[1] // width)
    ]
    return jnp.concatenate(parts, 1).reshape(-1, width)


ROOT = 0.7978845608028654
CUBIC = 0.044715


def mlp_kernel(att_ref, joined_ref, gain_ref, ao_ref, gate_ref, up_ref, out_ref, mid_ref, norm_ref, state_ref):
    width = att_ref.shape[1]

    @pl.when(pl.program_id(0) == 0)
    def _():
        mid = joined_ref[...] + nn(att_ref[...], ao_ref[...])
        mid_ref[...] = mid
        norm_ref[...] = normed(mid, gain_ref[...])
        state_ref[...] = mid

    norm = norm_ref[...]
    gate = nn(norm, gate_ref[...])
    turn = jnp.tanh(ROOT * (gate + CUBIC * gate * gate * gate))
    hidden = 0.5 * gate * (1.0 + turn) * nn(norm, up_ref[...])
    outward = outward_chunk(out_ref[...], SHARE, width)
    state_ref[...] += nn(hidden.astype(LOW), outward)


def rest_specs(width, quarters, layers, l):
    start = layers * quarters + l * (2 * quarters + 1)
    column = lambda first, moves: pl.BlockSpec(
        (width, width), lambda j: (0, start + first + j) if moves else (0, start + first)
    )
    return [
        column(0, False),
        column(1, True),
        column(1 + quarters, True),
        pl.BlockSpec((width // quarters, quarters * width), lambda j: (j, l)),
    ]


def mlp_forward(attended, joined, gain, rest, quarters, layers, l):
    rows, width = joined.shape
    whole = pl.BlockSpec((rows, width), lambda j: (0, 0))
    return pl.pallas_call(
        mlp_kernel,
        grid=(quarters,),
        in_specs=[whole, whole, pl.BlockSpec((1, width), lambda j: (0, 0))]
        + rest_specs(width, quarters, layers, l),
        out_specs=[whole] * 3,
        out_shape=[
            jax.ShapeDtypeStruct((rows, width), WIDE),
            jax.ShapeDtypeStruct((rows, width), LOW),
            jax.ShapeDtypeStruct((rows, width), WIDE),
        ],
        name="mlp",
    )(attended, joined, gain.reshape(1, width), rest, rest, rest, rest)


def mlp_back_kernel(
    info_ref,
    grad_ref,
    norm_ref,
    mid_ref,
    gain_ref,
    ao_ref,
    gate_ref,
    up_ref,
    out_ref,
    gmid_ref,
    gmid_low_ref,
    gatt_ref,
    ggain_ref,
    kept_ref,
    sent_ref,
    turned_ref,
    low_ref,
    gnorm_ref,
):
    core = info_ref[0]
    step = pl.program_id(0)
    owners, blocks, share, width = kept_ref.shape
    quarters = blocks // 3

    @pl.when(step == 0)
    def _():
        turned_ref[...] = jnp.transpose(norm_ref[...])
        low_ref[...] = grad_ref[...].astype(LOW)
        gnorm_ref[...] = jnp.zeros_like(gnorm_ref)

    norm, low = norm_ref[...], low_ref[...]
    gate, up = nn(norm, gate_ref[...]), nn(norm, up_ref[...])
    square = gate * gate
    turn = jnp.tanh(ROOT * gate * (1.0 + CUBIC * square))
    half = 0.5 * (1.0 + turn)
    slope = half + 0.5 * ROOT * gate * (1.0 - turn * turn) * (1.0 + 3.0 * CUBIC * square)
    bent = half * gate
    g_hidden = nt(low, outward_chunk(out_ref[...], share, width))
    g_gate = (g_hidden * up * slope).astype(LOW)
    g_up = (g_hidden * bent).astype(LOW)
    hidden = (bent * up).astype(LOW)
    every = slice(None)
    for at, part in ((step, g_gate), (step + quarters, g_up)):
        terms = nn(turned_ref[...], part).reshape(owners, 2, share, width)
        store_terms(core, terms, kept_ref, sent_ref, (every, at))
    few = owners // quarters
    terms = tn(hidden, low).reshape(few, 2, quarters, share, width)
    at = (pl.ds(step * few, few), slice(2 * quarters, blocks))
    store_terms(core, terms, kept_ref, sent_ref, at)
    gnorm_ref[...] += nt(g_gate, gate_ref[...]) + nt(g_up, up_ref[...])

    @pl.when(step == quarters - 1)
    def _():
        part, ggain_ref[...] = normed_back(gnorm_ref[...], mid_ref[...], gain_ref[...])
        g_mid = grad_ref[...] + part
        gmid_ref[...] = g_mid
        g_low = g_mid.astype(LOW)
        gmid_low_ref[...] = g_low
        gatt_ref[...] = nt(g_low, ao_ref[...]).astype(LOW)


def mlp_back(info, grad, norm, mid, gain, rest, quarters, layers, l, owners, share):
    rows, width = grad.shape
    shape = jax.ShapeDtypeStruct((owners, 3 * quarters, share, width), LOW)
    whole = pl.BlockSpec((rows, width), lambda j: (0, 0))
    line = pl.BlockSpec((1, width), lambda j: (0, 0))
    out = pl.BlockSpec(shape.shape, lambda j: (0, 0, 0, 0))
    return pl.pallas_call(
        mlp_back_kernel,
        grid=(quarters,),
        in_specs=[pl.BlockSpec(memory_space=pltpu.SMEM), whole, whole, whole, line]
        + rest_specs(width, quarters, layers, l),
        out_specs=[whole, whole, whole, line, out, out],
        out_shape=[
            jax.ShapeDtypeStruct((rows, width), WIDE),
            jax.ShapeDtypeStruct((rows, width), LOW),
            jax.ShapeDtypeStruct((rows, width), LOW),
            jax.ShapeDtypeStruct((1, width), WIDE),
            shape,
            shape,
        ],
        scratch_shapes=[
            pltpu.VMEM((width, rows), LOW),
            pltpu.VMEM((rows, width), LOW),
            pltpu.VMEM((rows, width), WIDE),
        ],
        name="mlp_back",
    )(info, grad, norm, mid, gain.reshape(1, width), rest, rest, rest, rest)


def inner_back_kernel(
    info_ref,
    gquery_ref,
    gown_ref,
    garrived_ref,
    weight_ref,
    taps_ref,
    gain_ref,
    joined_ref,
    gmid_ref,
    mixed_ref,
    norm_ref,
    att_ref,
    gmid_low_ref,
    extended_ref,
    lines_ref,
    kept_ref,
    sent_ref,
    grad_ref,
    head_ref,
    padded_ref,
    small_ref,
):
    core = info_ref[0]
    owners, blocks, share, width = kept_ref.shape
    rows = joined_ref.shape[0]

    def put(at, turned, right):
        terms = nn(turned, right).reshape(owners, 2, share, width)
        store_terms(core, terms, kept_ref, sent_ref, (slice(None), at))

    column = lambda at: weight_ref[:, at * width : (at + 1) * width]
    parts = [gquery_ref[...]] + [
        (gown_ref[c] + garrived_ref[c].astype(WIDE)).astype(LOW) for c in range(2)
    ]
    g_norm = sum(nt(part, column(1 + c)) for c, part in enumerate(parts))
    part, g_gain = normed_back(g_norm, joined_ref[...], gain_ref[...])
    g_joined = gmid_ref[...] + part
    g_low = g_joined.astype(LOW)
    g_mixed = nt(g_low, column(0)).astype(LOW).astype(WIDE)
    edge = jnp.zeros((8, width), WIDE)
    padded_ref[0:8] = edge
    padded_ref[8 : 8 + rows] = g_mixed
    padded_ref[8 + rows :] = edge
    taps = [taps_ref[k : k + 1] for k in range(4)]
    grad_ref[...] = g_joined + sum(taps[k] * padded_ref[11 - k : 11 - k + rows] for k in range(4))
    head_ref[...] = sum(taps[k] * padded_ref[8 - k : 16 - k] for k in range(4))
    small_ref[...] = jnp.zeros_like(small_ref)
    for k in range(4):
        small_ref[k : k + 1] = jnp.sum(g_mixed * extended_ref[5 + k : 5 + k + rows], 0, keepdims=True)
    small_ref[4:5] = jnp.sum(g_mixed, 0, keepdims=True)
    small_ref[5:6] = jnp.sum(g_low.astype(WIDE), 0, keepdims=True)
    small_ref[6:7] = g_gain
    small_ref[7:10] = lines_ref[...]
    put(0, jnp.transpose(mixed_ref[...]), g_low)
    turned = jnp.transpose(norm_ref[...])
    for c, part in enumerate(parts):
        put(1 + c, turned, part)
    put(4, jnp.transpose(att_ref[...]), gmid_low_ref[...])
    small = jnp.broadcast_to(small_ref[...].astype(LOW)[None], (owners, share, width))
    kept_ref[:, 5] = small
    sent_ref[:, 5] = small


def inner_back(info, g_query, g_own, g_arrived, weight, taps, gain, joined, g_mid, saved, extended, lines, owners):
    rows, width = joined.shape
    terms = jax.ShapeDtypeStruct((owners, 6, SHARE, width), LOW)
    full = lambda array: pl.BlockSpec(array.shape, lambda j: (0,) * len(array.shape))
    out_shape = [
        terms,
        terms,
        jax.ShapeDtypeStruct((rows, width), WIDE),
        jax.ShapeDtypeStruct((8, width), WIDE),
    ]
    before = (g_query, g_own, g_arrived)
    after = (taps, gain.reshape(1, width), joined, g_mid) + saved + (extended, lines)
    return pl.pallas_call(
        inner_back_kernel,
        grid=(1,),
        in_specs=[pl.BlockSpec(memory_space=pltpu.SMEM)]
        + [full(array) for array in before]
        + [pl.BlockSpec((width, 4 * width), lambda j: (0, 0))]
        + [full(array) for array in after],
        out_specs=[full(array) for array in out_shape],
        out_shape=out_shape,
        scratch_shapes=[pltpu.VMEM((rows + 16, width), WIDE), pltpu.VMEM((SHARE, width), WIDE)],
        name="inner_back",
    )(info, *before, weight, *after)


def pack_kernel(
    info_ref,
    lengths_ref,
    taps_ref,
    bias_ref,
    join_ref,
    join_bias_ref,
    gain_attn_ref,
    attn_in_ref,
    attn_out_ref,
    position_ref,
    gain_mlp_ref,
    mlp_in_ref,
    mlp_out_ref,
    *refs,
):
    small_ref = refs[-1]
    device = info_ref[0]
    layers, share, width = join_ref.shape
    lane = lax.broadcasted_iota(jnp.int32, (share, width), 1)
    item = lax.broadcasted_iota(jnp.int32, (share, width), 0)
    spread = jnp.where(lane == device * share + item, 1.0, 0.0).astype(LOW)
    place = lane[:1] - device * share - HEADS
    extra = jnp.zeros((1, width), WIDE)
    for m in range(lengths_ref.shape[0]):
        whole, rest = lengths_ref[m] // 32, lengths_ref[m] % 32
        extra = extra + jnp.where(place == 2 * m, whole, jnp.where(place == 2 * m + 1, rest, 0)).astype(WIDE)
    for l in range(layers):
        small_ref[0:9] = nn(taps_ref[:, l], spread)
        small_ref[9:12] = nn(bias_ref[:, l], spread)
        small_ref[12:13] = nn(join_bias_ref[l : l + 1], spread)
        small_ref[13:14] = nn(gain_attn_ref[l : l + 1], spread)
        small_ref[14:15] = nn(gain_mlp_ref[l : l + 1], spread)
        small_ref[15:16] = nn(position_ref[l : l + 1], spread[:HEADS]) + extra
        first = [join_ref[l]] + [attn_in_ref[l, c] for c in range(3)] + [small_ref[...].astype(LOW)]
        outward = [mlp_out_ref[l, a * share : (a + 1) * share] for a in range(mlp_out_ref.shape[1] // share)]
        inward = [attn_out_ref[l], mlp_in_ref[l, 0], mlp_in_ref[l, 1]]
        out_width = mlp_out_ref.shape[1] // share * width
        in_width = width + 2 * mlp_in_ref.shape[3]
        places = (
            (refs[l], 0, first),
            (refs[layers], l * out_width, outward),
            (refs[layers], layers * out_width + l * in_width, inward),
        )
        for out_ref, cursor, pieces in places:
            for piece in pieces:
                out_ref[:, cursor : cursor + piece.shape[1]] = piece
                cursor += piece.shape[1]


def pack(info, lengths, arrays, share):
    layers, width = arrays[2].shape[0], arrays[2].shape[2]
    quarters = arrays[-2].shape[3] // width
    first, rest = 5 * width, (1 + 3 * quarters) * width
    smem = pl.BlockSpec(memory_space=pltpu.SMEM)
    vmem = pl.BlockSpec(memory_space=pltpu.VMEM)
    return pl.pallas_call(
        pack_kernel,
        in_specs=[smem, smem] + [vmem] * len(arrays),
        out_specs=[vmem] * (layers + 1),
        out_shape=[
            jax.ShapeDtypeStruct((share, span), LOW) for span in [first] * layers + [layers * rest]
        ],
        scratch_shapes=[pltpu.VMEM((share, width), WIDE)],
        name="pack",
    )(info, lengths, *arrays)


def collected_kernel(device_ref, inverse_ref, *refs):
    device = device_ref[0]
    inputs, outputs = refs[:16], refs[16:]
    join_ref, attn_in_ref, attn_out_ref, mlp_in_ref, mlp_out_ref, loss_ref = outputs[:6]
    taps_ref, bias_ref, join_bias_ref, gain_attn_ref, gain_mlp_ref, position_ref = outputs[6:]
    share, width = join_ref.shape[1:]
    quarters = mlp_in_ref.shape[3] // width
    lane = lax.broadcasted_iota(jnp.int32, (share, width), 1)
    item = lax.broadcasted_iota(jnp.int32, (share, width), 0)
    own = jnp.where(lane == device * share + item, 1.0, 0.0)

    def total(pieces, at):
        return sum(piece[at].astype(WIDE) for piece in pieces)

    for l in range(2):
        mlp, attn = inputs[8 * l : 8 * l + 4], inputs[8 * l + 4 : 8 * l + 8]
        join_ref[l] = total(attn, 0)
        for c in range(3):
            attn_in_ref[l, c] = total(attn, 1 + c)
        attn_out_ref[l] = total(attn, 4)
        for c in range(2):
            for a in range(quarters):
                mlp_in_ref[l, c, :, a * width : (a + 1) * width] = total(mlp, c * quarters + a)
        for a in range(quarters):
            mlp_out_ref[l, a * share : (a + 1) * share] = total(mlp, 2 * quarters + a)
        small = total(attn, 5)
        small_own = lax.dot_general(
            small,
            own,
            (((1,), (1,)), ((), ())),
            precision=lax.Precision.HIGHEST,
            preferred_element_type=WIDE,
        )
        line = slice(l, l + 1)
        for at, tap in enumerate((2, 3, 1, 2, 3, 0, 1, 2, 3)):
            taps_ref[at, line] = small_own[tap : tap + 1]
        for at in range(3):
            bias_ref[at, line] = small_own[4:5]
        for at, out_ref in enumerate((join_bias_ref, gain_attn_ref, gain_mlp_ref)):
            out_ref[line] = small_own[5 + at : 6 + at]
        position_ref[line] = small_own[8:9, :HEADS]
        if l == 1:
            loss_ref[...] = jnp.sum(small[9:10], 1, keepdims=True) * inverse_ref[0]


def collected(device, inverse, layers, quarters):
    pieces = [piece for mlp, attn in layers for piece in list(mlp) + list(attn)]
    share, width = pieces[0].shape[1:]
    count = len(layers)
    shapes = [
        (count, share, width),
        (count, 3, share, width),
        (count, share, width),
        (count, 2, share, quarters * width),
        (count, quarters * share, width),
        (1, 1),
        (9, count, share),
        (3, count, share),
        (count, share),
        (count, share),
        (count, share),
        (count, HEADS),
    ]
    vmem = pl.BlockSpec(memory_space=pltpu.VMEM)
    return pl.pallas_call(
        collected_kernel,
        in_specs=[pl.BlockSpec(memory_space=pltpu.SMEM)] * 2 + [vmem] * len(pieces),
        out_specs=[vmem] * len(shapes),
        out_shape=[jax.ShapeDtypeStruct(shape, WIDE) for shape in shapes],
        name="collected",
    )(device, inverse, *pieces)


def tie(*values):
    return lax.optimization_barrier(values)


def chip_body(
    byte_states,
    teacher,
    lengths,
    conv_taps,
    conv_bias,
    join_weight,
    join_bias,
    gain_attn,
    attn_in_weight,
    attn_out_weight,
    position_bias,
    gain_mlp,
    mlp_in_weight,
    mlp_out_weight,
):
    layer_count = conv_taps.shape[0]
    model_width = byte_states.shape[3]
    slot_rows = byte_states.shape[2]
    rows = 2 * slot_rows
    hidden_width = mlp_in_weight.shape[3]
    quarters = hidden_width // model_width
    seqs, zs, cores = (lax.axis_size(name) for name in ALL)
    devices = seqs * zs * cores
    share = SHARE
    s_at, z_at, c_at = (lax.axis_index(name) for name in ALL)
    device_at = (s_at * zs + z_at) * cores + c_at

    def number(s, z, c):
        return (s * zs + z) * cores + c

    places = [(s, z, c) for s in range(seqs) for z in range(zs) for c in range(cores)]
    swap = [(number(s, z, c), number(s, z, 1 - c)) for s, z, c in places]
    routes = [
        [(number(s, z, c), number(2 * (s % 2 if turn == 0 else 1 - s % 2) + c, z, s // 2)) for s, z, c in places]
        for turn in range(2)
    ]
    back_routes = [[(b, a) for a, b in route] for route in routes]

    def to_chips(block):
        odd, high = s_at % 2, s_at // 2
        first, second = (
            lax.ppermute(jnp.where(odd == turn, block[0], block[1]), ALL, routes[turn]) for turn in range(2)
        )
        return jnp.concatenate(
            [jnp.where(high == 0, first, second), jnp.where(high == 0, second, first)], 0
        )

    def leave(block):
        high = s_at // 2
        halves = (block[:slot_rows], block[slot_rows:])
        return [
            lax.ppermute(jnp.where(high == turn, halves[0], halves[1]), ALL, back_routes[turn])
            for turn in range(2)
        ]

    def arrive(pieces):
        first, second = pieces
        odd = s_at % 2
        whole = jnp.stack([jnp.where(odd == 0, first, second), jnp.where(odd == 0, second, first)])
        return whole.astype(WIDE)[:, None]

    def trade(block):
        return lax.ppermute(block, ALL, swap)

    to_high = [(number(s, z, 0), number(s, z, 1)) for s, z, c in places if c == 0]
    to_low = [(b, a) for a, b in to_high]

    lanes = jnp.arange(model_width)
    lane_owner, lane_item = lanes // share, lanes % share
    every_layer = range(layer_count)
    packed = pack(
        device_at.astype(jnp.int32).reshape(1),
        lengths.reshape(-1),
        (
            conv_taps.transpose(1, 0, 2),
            conv_bias.transpose(1, 0, 2),
            join_weight,
            join_bias,
            gain_attn,
            attn_in_weight,
            attn_out_weight,
            position_bias,
            gain_mlp,
            mlp_in_weight,
            mlp_out_weight,
        ),
        share,
    )

    def moved(block, name, change):
        def target(s, z, c):
            return number(s ^ change, z, c) if name == "seq" else number(s, z ^ change, c)

        return lax.ppermute(block, ALL, [(number(s, z, c), target(s, z, c)) for s, z, c in places])

    def spread_out(block, name, at, size):
        whole = jnp.zeros((size,) + block.shape, block.dtype)
        pieces = [block] + [moved(block, name, change) for change in range(1, size)]
        for change, piece in enumerate(pieces):
            whole = lax.dynamic_update_index_in_dim(whole, piece, at ^ change, 0)
        return whole

    def pair_up(block):
        other = trade(block)
        return jnp.stack(
            [jnp.where(c_at == 0, block, other), jnp.where(c_at == 0, other, block)], 2
        ).reshape(model_width, -1)

    def split_halves(kept, arrived):
        shape = (seqs, zs) + kept.shape[1:]
        return kept.reshape(shape), arrived.reshape(shape)

    def plane_terms(kept, arrived):
        kept, arrived = split_halves(kept, arrived)
        pick = lambda whole, s: lax.dynamic_index_in_dim(whole, s, 0, False).astype(WIDE)
        return [
            (pick(kept, s_at ^ change) + pick(arrived, s_at ^ change)).astype(LOW)
            for change in range(seqs)
        ]

    def line_terms(pieces):
        total = finish(pieces).astype(LOW)
        return [lax.dynamic_index_in_dim(total, z_at ^ change, 0, False) for change in range(zs)]

    def send(name, terms):
        return [moved(part, name, change) if change else part for change, part in enumerate(terms)]

    def finish(pieces):
        return sum(piece.astype(WIDE) for piece in pieces)

    early, behind = spread_out(packed[0], "z", z_at, zs), packed[1]
    early = spread_out(early, "seq", s_at, seqs)
    early, behind = tie(early, behind)
    early = [pair_up(early), spread_out(behind, "z", z_at, zs)]
    later = lax.all_gather(packed[2], ALL, axis=0, tiled=True)

    def unpack_first(first):
        small = jnp.sum(first[:, 4 * model_width :].reshape(devices, share, model_width).astype(WIDE), 0)
        return dict(
            whole=first,
            join=first[:, :model_width],
            attn_in=first[:, model_width : 4 * model_width],
            taps=jnp.stack(
                [
                    small[5],
                    small[2] + small[6],
                    small[0] + small[3] + small[7],
                    small[1] + small[4] + small[8],
                ]
            ),
            bias=small[9] + small[10] + small[11],
            join_bias=small[12],
            gain_attn=small[13],
            gain_mlp=small[14],
            last=small[15],
        )

    weights = [unpack_first(early[0])]
    state = to_chips(byte_states[:, 0]).astype(WIDE)

    counts = weights[0]["last"]
    scale = jnp.where((lane_item >= HEADS) & (lane_item < HEADS + 4), jnp.where(lane_item % 2 == 0, 32.0, 1.0), 0.0)
    total_valid = jnp.sum(jnp.where(lane_owner < zs * cores, counts * scale, 0.0))
    mine = (lane_owner == z_at * cores + s_at % 2) & ((lane_item - HEADS) // 2 == s_at // 2)
    length = jnp.sum(jnp.where(mine, counts * scale, 0.0)).astype(jnp.int32)
    info = jnp.stack([c_at.astype(jnp.int32), length])
    row_valid = (rows * c_at + jnp.arange(rows) < length)[:, None]

    offsets = -((jnp.arange(4 * BLOCK) + 2 * BLOCK) % (4 * BLOCK) - 2 * BLOCK)
    in_bucket = (lane_owner[:, None] == bucket_ids(offsets)[None, :]).astype(LOW)
    of_head = (lane_item[None, :] == jnp.arange(HEADS)[:, None]).astype(WIDE)
    far_bucket = (lane_owner == jnp.where(c_at == 0, 31, 15)).astype(WIDE)

    def bias_of(last):
        line = jnp.dot((of_head * last).astype(LOW), in_bucket, preferred_element_type=WIDE)
        return jnp.sum(of_head * (last * far_bucket), 1), build_band(line)

    biases = [bias_of(weights[0]["last"])]
    kept = []
    for l in range(layer_count):
        w = weights[l]
        low_state = state.astype(LOW)
        prior = lax.ppermute(low_state[rows - 8 :], ALL, to_high)
        extended = jnp.concatenate([prior, low_state], 0).astype(WIDE)
        mixed = w["bias"] + sum(w["taps"][k] * extended[5 + k : 5 + k + rows] for k in range(4))
        mixed = mixed.astype(LOW)
        joined = state + nn(mixed, w["join"]) + w["join_bias"]
        norm_a = normed(joined, w["gain_attn"])
        inner = HEADS * HEAD_DIM
        own = nn(norm_a, w["attn_in"][:, inner:]).astype(LOW)
        if l + 1 < layer_count:
            own, early[l + 1] = tie(own, early[l + 1])
            early[l + 1] = spread_out(early[l + 1], "seq", s_at, seqs)
        others = trade(own)
        projected = (nn(norm_a, w["attn_in"][:, :inner]).astype(LOW), own)
        far, band = biases[l]
        attended, lse = attend(info, far, projected, others, band)
        if l + 1 < layer_count:
            attended, lse, early[l + 1] = tie(attended, lse, early[l + 1])
            weights.append(unpack_first(pair_up(early[l + 1])))
            biases.append(bias_of(weights[l + 1]["last"]))
            attended, lse, later, biases[l + 1], weights[l + 1], teacher = tie(
                attended, lse, later, biases[l + 1], weights[l + 1], teacher
            )
        mid, norm_m, state = mlp_forward(attended, joined, w["gain_mlp"], later, quarters, layer_count, l)
        if l == 0:
            state, target = tie(state, to_chips(teacher[:, 0]))
        kept.append(
            (extended, mixed, joined, norm_a, projected, others, far, band, attended, lse, mid, norm_m)
        )

    activations = leave(state)
    diff = jnp.where(row_valid, state - target.astype(WIDE), 0.0)
    squares = jnp.sum(diff * diff, 0)
    grad = 2.0 * diff / (total_valid * model_width)
    owners = seqs * zs
    mlp_way = attn_way = None
    for l in reversed(every_layer):
        w = weights[l]
        (extended, mixed, joined, norm_a, projected, others, far, band, attended, lse, mid, norm_m) = kept[l]
        g_mid, g_mid_low, g_att, g_gain_mlp, mlp_kept, mlp_sent = mlp_back(
            info, grad, norm_m, mid, w["gain_mlp"], later, quarters, layer_count, l, owners, share
        )
        if mlp_way is None:
            g_att, mlp_kept, mlp_sent, activations = tie(g_att, mlp_kept, mlp_sent, activations)
        else:
            g_att, mlp_kept, mlp_sent, mlp_way, attn_way = tie(
                g_att, mlp_kept, mlp_sent, mlp_way, attn_way
            )
            line = line_terms(attn_way)
            g_att, line = tie(g_att, line)
            attn_way = send("z", line)
        mlp_half = (mlp_kept, trade(mlp_sent))
        attention = (info, far, projected, others, band, attended, g_att, lse)
        back = attend_back(*attention, 0, 1)
        back, mlp_half = tie(back, mlp_half)
        plane = plane_terms(*mlp_half)
        back, plane = tie(back, plane)
        mlp_half = send("seq", plane)
        back = attend_back(*attention, 1, HEADS // 2 - 1, back)
        mlp_near = mlp_half[: seqs - 1]
        if attn_way is None:
            back, mlp_near = tie(back, mlp_near)
        else:
            back, mlp_near, attn_way = tie(back, mlp_near, attn_way)
        mlp_half = mlp_near + mlp_half[seqs - 1 :]
        g_query, g_own, g_other, g_band, g_far = back
        g_arrived = trade(g_other)
        by_lane = jnp.dot(
            g_band.reshape(HEADS, -1),
            in_bucket.T.astype(WIDE),
            precision=lax.Precision.HIGHEST,
            preferred_element_type=WIDE,
        )
        g_far = jnp.sum(g_far.reshape(HEADS, -1), 1)[:, None]
        g_last = jnp.sum(of_head * (by_lane + g_far * far_bucket), 0)
        attn_kept, attn_sent, grad, head = inner_back(
            info,
            g_query,
            g_own,
            g_arrived,
            w["whole"],
            w["taps"],
            w["gain_attn"],
            joined,
            g_mid,
            (mixed, norm_a, attended, g_mid_low),
            extended,
            jnp.stack([g_gain_mlp[0], g_last, squares]),
            owners,
        )
        beyond = lax.ppermute(head, ALL, to_low)
        last = grad[rows - 8 :] + jnp.concatenate([jnp.zeros((5, model_width), WIDE), beyond[:3]], 0)
        grad = lax.dynamic_update_slice(grad, last, (rows - 8, 0))
        if l > 0:
            attn_kept, attn_sent, mlp_half = tie(attn_kept, attn_sent, mlp_half)
            attn_arrived = trade(attn_sent)
            line, plane = line_terms(mlp_half), plane_terms(attn_kept, attn_arrived)
            grad, line, plane = tie(grad, line, plane)
            attn_way, mlp_way = send("seq", plane), send("z", line)

    above_mlp, above_attn = mlp_way, attn_way
    attn_kept, attn_sent, mlp_half = tie(attn_kept, attn_sent, mlp_half)
    attn_arrived = trade(attn_sent)
    plane = plane_terms(attn_kept, attn_arrived)
    plane, mlp_half = tie(plane, mlp_half)
    mlp_half = send("z", line_terms(mlp_half))
    attn_way = send("seq", plane)
    attn_way, mlp_way = tie(attn_way, mlp_half)
    grad, line = tie(grad.astype(LOW), line_terms(attn_way))
    attn_way = send("z", line)
    input_grad = leave(grad)
    (
        g_join,
        g_attn_in,
        g_attn_out,
        g_mlp_in,
        g_mlp_out,
        loss,
        g_taps,
        g_bias,
        g_join_bias,
        g_gain_attn,
        g_gain_mlp,
        g_position,
    ) = collected(
        device_at.astype(jnp.int32).reshape(1),
        (1.0 / (total_valid * model_width)).reshape(1),
        [(mlp_way, attn_way), (above_mlp, above_attn)],
        quarters,
    )
    loss = loss.reshape(())
    return (
        arrive(activations),
        loss,
        arrive(input_grad),
        g_taps.transpose(1, 0, 2),
        g_bias.transpose(1, 0, 2),
        g_join,
        g_join_bias,
        g_gain_attn,
        g_attn_in,
        g_attn_out,
        g_position,
        g_gain_mlp,
        g_mlp_in,
        g_mlp_out,
    )


def chip_plan(mesh):
    grid = Mesh(
        mesh.devices.reshape(mesh.shape["seq"], mesh.shape["batch"] // 2, 2),
        ALL,
    )
    batch = ("z", "core")
    in_specs = (
        P(None, batch, "seq", None),
        P(None, batch, "seq", None),
        P(None, batch),
        P(None, None, ALL),
        P(None, None, ALL),
        P(None, ALL, None),
        P(None, ALL),
        P(None, ALL),
        P(None, None, ALL, None),
        P(None, ALL, None),
        P(None, ALL),
        P(None, ALL),
        P(None, None, ALL, None),
        P(None, ALL, None),
    )
    out_specs = (in_specs[0], P(), in_specs[0]) + in_specs[3:]
    return jax.shard_map(chip_body, mesh=grid, in_specs=in_specs, out_specs=out_specs, check_vma=False)


def shared_plan(mesh):
    in_specs = (
        P(None, "batch", "seq", None),
        P(None, "batch", "seq", None),
        P(None, "batch"),
        P(None, None, ("seq", "batch")),
        P(None, None, ("seq", "batch")),
        P(None, ("seq", "batch"), None),
        P(None, ("seq", "batch")),
        P(None, ("seq", "batch")),
        P(None, None, ("seq", "batch"), None),
        P(None, ("seq", "batch"), None),
        P(None, ("seq", "batch")),
        P(None, ("seq", "batch")),
        P(None, None, ("seq", "batch"), None),
        P(None, ("seq", "batch"), None),
    )
    out_specs = (
        P(None, "batch", "seq", None),
        P(),
        P(None, "batch", "seq", None),
        P(None, None, ("seq", "batch")),
        P(None, None, ("seq", "batch")),
        P(None, ("seq", "batch"), None),
        P(None, ("seq", "batch")),
        P(None, ("seq", "batch")),
        P(None, None, ("seq", "batch"), None),
        P(None, ("seq", "batch"), None),
        P(None, ("seq", "batch")),
        P(None, ("seq", "batch")),
        P(None, None, ("seq", "batch"), None),
        P(None, ("seq", "batch"), None),
    )
    return jax.shard_map(body, mesh=mesh, in_specs=in_specs, out_specs=out_specs, check_vma=False)


def solution(mesh):
    shared = shared_plan(mesh)

    def run(*arrays):
        sequences = arrays[0].shape[0] * arrays[0].shape[1]
        one_per_chip = 2 * sequences == mesh.devices.size and 2 * arrays[0].shape[0] == mesh.shape["seq"]
        two_layers = arrays[3].shape[0] == 2
        lanes_fit = arrays[5].shape[1] == SHARE * mesh.devices.size and arrays[0].shape[2] == 4 * BLOCK
        plan = chip_plan(mesh) if one_per_chip and lanes_fit and two_layers else shared
        return plan(*arrays)

    return run
```
